32 devices in a mesh: dp: 16 (over z, y, core), fsdp: 2 (over x).
Axes of the slice: x: 2, y: 2, z: 4, core: 2. Of those that a mesh axis runs over, the one named last changes fastest.
Arguments:
- tokens: bfloat16 [32768, 768], P(('dp', 'fsdp')), may hold values from -6 to 6
- segment_ids: int32 [32768], P(('dp', 'fsdp')), may hold values from 0 to 255, never falling along the last dimension, each value on 1 to 384 neighbouring positions
- cotangent: bfloat16 [32768, 768], P(('dp', 'fsdp')), may hold values from -6 to 6
- norm1_gain: float32 [768], P('fsdp'), may hold values from 0.5 to 1.5
- norm1_shift: float32 [768], P('fsdp'), may hold values from -1.75 to 1.75
- qkv_weight: float32 [768, 2304], P('fsdp'), may hold values from -0.21875 to 0.21875
- query_bias: float32 [768], P('fsdp'), may hold values from -3 to 3
- value_bias: float32 [768], P('fsdp'), may hold values from -3 to 3
- out_weight: float32 [768, 768], P('fsdp'), may hold values from -1.75 to 1.75
- out_bias: float32 [768], P('fsdp'), may hold values from -1.75 to 1.75
- norm2_gain: float32 [768], P('fsdp'), may hold values from 0.5 to 1.5
- norm2_shift: float32 [768], P('fsdp'), may hold values from -1.75 to 1.75
- up_weight: float32 [768, 3072], P('fsdp'), may hold values from -0.21875 to 0.21875
- up_bias: float32 [3072], P('fsdp'), may hold values from -3 to 3
- down_weight: float32 [3072, 768], P('fsdp'), may hold values from -0.109375 to 0.109375
- down_bias: float32 [768], P('fsdp'), may hold values from -1.75 to 1.75
Outputs:
- output: bfloat16 [32768, 768], P(('dp', 'fsdp'))
- input_grad: bfloat16 [32768, 768], P(('dp', 'fsdp'))
- norm1_gain_grad: float32 [768], P('fsdp')
- norm1_shift_grad: float32 [768], P('fsdp')
- qkv_weight_grad: float32 [768, 2304], P('fsdp')
- query_bias_grad: float32 [768], P('fsdp')
- value_bias_grad: float32 [768], P('fsdp')
- out_weight_grad: float32 [768, 768], P('fsdp')
- out_bias_grad: float32 [768], P('fsdp')
- norm2_gain_grad: float32 [768], P('fsdp')
- norm2_shift_grad: float32 [768], P('fsdp')
- up_weight_grad: float32 [768, 3072], P('fsdp')
- up_bias_grad: float32 [3072], P('fsdp')
- down_weight_grad: float32 [3072, 768], P('fsdp')
- down_bias_grad: float32 [768], P('fsdp')
The draws below stay inside these ranges and needn't reach their ends.
Inputs may be any that keep to these rules, and one draw needn't show every extreme that they name: segment_ids never fall along the rows; each id covers 1 to 384 consecutive rows and some id covers exactly 384.
All inputs are finite; a program needn't handle non-finite values.
Results may differ from the reference program's by a relative error of at most 0.019.
Values may be sent and summed in bfloat16 or wider, within the bound.
A program may use at most 192 MiB of HBM per device.

```python
import math
import jax
import jax.numpy as jnp
import numpy as np
from jax import lax

D = 768
HEADS = 12
FF = 3072
SEQ = 512
SEG_MOST = 384
TOKENS = 32768
SEG_COUNT = 256


def strengthened(array, stream_key, source, target, parts, factor):
    def block_of(position):
        return (jnp.arange(array.shape[position]) // (array.shape[position] // parts)).reshape((-1,) + (1,) * (array.ndim - 1 - position))

    one_side = jax.random.permutation(stream_key, parts)[block_of(target)]
    other_side = (block_of(target) + parts // 2) % parts
    return jnp.where((block_of(source) == one_side) | (block_of(source) == other_side), factor * array, array)


def level_of(stream_key, dims, split, low, largest):
    level, own = 1.0, jax.random.fold_in(stream_key, 6)
    for axis_at, shards_of in split:
        steps = jnp.exp(jax.random.uniform(jax.random.fold_in(own, axis_at), (shards_of,), jnp.float32, low / len(split), largest / len(split)))
        level = level * jnp.repeat(steps, dims[axis_at] // shards_of).reshape([-1 if axis == axis_at else 1 for axis in range(len(dims))])
    return level


def split_up(count, total, limit, skew):
    loads = [(1 << 20) // math.isqrt(grade ** skew) + 1 for grade in range(2, count + 1)]
    surplus, counts = total - limit - (count - 1), [1] * (count - 1)
    while surplus > 0:
        free = [i for i in range(count - 1) if counts[i] < limit]
        mass, remaining = sum([loads[i] for i in free]), surplus
        for i in free:
            extra = min(limit - counts[i], max(1, remaining * loads[i] // mass), surplus)
            counts[i] = counts[i] + extra
            surplus = surplus - extra
    return np.array([limit] + counts)


def uneven_parts(own_key, amount, total, bound, slope):
    if amount == 2:
        one = jax.random.randint(own_key, (), max(1, total - bound), min(bound, total - 1) + 1)
        return jnp.stack([one, total - one])
    sizes = jnp.asarray(split_up(amount, total, bound, slope), jnp.int32)
    twos = (amount - 1) // 2
    giver, receiver = sizes[1:1 + 2 * twos:2], sizes[2:2 + 2 * twos:2]
    room = jnp.minimum(giver - 1, bound - receiver)
    passed = jax.random.randint(jax.random.fold_in(own_key, 1), (twos,), 0, 1 << 20) % (room + 1)
    sizes = sizes.at[1:1 + 2 * twos:2].set(giver - passed).at[2:2 + 2 * twos:2].set(receiver + passed)
    return sizes[jax.random.permutation(jax.random.fold_in(own_key, 2), amount)]


def scatter_about(key, dims, scale, bound, shards=(), kind=jnp.bfloat16):
    level = level_of(key, dims, shards, -0.22, 0.18) if shards else 1.0
    entries = jax.random.normal(key, dims, jnp.float32) * scale * level
    return jnp.minimum(jnp.maximum(entries, -bound), bound).astype(kind)


def noise_with(stream_key, shape, scale, limit, pieces, heavy, held_as=jnp.bfloat16):
    array = scale * jax.random.normal(stream_key, shape, jnp.float32)
    if pieces:
        array = array * level_of(stream_key, shape, pieces, -0.22, 0.18)
    return jnp.clip(strengthened(array, jax.random.fold_in(stream_key, 3), *heavy), -limit, limit).astype(held_as)


def setup_inputs(seed: int = 0) -> dict:
    arg_keys = jax.random.split(jax.random.key(seed), 17)
    return {
        "tokens": scatter_about(arg_keys[0], (TOKENS, D), 1.0, 6.0, ((0, 32),)),
        "segment_ids": jnp.searchsorted(jnp.cumsum(uneven_parts(arg_keys[1], SEG_COUNT, TOKENS, SEG_MOST, 2)), jnp.arange(TOKENS), side="right").astype(jnp.int32),
        "cotangent": noise_with(arg_keys[2], (TOKENS, D), 1.0, 6.0, ((0, 32),), (0, 1, 32, 2.75)),
        "norm1_gain": jnp.clip(1.0 + 0.1 * jax.random.normal(arg_keys[3], (D,), jnp.float32), 0.5, 1.5),
        "norm1_shift": scatter_about(arg_keys[4], (D,), 0.3, 1.75, ((0, 2),), jnp.float32),
        "qkv_weight": scatter_about(arg_keys[5], (D, 3 * D), D ** -0.5, 0.21875, ((0, 2),), jnp.float32),
        "query_bias": scatter_about(arg_keys[6], (D,), 0.5, 3.0, ((0, 2),), jnp.float32),
        "value_bias": scatter_about(arg_keys[7], (D,), 0.5, 3.0, ((0, 2),), jnp.float32),
        "out_weight": scatter_about(arg_keys[8], (D, D), (D // 64) ** -0.5, 1.75, ((0, 2),), jnp.float32),
        "out_bias": scatter_about(arg_keys[9], (D,), 0.3, 1.75, ((0, 2),), jnp.float32),
        "norm2_gain": jnp.clip(1.0 + 0.1 * jax.random.normal(arg_keys[10], (D,), jnp.float32), 0.5, 1.5),
        "norm2_shift": scatter_about(arg_keys[11], (D,), 0.3, 1.75, ((0, 2),), jnp.float32),
        "up_weight": scatter_about(arg_keys[12], (D, FF), D ** -0.5, 0.21875, ((0, 2),), jnp.float32),
        "up_bias": scatter_about(arg_keys[13], (FF,), 0.5, 3.0, ((0, 2),), jnp.float32),
        "down_weight": scatter_about(arg_keys[14], (FF, D), FF ** -0.5, 0.109375, ((0, 2),), jnp.float32),
        "down_bias": scatter_about(arg_keys[15], (D,), 0.3, 1.75, ((0, 2),), jnp.float32),
    }


@jax.custom_vjp
def low(v):
    return lax.optimization_barrier(v.astype(jnp.bfloat16)).astype(jnp.float32)

@jax.custom_vjp
def low_back(v):
    return v

def low_keep(v):
    return (low(v), None)

def low_pass(kept, grad):
    return (grad,)

def back_keep(v):
    return (v, None)

def back_low(kept, grad):
    return (low(grad),)
low.defvjp(low_keep, low_pass)
low_back.defvjp(back_keep, back_low)
EPSILON = 1e-06
LARGE_NEG = -1000000000.0
HIGHEST = lax.Precision.HIGHEST

def layer_norm(inputs, gain_vec, shift_vec):
    centre = inputs - lax.optimization_barrier(jnp.mean(inputs, -1, keepdims=True))
    spread = lax.optimization_barrier(jnp.mean(centre * centre, -1, keepdims=True))
    return centre * lax.rsqrt(spread + EPSILON) * gain_vec + shift_vec

def matmul(left, right):
    return jnp.dot(left, right, precision=HIGHEST)

def reference(tokens, segment_ids, cotangent, norm1_gain, norm1_shift, qkv_weight, query_bias, value_bias, out_weight, out_bias, norm2_gain, norm2_shift, up_weight, up_bias, down_weight, down_bias):
    head_dim = D // HEADS
    scaling = head_dim ** (-0.5)
    groups = TOKENS // SEQ // 8
    seg_groups = segment_ids.reshape(groups, 8, SEQ)

    def attend_group(block):
        queries, key_rows, value_rows, seg_block = block
        raw_scores = jnp.einsum('bqhd,bkhd->bhqk', queries, key_rows, precision=HIGHEST)
        allowed = seg_block[:, None, :, None] == seg_block[:, None, None, :]
        scores = low_back(jnp.where(allowed, raw_scores * scaling, LARGE_NEG))
        row_max = lax.optimization_barrier(jnp.max(scores, -1, keepdims=True))
        expo = jnp.exp(scores - row_max)
        attn_probs = low(expo / lax.optimization_barrier(jnp.sum(expo, -1, keepdims=True)))
        return jnp.einsum('bhqk,bkhd->bqhd', attn_probs, value_rows, precision=HIGHEST)

    def forward(inputs, gain_one, shift_one, w_qkv, q_bias, v_bias, w_out, o_bias, gain_two, shift_two, w_up, u_bias, w_down, d_bias):
        gain_one, shift_one, w_qkv, q_bias, v_bias = (low(gain_one), low(shift_one), low(w_qkv), low(q_bias), low(v_bias))
        w_out, o_bias, gain_two, shift_two = (low(w_out), low(o_bias), low(gain_two), low(shift_two))
        w_up, u_bias, w_down, d_bias = (low(w_up), low(u_bias), low(w_down), low(d_bias))
        act_one = low(layer_norm(inputs, gain_one, shift_one))
        linear = matmul(act_one, w_qkv) + jnp.concatenate([q_bias, jnp.zeros_like(q_bias), v_bias])
        linear = low(low_back(linear))
        shaped = linear.reshape(groups, 8, SEQ, 3, HEADS, head_dim)
        attended = lax.map(jax.checkpoint(attend_group), (shaped[:, :, :, 0], shaped[:, :, :, 1], shaped[:, :, :, 2], seg_groups))
        attended = low(low_back(attended.reshape(TOKENS, D)))
        branch = low_back(matmul(attended, w_out) + o_bias)
        middle = inputs + branch
        act_two = low(layer_norm(middle, gain_two, shift_two))
        hidden_pre = low_back(matmul(act_two, w_up) + u_bias)
        hidden_act = low(jax.nn.gelu(hidden_pre, approximate=False))
        mlp_out = low_back(matmul(hidden_act, w_down) + d_bias)
        return middle + mlp_out
    inputs = tokens.astype(jnp.float32)
    result, pullback = jax.vjp(forward, inputs, norm1_gain, norm1_shift, qkv_weight, query_bias, value_bias, out_weight, out_bias, norm2_gain, norm2_shift, up_weight, up_bias, down_weight, down_bias)
    grads = pullback(cotangent.astype(jnp.float32))
    return (result.astype(jnp.bfloat16), grads[0].astype(jnp.bfloat16), grads[1], grads[2], grads[3], grads[4], grads[5], grads[6], grads[7], grads[8], grads[9], grads[10], grads[11], grads[12], grads[13])
```

```python
import functools
import math

import jax
import jax.numpy as jnp
from jax import lax
from jax.experimental import pallas as pl
from jax.experimental.pallas import tpu as pltpu
from jax.sharding import PartitionSpec as P

HEADS = 12
SEQ = 512
EPSILON = 1e-06
LARGE_NEG = -1000000000.0
BF = jnp.bfloat16
F32 = jnp.float32
ROWS = 256


def dot_of(left, right, over):
    return lax.dot_general(left, right, (over, ((), ())), preferred_element_type=F32)


def dot_nn(left, right):
    return dot_of(left, right, ((1,), (0,)))


def dot_nt(left, right):
    return dot_of(left, right, ((1,), (1,)))


def dot_tn(left, right):
    return dot_of(left, right, ((0,), (0,)))


def at(index, size):
    return pl.ds(pl.multiple_of(index * size, size), size)


def span(start, size):
    return pl.ds(pl.multiple_of(start, 128), size)


def mean_of(value):
    return jnp.sum(value, -1, keepdims=True) * (1.0 / value.shape[-1])


def normed(value):
    centre = value - mean_of(value)
    inverse = lax.rsqrt(mean_of(centre * centre) + EPSILON)
    return centre * inverse, inverse


def down_sum(value):
    return jnp.sum(value, 0, keepdims=True)


def gelu_pair(value):
    cumulative = 0.5 + 0.5 * lax.erf(value * 0.7071067811865476)
    density = jnp.exp(-0.5 * value * value) * 0.3989422804014327
    return value * cumulative, cumulative + value * density


def norm_back(grad, xhat, inverse, gain):
    scaled = grad * gain
    return inverse * (scaled - mean_of(scaled) - xhat * mean_of(scaled * xhat))


class Sizes:
    def __init__(self, rows, width, hidden, shards):
        self.rows, self.width, self.hidden, self.shards = rows, width, hidden, shards
        self.seqs = rows // SEQ
        self.pairs = HEADS // 2
        share = hidden // shards
        self.tiles = max(n for n in range(1, 7) if share % n == 0 and (share // n) % 128 == 0)
        self.share = share
        self.piece = share // self.tiles
        self.tile = self.piece * shards
        self.blocks = rows // ROWS


def setup_masks(s, seg, segcol):
    for i in range(s.seqs):
        segcol[i] = jnp.broadcast_to(seg[i].astype(F32), (128, SEQ)).T


def norm_one(s, tok, vec, a1):
    def step(i, _):
        rows = at(i, ROWS)
        xhat, _inv = normed(tok[rows, :].astype(F32))
        a1[rows, :] = (xhat * vec[0:1, :] + vec[1:2, :]).astype(BF)
        return 0

    lax.fori_loop(0, s.blocks, step, 0)


def norm_one_flipped(s, tok, vec, a1T):
    def step(i, _):
        rows = at(i, ROWS)
        xhat, _inv = normed(tok[rows, :].astype(F32))
        a1T[:, rows] = (xhat * vec[0:1, :] + vec[1:2, :]).T.astype(BF)
        return 0

    lax.fori_loop(0, s.blocks, step, 0)


def project_qkv(s, a1, wqkv, vec, qkv, block):
    n = 256
    width = s.width
    row = {0: 2, 1: None, 2: 3}[block]

    def step(j, _):
        cols = span(block * width + j * n, n)
        lin = dot_nn(a1[...], wqkv[:, cols])
        if row is not None:
            lin = lin + vec[row : row + 1, at(j, n)]
        qkv[:, cols] = lin.astype(BF)
        return 0

    lax.fori_loop(0, width // n, step, 0)


def allowed_of(seg, segcol, i):
    col = segcol[i]
    full = jnp.concatenate([col] * (SEQ // 128), axis=1)
    return full == seg[i].astype(F32)


def lane_of(half):
    lanes = lax.broadcasted_iota(jnp.int32, (1, 128), 1)
    return (lanes < 64) if half == 0 else (lanes >= 64)


def pick_lanes(half, value):
    return jnp.where(lane_of(half), value, jnp.zeros_like(value))


def attend(s, first, count, qkv, seg, segcol, lse, att, attT):
    width = s.width

    def step(n, _):
        it = first + n
        i, p = it // s.pairs, it % s.pairs
        rows = at(i, SEQ)
        q = qkv[rows, at(p, 128)] * jnp.asarray(0.125, BF)
        k = qkv[rows, span(width + p * 128, 128)]
        vT = qkv[rows, span(2 * width + p * 128, 128)].T
        ok = allowed_of(seg, segcol, i)
        outs = []
        for half in (0, 1):
            scores = jnp.where(ok, dot_nt(k, pick_lanes(half, q)), LARGE_NEG)
            top = jnp.max(scores, 0, keepdims=True)
            expo = jnp.exp(scores - top)
            total = jnp.sum(expo, 0, keepdims=True)
            lse[2 * it + half] = top + jnp.log(total)
            out = dot_nn(vT[64 * half : 64 * half + 64], expo.astype(BF))
            outs.append(out * (1.0 / total))
        both = jnp.concatenate(outs, 0)
        attT[at(p, 128), rows] = both.astype(BF)
        att[rows, at(p, 128)] = both.T.astype(BF)
        return 0

    lax.fori_loop(0, count, step, 0)


def project_out(s, tok, vec, att, wout, x2, a2, a2T):
    def step(i, _):
        rows = at(i, ROWS)
        value = tok[rows, :].astype(F32) + (dot_nn(att[rows, :], wout[...]) + vec[4:5, :])
        x2[rows, :] = value
        xhat, _inv = normed(value)
        act = xhat * vec[5:6, :] + vec[6:7, :]
        a2[rows, :] = act.astype(BF)
        a2T[:, rows] = act.T.astype(BF)
        return 0

    lax.fori_loop(0, s.blocks, step, 0)


def mlp_tile(s, t, cot, ubias, a2, wup, wdown, mo, da2, hid, du, ugrad):
    starts = [f * s.share + t * s.piece for f in range(s.shards)]
    fresh = t == 0

    def step(i, sums):
        rows = at(i, ROWS)
        act, dy = a2[rows, :], cot[rows, :]
        more, back = 0.0, 0.0
        parts = []
        for f, start in enumerate(starts):
            up, down = wup[:, span(start, s.piece)], wdown[span(start, s.piece), :]
            u = dot_nn(act, up) + ubias[f, :, at(t, s.piece)]
            h, slope = gelu_pair(u)
            h = h.astype(BF)
            d = (dot_nt(dy, down) * slope).astype(BF)
            hid[rows, f * s.piece : (f + 1) * s.piece] = h
            du[rows, f * s.piece : (f + 1) * s.piece] = d
            more = more + dot_nn(h, down)
            back = back + dot_nt(d, up)
            parts.append(down_sum(d.astype(F32)))
        mo[rows, :] = jnp.where(fresh, 0.0, mo[rows, :]) + more
        da2[rows, :] = jnp.where(fresh, 0.0, da2[rows, :]) + back
        return tuple(a + b for a, b in zip(sums, parts))

    zero = jnp.zeros((1, s.piece), F32)
    sums = lax.fori_loop(0, s.blocks, step, (zero,) * s.shards)
    for f in range(s.shards):
        ugrad[f, :, at(t, s.piece)] = sums[f]


def up_grad(s, a2T, du, unit):
    half = s.tile // 2

    def step(r, _):
        rows = at(r, ROWS)
        value = dot_nn(a2T[rows, :], du[...]).astype(BF)
        unit(0)[rows, :] = value[:, :half]
        unit(1)[rows, :] = value[:, half:]
        return 0

    lax.fori_loop(0, s.width // ROWS, step, 0)


def down_grad(s, hid, cot, unit):
    half = s.width // 2

    def step(r, _):
        rows = at(r, ROWS)
        value = dot_tn(hid[:, rows], cot[...]).astype(BF)
        unit(0)[rows, :] = value[:, :half]
        unit(1)[rows, :] = value[:, half:]
        return 0

    lax.fori_loop(0, s.tile // ROWS, step, 0)


def norm_two_back(s, cot, vec, x2, mo, da2, out, dbr, vgrad):
    def step(i, sums):
        rows = at(i, ROWS)
        value = x2[rows, :]
        dy = cot[rows, :].astype(F32)
        out[rows, :] = (value + (mo[rows, :] + vec[7:8, :])).astype(BF)
        xhat, inverse = normed(value)
        grad = da2[rows, :]
        total = dy + norm_back(grad, xhat, inverse, vec[5:6, :])
        x2[rows, :] = total
        low = total.astype(BF)
        dbr[rows, :] = low
        return tuple(
            a + down_sum(b) for a, b in zip(sums, (low.astype(F32), grad * xhat, grad, dy))
        )

    zero = jnp.zeros((1, s.width), F32)
    sums = lax.fori_loop(0, s.blocks, step, (zero,) * 4)
    for j, value in enumerate(sums):
        vgrad[4 + j : 5 + j, :] = value


def att_grad(s, dbr, wout, datt):
    def step(i, _):
        rows = at(i, ROWS)
        datt[rows, :] = dot_nt(dbr[rows, :], wout[...]).astype(BF)
        return 0

    lax.fori_loop(0, s.blocks, step, 0)


def out_grad(s, attT, dbr, unit):
    half = s.width // 2

    def step(r, _):
        rows = at(r, ROWS)
        value = dot_nn(attT[rows, :], dbr[...]).astype(BF)
        unit(0)[rows, :] = value[:, :half]
        unit(1)[rows, :] = value[:, half:]
        return 0

    lax.fori_loop(0, s.width // ROWS, step, 0)


def attend_back(s, p, qkv, seg, segcol, lse, datt, qsum, vsum):
    width = s.width
    qc, kc, vc = [slice(j * width + p * 128, j * width + p * 128 + 128) for j in range(3)]

    def step(i, sums):
        rows = at(i, SEQ)
        q = qkv[rows, qc] * jnp.asarray(0.125, BF)
        k, v, g = qkv[rows, kc], qkv[rows, vc], datt[rows, qc]
        kT = k.T
        ok = allowed_of(seg, segcol, i)
        dqs, dks, dvs = [], [], []
        for half in (0, 1):
            scores = jnp.where(ok, dot_nt(k, pick_lanes(half, q)), LARGE_NEG)
            prob = jnp.exp(scores - lse[2 * (i * s.pairs + p) + half])
            dprob = dot_nt(v, pick_lanes(half, g))
            weighted = jnp.sum(prob * dprob, 0, keepdims=True)
            dscore = (prob * (dprob - weighted)).astype(BF)
            dvs.append(dot_nn(prob.astype(BF), g))
            dks.append(dot_nn(dscore, q))
            dqs.append(dot_nn(kT[64 * half : 64 * half + 64], dscore))
        mask = lane_of(0)
        dq = (jnp.concatenate(dqs, 0) * 0.125).T.astype(BF)
        dk = jnp.where(mask, dks[0], dks[1]).astype(BF)
        dv = jnp.where(mask, dvs[0], dvs[1]).astype(BF)
        qkv[rows, qc] = dq
        qkv[rows, kc] = dk
        qkv[rows, vc] = dv
        return sums[0] + down_sum(dq.astype(F32)), sums[1] + down_sum(dv.astype(F32))

    zero = jnp.zeros((1, 128), F32)
    qs, vs = lax.fori_loop(0, s.seqs, step, (zero, zero))
    qsum[:, p * 128 : p * 128 + 128] = qs
    vsum[:, p * 128 : p * 128 + 128] = vs


def qkv_grad(s, a1T, dqkv, p, part):
    width = s.width

    def step(r, _):
        rows = at(r, ROWS)
        for j in range(3):
            cols = slice(j * width + p * 128, j * width + p * 128 + 128)
            part(j)[rows, :] = dot_nn(a1T[rows, :], dqkv[:, cols]).astype(BF)
        return 0

    lax.fori_loop(0, width // ROWS, step, 0)


def norm_one_back(s, tok, vec, dqkv, wqkv, dx2, ingrad, vgrad):
    def step(i, sums):
        rows = at(i, ROWS)
        grad = dot_nt(dqkv[rows, :], wqkv[...])
        xhat, inverse = normed(tok[rows, :].astype(F32))
        ingrad[rows, :] = (dx2[rows, :] + norm_back(grad, xhat, inverse, vec[0:1, :])).astype(BF)
        return sums[0] + down_sum(grad * xhat), sums[1] + down_sum(grad)

    zero = jnp.zeros((1, s.width), F32)
    sums = lax.fori_loop(0, s.blocks, step, (zero,) * 2)
    vgrad[0:1, :] = sums[0]
    vgrad[1:2, :] = sums[1]


def block_kernel(
    s, tok_h, cot_h, seg, vec, ubias, wqkv_h, wout_h, wup_h, wdown_h,
    out_h, ingrad_h, gqkv_h, gout_h, gup_h, gdown_h, vgrad, ugrad,
    tok, cot, act, actT, attT, qkv, x2, mo, da2, hid, du,
    wqkv, wout, wup, wdown, segcol, lse, narrow, wide, thin, sems,
):
    rows, width = s.rows, s.width
    loads = [
        pltpu.make_async_copy(a, b, sems.at[i])
        for i, (a, b) in enumerate(
            ((tok_h, tok), (wqkv_h, wqkv), (wout_h, wout), (wup_h, wup), (wdown_h, wdown))
        )
    ]
    for load in loads:
        load.start()
    setup_masks(s, seg, segcol)
    vgrad[...] = jnp.zeros_like(vgrad)
    loads[0].wait()
    norm_one(s, tok, vec, act)
    loads[1].wait()
    for block in range(3):
        project_qkv(s, act, wqkv, vec, qkv, block)
    attend(s, 0, s.seqs * s.pairs, qkv, seg, segcol, lse, cot, attT)
    loads[2].wait()
    project_out(s, tok, vec, cot, wout, x2, act, actT)
    load = pltpu.make_async_copy(cot_h, cot, sems.at[5])
    load.start()
    load.wait()
    loads[3].wait()
    loads[4].wait()

    def dump(src, dst):
        copy = pltpu.make_async_copy(src, dst, sems.at[6])
        copy.start()
        copy.wait()

    def tile_step(t, _):
        mlp_tile(s, t, cot, ubias, act, wup, wdown, mo, da2, hid, du, ugrad)
        up_grad(s, actT, du, lambda h: narrow.at[h])
        dump(narrow, gup_h.at[t])
        down_grad(s, hid, cot, lambda h: wide.at[h, pl.ds(0, s.tile)])
        dump(wide.at[:, pl.ds(0, s.tile)], gdown_h.at[t])
        return 0

    lax.fori_loop(0, s.tiles, tile_step, 0)
    datt, dbr, stage = (wdown.at[j * rows : (j + 1) * rows] for j in range(3))
    a1T = wup.at[:, 0:rows]
    norm_two_back(s, cot, vec, x2, mo, da2, stage, dbr, vgrad)
    dump(stage, out_h)
    att_grad(s, dbr, wout, datt)
    out_grad(s, attT, dbr, lambda h: wide.at[h, pl.ds(0, width)])
    dump(wide.at[:, pl.ds(0, width)], gout_h)
    norm_one_flipped(s, tok, vec, a1T)
    for g in range(s.pairs // 2):
        for h in range(2):
            p = 2 * g + h
            attend_back(s, p, qkv, seg, segcol, lse, datt, vgrad.at[2:3, :], vgrad.at[3:4, :])
            qkv_grad(s, a1T, qkv, p, lambda j: thin.at[h, j])
        dump(thin, gqkv_h.at[g])
    norm_one_back(s, tok, vec, qkv, wqkv, x2, stage, vgrad)
    dump(stage, ingrad_h)


MESH = pl.DeviceIdType.MESH
LINK_RATE = 85e3
CORE_RATE = 400e3
LATENCY = 1.5


class Timeline:
    def __init__(self):
        self.now, self.free, self.jobs = 0.0, {}, []

    def begin(self, job):
        self.jobs.append(job)
        self.launch(job, job.first)

    def launch(self, job, made):
        link, cost = made
        start = max(self.now, self.free.get(link, 0.0))
        self.free[link] = start + cost
        job.ready = start + cost + LATENCY

    def advance(self, job):
        self.now = max(self.now, job.ready)
        made = job.steps[job.done]()
        job.done += 1
        if made is None:
            self.jobs.remove(job)
        else:
            self.launch(job, made)

    def tick(self, cost):
        end = self.now + cost
        while True:
            due = [job for job in self.jobs if job.ready <= end]
            if not due:
                break
            job = min(due, key=lambda j: j.ready)
            self.now = max(self.now, min(job.ready, end))
            self.advance(job)
        self.now = max(self.now, end)

    def need(self, job, steps=None):
        while job in self.jobs and (steps is None or job.done < steps):
            self.advance(job)

    def drain(self):
        while self.jobs:
            self.advance(min(self.jobs, key=lambda j: j.ready))


class Job:
    def __init__(self, first, steps):
        self.first, self.steps, self.done, self.ready = first, steps, 0, 0.0


def cut(ref, start, count):
    rows = pl.ds(pl.multiple_of(start, 16), count)
    return ref.at[rows, :] if len(ref.shape) == 2 else ref.at[:, rows, :]


def size_of(ref):
    total = 2
    for n in ref.shape:
        total *= n
    return total


class Place:
    def __init__(self, far):
        d, self.f = lax.axis_index("dp"), lax.axis_index("fsdp")
        self.d, self.far = d, far
        self.c, self.b, self.a = d % 2, (d // 2) % 2, d // 4
        self.core = {"dp": d + 1 - 2 * self.c, "fsdp": self.f}
        self.near = {"dp": d + 2 - 4 * self.b, "fsdp": self.f}
        self.across = {"dp": d, "fsdp": 1 - self.f}

    def other(self, k):
        return {"dp": lax.rem(self.a + k, self.far) * 4 + self.b * 2 + self.c, "fsdp": self.f}


def remote(src, dst, send, recv, device):
    return pltpu.make_async_remote_copy(
        src_ref=src, dst_ref=dst, send_sem=send, recv_sem=recv, device_id=device, device_id_type=MESH
    )


def gather_job(s, me, j, view, sems):
    send, recv = sems
    size = s.width // 2 // 4
    quarter = (me.c * 2 + me.b) * size
    first = remote(view(j, me.f, quarter, size), view(j, me.f, quarter, size), send.at[j, 0], recv.at[j, 0], me.across)
    g = 1 - me.f
    second = remote(view(j, g, quarter, size), view(j, g, quarter, size), send.at[j, 1], recv.at[j, 1], me.near)
    half = me.c * 2 * size
    third = remote(view(j, g, half, 2 * size), view(j, g, half, 2 * size), send.at[j, 2], recv.at[j, 2], me.core)
    cost = 2 * 2 * size * s.width / LINK_RATE

    def step_one():
        first.wait_recv()
        second.start()
        return ("y", cost)

    def step_two():
        second.wait_recv()
        third.start()
        return ("core", 2 * 2 * size * s.width / CORE_RATE)

    def step_three():
        third.wait_recv()
        return None

    first.start()
    return Job(("x", cost), [step_one, step_two, step_three]), [first, second, third]


class Unit:
    def __init__(self, index, own, other, into, out, credit=None):
        self.index, self.own, self.other, self.into, self.out, self.credit = index, own, other, into, out, credit
        self.rows = own.shape[-2]


def unit_job(s, me, unit, send, recv, give, take):
    u, own, far = unit.index, unit.own, me.far
    half, quarter = unit.rows // 2, unit.rows // 4
    piece = quarter // far
    r1, r2, r3, r4 = unit.into
    size = size_of(own)
    mine, mine_b = me.f * half, me.f * half + me.b * quarter
    mine_a = mine_b + me.a * piece
    one = remote(unit.other, r1, send.at[u, 0], recv.at[u, 0], me.core)
    two = remote(cut(own, (1 - me.f) * half, half), r2, send.at[u, 1], recv.at[u, 1], me.across)
    three = remote(cut(own, mine + (1 - me.b) * quarter, quarter), r3, send.at[u, 2], recv.at[u, 2], me.near)
    four, five = [], []
    for k in range(1, far):
        to = lax.rem(me.a + k, far)
        four.append(
            remote(cut(own, mine_b + to * piece, piece), r4[k - 1], send.at[u, 2 + k], recv.at[u, 2 + k], me.other(k))
        )
        target = unit.out(me.b * quarter + me.a * piece, piece)
        five.append(
            remote(cut(own, mine_a, piece), target, send.at[u, 1 + far + k], recv.at[u, 1 + far + k], me.other(k))
        )
    n = 2 * far + 1
    keep = pltpu.make_async_copy(cut(own, mine_a, piece), unit.out(me.b * quarter + me.a * piece, piece), send.at[u, n + 2])
    block = unit.out(me.b * quarter, quarter)
    six = remote(block, block, send.at[u, n], recv.at[u, n], me.near)
    all_rows = unit.out(0, half)
    seven = remote(all_rows, all_rows, send.at[u, n + 1], recv.at[u, n + 1], me.core)

    def add_into(part, arrived):
        part[...] = part[...] + arrived[...]

    def step_one():
        one.wait_recv()
        add_into(own, r1)
        if give is not None:
            pl.semaphore_signal(give, inc=1, device_id=me.core, device_id_type=MESH)
        two.start()
        return ("x", size / LINK_RATE)

    def step_two():
        two.wait_recv()
        add_into(cut(own, mine, half), r2)
        three.start()
        return ("y", size / 2 / LINK_RATE)

    def step_three():
        three.wait_recv()
        add_into(cut(own, mine_b, quarter), r3)
        for copy in four:
            copy.start()
        return ("z", size / 2 / LINK_RATE)

    def step_four():
        total = cut(own, mine_a, piece)
        value = total[...].astype(F32)
        for k, copy in enumerate(four):
            copy.wait_recv()
            value = value + r4[k][...].astype(F32)
        total[...] = value.astype(BF)
        keep.start()
        for copy in five:
            copy.start()
        return ("z", size / 2 / LINK_RATE)

    def step_five():
        keep.wait()
        for copy in five:
            copy.wait_recv()
        six.start()
        return ("y", size / 2 / LINK_RATE)

    def step_six():
        six.wait_recv()
        seven.start()
        return ("core", size / 2 / CORE_RATE)

    def step_seven():
        seven.wait_recv()
        return None

    if take is not None:
        pl.semaphore_wait(take, 1)
    one.start()
    steps = [step_one, step_two, step_three, step_four, step_five, step_six, step_seven]
    return Job(("core", size / CORE_RATE), steps), one, [two, three, *four, *five, six, seven]


def exchange_vectors(me, slots, sends, recvs):
    core_s, x_s, near_s, far_s = slots
    pairs = ((core_s, me.c, me.core, 0), (x_s, me.f, me.across, 1), (near_s, me.b, me.near, 2))
    for n, (slot, mine, device, i) in enumerate(pairs):
        copy = remote(slot.at[mine], slot.at[mine], sends.at[i], recvs.at[i], device)
        copy.start()
        copy.wait()
        total = slot[0] + slot[1]
        if n < 2:
            pairs[n + 1][0][pairs[n + 1][1]] = total
        else:
            far_s[me.a] = total
    copies = [
        remote(far_s.at[me.a], far_s.at[me.a], sends.at[2 + k], recvs.at[2 + k], me.other(k)) for k in range(1, me.far)
    ]
    for copy in copies:
        copy.start()
    for copy in copies:
        copy.wait()
    total = far_s[0]
    for k in range(1, me.far):
        total = total + far_s[k]
    return total


def linked_kernel(
    s, far, tok_h, cot_h, seg, small, wqkv_h, wout_h, wup_h, wdown_h,
    out_h, ingrad_h, gqkv_h, gout_h, gup_h, gdown_h, vout,
    tok, cot, act, actT, attT, qkv, x2, mo, da2, hid, du,
    wqkv, wout, wup, wdown, segcol, lse, packed, vec, ubias, ugrad, core_s, x_s, near_s, far_s,
    own_up, own_down, own_qkv, oth_up, oth_down, oth_qkv,
    r1_up, r1_down, r1_out, r1_qkv, r2_up, r2_down, r2_out, r2_qkv,
    r3_up, r3_down, r3_out, r3_qkv, r4_up, r4_down, r4_out, r4_qkv,
    loads, wsend, wrecv, usend, urecv, vsend, vrecv, credit,
):
    rows, width = s.rows, s.width
    me = Place(far)
    line = Timeline()
    shard = width // 2
    count = s.hidden // width
    folds = s.hidden // 2 // shard

    barrier = pltpu.get_barrier_semaphore()
    partners = [me.core, me.near, me.across] + [me.other(k) for k in range(1, far)]
    for device in partners:
        pl.semaphore_signal(barrier, inc=1, device_id=device, device_id_type=MESH)

    names = [("qkv", 0), ("qkv", 1), ("qkv", 2), ("out", 0)]
    order = [i for k in range(count // 2) for i in (k, k + count // 2)]
    for n in range(0, count, 2):
        names += [("up", order[n]), ("up", order[n + 1]), ("down", n), ("down", n + 1)]

    def view(j, f, start, size):
        kind, i = names[j]
        if kind == "down":
            return wdown.at[pl.ds(pl.multiple_of(f * s.share + i * shard + start, 16), size), :]
        part = pl.ds(pl.multiple_of(f * shard + start, 16), size)
        if kind == "out":
            return wout.at[part, :]
        return (wqkv if kind == "qkv" else wup).at[part, i * width : (i + 1) * width]

    def master(j):
        kind, i = names[j]
        if kind == "down":
            return wdown_h.at[i * shard : (i + 1) * shard, :]
        if kind == "out":
            return wout_h.at[...]
        return (wqkv_h if kind == "qkv" else wup_h).at[:, i * width : (i + 1) * width]

    stages = [mo.at[0:shard], mo.at[shard : 2 * shard], da2.at[0:shard], da2.at[shard : 2 * shard]]
    copies = [
        pltpu.make_async_copy(master(j), stages[j % 4], loads.at[j % 4]) for j in range(len(names))
    ]
    for j in range(4):
        copies[j].start()
    load_tok = pltpu.make_async_copy(tok_h, tok, loads.at[4])
    load_tok.start()
    packed[me.f] = small[...]
    share_small = remote(packed.at[me.f], packed.at[me.f], vsend.at[2 + far], vrecv.at[2 + far], me.across)
    pl.semaphore_wait(barrier, len(partners))
    share_small.start()
    sent, moved, jobs = [share_small], [], []
    for j in range(len(names)):
        copies[j].wait()
        view(j, me.f, 0, shard)[...] = stages[j % 4][...].astype(BF)
        if j + 4 < len(names):
            copies[j + 4].start()
        job, made = gather_job(s, me, j, view, (wsend, wrecv))
        line.begin(job)
        line.now += 0.5
        jobs.append(job)
        (moved if names[j][0] in ("up", "down") else sent).extend(made)
    setup_masks(s, seg, segcol)
    core_s[...] = jnp.zeros_like(core_s)
    share_small.wait_recv()
    for f in range(2):
        vec[:, f * shard : (f + 1) * shard] = packed[f, 0:8, :]
        for i in range(folds):
            ubias[f, :, i * shard : (i + 1) * shard] = packed[f, 8 + i : 9 + i, :]
    load_tok.wait()
    norm_one(s, tok, vec, act)
    line.tick(3.0)
    for block in range(3):
        line.need(jobs[block])
        project_qkv(s, act, wqkv, vec, qkv, block)
        line.tick(1.5)
    for n in range(s.seqs * s.pairs // 2):
        attend(s, 2 * n, 2, qkv, seg, segcol, lse, cot, attT)
        line.tick(2.5)
    line.need(jobs[3])
    project_out(s, tok, vec, cot, wout, x2, act, actT)
    load_cot = pltpu.make_async_copy(cot_h, cot, loads.at[5])
    load_cot.start()
    line.tick(2.5)

    c = me.c
    units, firsts, later = [], [], []
    pending = {}

    def start_unit(unit, kind=None, slot=0, reuse=False, again=False):
        give = credit.at[kind * 2 + slot] if again else None
        take = credit.at[kind * 2 + slot] if reuse else None
        job, one, made = unit_job(s, me, unit, usend, urecv, give, take)
        line.begin(job)
        later.extend(made)
        return job, one

    vgrad = core_s.at[c]
    load_cot.wait()
    for t in range(s.tiles):
        for j, (kind, i) in enumerate(names):
            if kind == "up":
                lo, hi = i * width, (i + 1) * width
                used = any(f * s.share + t * s.piece < hi and f * s.share + (t + 1) * s.piece > lo for f in range(2))
            elif kind == "down":
                used = t * s.piece < (i + 1) * shard and (t + 1) * s.piece > i * shard
            else:
                used = False
            if used:
                line.need(jobs[j])
        slot = t % 2
        mlp_tile(s, t, cot, ubias, act, wup, wdown, mo, da2, hid, du, ugrad)
        line.tick(4.0)
        if t >= 2:
            job, one = pending["up", t - 2]
            line.need(job, 1)
            one.wait_send()
        up_grad_linked(s, actT, du, c, own_up.at[t], oth_up.at[slot])
        unit = Unit(
            2 * t, own_up.at[t], oth_up.at[slot],
            (r1_up.at[slot], r2_up.at[t], r3_up.at[t], [r4_up.at[t, k] for k in range(far - 1)]),
            lambda start, n, t=t: gup_h.at[pl.ds(pl.multiple_of(start, 16), n), span(c * s.share + t * s.piece, s.piece)],
        )
        pending["up", t] = start_unit(unit, 0, slot, t >= 2, t + 2 < s.tiles)
        line.tick(1.3)
        if t >= 2:
            job, one = pending["down", t - 2]
            line.need(job, 1)
            one.wait_send()
        down_grad_linked(s, hid, cot, c, own_down.at[t], oth_down.at[slot])
        unit = Unit(
            2 * t + 1, own_down.at[t], oth_down.at[slot],
            (r1_down.at[slot], r2_down.at[t], r3_down.at[t], [r4_down.at[t, k] for k in range(far - 1)]),
            lambda start, n, t=t: gdown_h.at[
                pl.ds(pl.multiple_of(t * s.piece + start, 16), n), span(c * shard, shard)
            ],
        )
        pending["down", t] = start_unit(unit, 1, slot, t >= 2, t + 2 < s.tiles)
        line.tick(1.3)
    for job in jobs:
        line.need(job)
    for copy in moved:
        copy.wait_send()
    datt, dbr, stage = (wdown.at[j * rows : (j + 1) * rows] for j in range(3))
    a1T = wup.at[:, 0:rows]
    own_out, oth_out = (wup.at[:, rows + j * shard : rows + (j + 1) * shard] for j in range(2))
    norm_two_back(s, cot, vec, x2, mo, da2, stage, dbr, vgrad)
    save_out = pltpu.make_async_copy(stage, out_h, loads.at[5])
    save_out.start()
    line.tick(2.5)
    out_grad_linked(s, attT, dbr, c, own_out, oth_out)
    unit = Unit(
        2 * s.tiles, own_out, oth_out,
        (r1_out, r2_out, r3_out, [r4_out.at[k] for k in range(far - 1)]),
        lambda start, n: gout_h.at[pl.ds(pl.multiple_of(start, 16), n), span(c * shard, shard)],
    )
    pending["out"] = start_unit(unit)
    line.tick(1.3)
    att_grad(s, dbr, wout, datt)
    norm_one_flipped(s, tok, vec, a1T)
    line.tick(3.0)
    for g in range(s.pairs // 2):
        for h in range(2):
            attend_back(s, 2 * g + h, qkv, seg, segcol, lse, datt, vgrad.at[2:3, :], vgrad.at[3:4, :])
            line.tick(5.0)
        qkv_grad_linked(s, a1T, qkv, g, c, own_qkv.at[g], oth_qkv.at[g])
        unit = Unit(
            2 * s.tiles + 1 + g, own_qkv.at[g], oth_qkv.at[g],
            (r1_qkv.at[g], r2_qkv.at[g], r3_qkv.at[g], [r4_qkv.at[g, k] for k in range(far - 1)]),
            lambda start, n, g=g: gqkv_h.at[
                :, pl.ds(pl.multiple_of(start, 16), n), span((2 * g + c) * 128, 128)
            ],
        )
        pending["qkv", g] = start_unit(unit)
        line.tick(1.5)
    save_out.wait()
    norm_one_back(s, tok, vec, qkv, wqkv, x2, stage, vgrad)
    line.tick(5.0)
    save_in = pltpu.make_async_copy(stage, ingrad_h, loads.at[4])
    save_in.start()
    part = math.gcd(s.share, width)
    for i in range(s.hidden // part):
        start = i * part
        f, off = start // s.share, start % s.share
        r, col = 8 + start // width, start % width
        vgrad[r : r + 1, col : col + part] = ugrad[f, :, off : off + part]
    total = exchange_vectors(me, (core_s, x_s, near_s, far_s), vsend, vrecv)
    far_s[0] = total
    vout[...] = far_s[0, :, pl.ds(pl.multiple_of(me.f * shard, shard), shard)]
    for i in range(folds):
        start = i * shard
        for f in range(2):
            flat = f * s.share + start
            r, col = 8 + flat // width, flat % width

            @pl.when(me.f == f)
            def _(r=r, col=col, i=i):
                vout[8 + i : 9 + i, :] = far_s[0, r : r + 1, col : col + shard]

    line.drain()
    save_in.wait()
    for key, (job, one) in pending.items():
        if key == "out" or key[0] == "qkv" or key[1] + 2 >= s.tiles:
            one.wait_send()
    for copy in later + sent:
        copy.wait_send()


def split_store(c, value, own, other, rows):
    half = value.shape[-1] // 2
    left, right = value[:, :half].astype(BF), value[:, half:].astype(BF)
    own[rows, :] = jnp.where(c == 0, left, right)
    other[rows, :] = jnp.where(c == 0, right, left)


def up_grad_linked(s, a2T, du, c, own, other):
    def step(r, _):
        rows = at(r, ROWS)
        split_store(c, dot_nn(a2T[rows, :], du[...]), own, other, rows)
        return 0

    lax.fori_loop(0, s.width // ROWS, step, 0)


def down_grad_linked(s, hid, cot, c, own, other):
    def step(r, _):
        rows = at(r, ROWS)
        split_store(c, dot_tn(hid[:, rows], cot[...]), own, other, rows)
        return 0

    lax.fori_loop(0, s.tile // ROWS, step, 0)


def out_grad_linked(s, attT, dbr, c, own, other):
    def step(r, _):
        rows = at(r, ROWS)
        split_store(c, dot_nn(attT[rows, :], dbr[...]), own, other, rows)
        return 0

    lax.fori_loop(0, s.width // ROWS, step, 0)


def qkv_grad_linked(s, a1T, dqkv, g, c, own, other):
    width = s.width

    def step(r, _):
        rows = at(r, ROWS)
        for j in range(3):
            start = j * width + 2 * g * 128
            value = dot_nn(a1T[rows, :], dqkv[:, start : start + 256])
            left, right = value[:, :128].astype(BF), value[:, 128:].astype(BF)
            own[j, rows, :] = jnp.where(c == 0, left, right)
            other[j, rows, :] = jnp.where(c == 0, right, left)
        return 0

    lax.fori_loop(0, width // ROWS, step, 0)


def linked_body(far, tokens, segment_ids, cotangent, *params):
    (
        norm1_gain, norm1_shift, qkv_weight, query_bias, value_bias, out_weight, out_bias, norm2_gain, norm2_shift,
        up_weight, up_bias, down_weight, down_bias,
    ) = params
    rows, width = tokens.shape
    hidden = up_weight.shape[1]
    s = Sizes(rows, width, hidden, 2)
    shard, tiles, tile, groups = width // 2, s.tiles, s.tile, s.pairs // 2
    vectors = [norm1_gain, norm1_shift, query_bias, value_bias, out_bias, norm2_gain, norm2_shift, down_bias]
    small = jnp.concatenate([jnp.stack(vectors), up_bias.reshape(-1, shard), jnp.zeros((4, shard), F32)])
    small = small.astype(BF).astype(F32)
    seg = segment_ids.reshape(s.seqs, 1, SEQ)
    whole = pl.BlockSpec(memory_space=pltpu.VMEM)
    away = pl.BlockSpec(memory_space=pl.ANY)

    def vm(*shape, kind=BF):
        return pltpu.VMEM(shape, kind)

    n_units, n_blocks = 2 * tiles + 1 + groups, 4 + 2 * (hidden // width)
    up, down, out, qk = (width, tile // 2), (tile, shard), (width, shard), (3, width, 128)

    def part(shape, by):
        return shape[:-2] + (shape[-2] // by, shape[-1])

    slots = min(2, tiles)
    scratch = [
        vm(rows, width), vm(rows, width), vm(rows, width), vm(width, rows), vm(width, rows), vm(rows, 3 * width),
        vm(rows, width, kind=F32), vm(rows, width, kind=F32), vm(rows, width, kind=F32), vm(rows, tile), vm(rows, tile),
        vm(width, 3 * width), vm(width, width), vm(width, hidden), vm(hidden, width),
        vm(s.seqs, SEQ, 128, kind=F32), vm(s.seqs * HEADS, 1, SEQ, kind=F32),
        vm(2, 16, shard, kind=F32), vm(8, width, kind=F32), vm(2, 1, s.share, kind=F32), vm(2, 1, s.share, kind=F32),
        vm(2, 16, width, kind=F32), vm(2, 16, width, kind=F32), vm(2, 16, width, kind=F32), vm(far, 16, width, kind=F32),
        vm(tiles, *up), vm(tiles, *down), vm(groups, *qk),
        vm(slots, *up), vm(slots, *down), vm(groups, *qk),
        vm(slots, *up), vm(slots, *down), vm(*out), vm(groups, *qk),
        vm(tiles, *part(up, 2)), vm(tiles, *part(down, 2)), vm(*part(out, 2)), vm(groups, *part(qk, 2)),
        vm(tiles, *part(up, 4)), vm(tiles, *part(down, 4)), vm(*part(out, 4)), vm(groups, *part(qk, 4)),
        vm(tiles, far - 1, *part(up, 4 * far)), vm(tiles, far - 1, *part(down, 4 * far)),
        vm(far - 1, *part(out, 4 * far)), vm(groups, far - 1, *part(qk, 4 * far)),
        pltpu.SemaphoreType.DMA((6,)),
        pltpu.SemaphoreType.DMA((n_blocks, 3)),
        pltpu.SemaphoreType.DMA((n_blocks, 3)),
        pltpu.SemaphoreType.DMA((n_units, 2 * far + 4)),
        pltpu.SemaphoreType.DMA((n_units, 2 * far + 3)),
        pltpu.SemaphoreType.DMA((far + 3,)),
        pltpu.SemaphoreType.DMA((far + 3,)),
        pltpu.SemaphoreType.REGULAR((4,)),
    ]
    output, input_grad, gqkv, gout, gup, gdown, v = pl.pallas_call(
        functools.partial(linked_kernel, s, far),
        out_shape=(
            jax.ShapeDtypeStruct((rows, width), BF),
            jax.ShapeDtypeStruct((rows, width), BF),
            jax.ShapeDtypeStruct((3, shard, width), BF),
            jax.ShapeDtypeStruct((shard, width), BF),
            jax.ShapeDtypeStruct((shard, hidden), BF),
            jax.ShapeDtypeStruct((hidden // 2, width), BF),
            jax.ShapeDtypeStruct((16, shard), F32),
        ),
        in_specs=[away, away, whole, whole, away, away, away, away],
        out_specs=(away,) * 6 + (whole,),
        scratch_shapes=scratch,
        compiler_params=pltpu.CompilerParams(
            vmem_limit_bytes=61 << 20, collective_id=0, has_side_effects=True
        ),
    )(tokens, cotangent, seg, small, qkv_weight, out_weight, up_weight, down_weight)
    gqkv = jnp.concatenate([gqkv[0], gqkv[1], gqkv[2]], 1).astype(F32)
    return (
        output, input_grad, v[0], v[1], gqkv, v[2], v[3], gout.astype(F32), v[4], v[5], v[6],
        gup.astype(F32), v[8 : 8 + s.share // shard].reshape(-1), gdown.astype(F32), v[7],
    )


def body(
    tokens, segment_ids, cotangent, norm1_gain, norm1_shift, qkv_weight, query_bias, value_bias,
    out_weight, out_bias, norm2_gain, norm2_shift, up_weight, up_bias, down_weight, down_bias,
):
    shards = lax.axis_size("fsdp")
    rows, width = tokens.shape
    hidden = up_weight.shape[1]
    s = Sizes(rows, width, hidden, shards)
    small = [norm1_gain, norm1_shift, query_bias, value_bias, out_bias, norm2_gain, norm2_shift, down_bias]
    vec = lax.all_gather(jnp.stack(small).astype(BF), "fsdp", axis=1, tiled=True).astype(F32)
    ubias = lax.all_gather(up_bias.astype(BF), "fsdp", axis=0).astype(F32)[:, None, :]
    weights = [
        lax.all_gather(w.astype(BF), "fsdp", axis=0, tiled=True)
        for w in (qkv_weight, out_weight, up_weight, down_weight)
    ]
    seg = segment_ids.reshape(s.seqs, 1, SEQ)
    whole = pl.BlockSpec(memory_space=pltpu.VMEM)
    away = pl.BlockSpec(memory_space=pl.ANY)
    groups = s.pairs // 2
    results = pl.pallas_call(
        functools.partial(block_kernel, s),
        out_shape=(
            jax.ShapeDtypeStruct((rows, width), BF),
            jax.ShapeDtypeStruct((rows, width), BF),
            jax.ShapeDtypeStruct((groups, 2, 3, width, 128), BF),
            jax.ShapeDtypeStruct((2, width, width // 2), BF),
            jax.ShapeDtypeStruct((s.tiles, 2, width, s.tile // 2), BF),
            jax.ShapeDtypeStruct((s.tiles, 2, s.tile, width // 2), BF),
            jax.ShapeDtypeStruct((8, width), F32),
            jax.ShapeDtypeStruct((shards, 1, s.share), F32),
        ),
        in_specs=[away, away, whole, whole, whole, away, away, away, away],
        out_specs=(away,) * 6 + (whole, whole),
        scratch_shapes=[
            pltpu.VMEM((rows, width), BF),
            pltpu.VMEM((rows, width), BF),
            pltpu.VMEM((rows, width), BF),
            pltpu.VMEM((width, rows), BF),
            pltpu.VMEM((width, rows), BF),
            pltpu.VMEM((rows, 3 * width), BF),
            pltpu.VMEM((rows, width), F32),
            pltpu.VMEM((rows, width), F32),
            pltpu.VMEM((rows, width), F32),
            pltpu.VMEM((rows, s.tile), BF),
            pltpu.VMEM((rows, s.tile), BF),
            pltpu.VMEM((width, 3 * width), BF),
            pltpu.VMEM((width, width), BF),
            pltpu.VMEM((width, hidden), BF),
            pltpu.VMEM((hidden, width), BF),
            pltpu.VMEM((s.seqs, SEQ, 128), F32),
            pltpu.VMEM((s.seqs * HEADS, 1, SEQ), F32),
            pltpu.VMEM((2, width, s.tile // 2), BF),
            pltpu.VMEM((2, max(width, s.tile), width // 2), BF),
            pltpu.VMEM((2, 3, width, 128), BF),
            pltpu.SemaphoreType.DMA((8,)),
        ],
        compiler_params=pltpu.CompilerParams(vmem_limit_bytes=61 << 20),
    )(tokens, cotangent, seg, vec, ubias, *weights)
    output, input_grad, gqkv, gout, gup, gdown, vgrad, ugrad = results
    gqkv = gqkv.transpose(3, 2, 0, 1, 4).reshape(width, 3 * width)
    gout = gout.transpose(1, 0, 2).reshape(width, width)
    half = s.tile // 2
    gup = gup.transpose(2, 0, 1, 3).reshape(width, s.tiles, shards, s.piece)
    gup = gup.transpose(0, 2, 1, 3).reshape(width, hidden)
    gdown = gdown.transpose(0, 2, 1, 3).reshape(s.tiles, shards, s.piece, width)
    gdown = gdown.transpose(1, 0, 2, 3).reshape(hidden, width)

    def summed(value):
        part = lax.psum_scatter(value.astype(BF), "fsdp", scatter_dimension=0, tiled=True)
        return lax.psum(part, "dp").astype(F32)

    gqkv, gout, gup, gdown = [summed(v) for v in (gqkv, gout, gup, gdown)]
    ugrad = summed(ugrad.reshape(hidden))
    v = [summed(vgrad[i]) for i in range(8)]
    return (
        output, input_grad, v[0], v[1], gqkv, v[2], v[3], gout, v[4], v[5], v[6], gup, ugrad, gdown, v[7],
    )


def solution(mesh):
    rows, wide, long = P(("dp", "fsdp"), None), P("fsdp", None), P("fsdp")
    shards, copies = mesh.shape["fsdp"], mesh.shape["dp"]
    linked = shards == 2 and copies % 4 == 0 and 4 < copies <= 16
    return jax.shard_map(
        functools.partial(linked_body, copies // 4) if linked else body,
        mesh=mesh,
        in_specs=(
            rows, P(("dp", "fsdp")), rows, long, long, wide, long, long, wide, long, long, long, wide, long, wide, long,
        ),
        out_specs=(
            rows, rows, long, long, wide, long, long, wide, long, long, long, wide, long, wide, long,
        ),
        check_vma=False,
    )
```

```python
import functools
import math

import jax
import jax.numpy as jnp
from jax import lax
from jax.experimental import pallas as pl
from jax.experimental.pallas import tpu as pltpu
from jax.sharding import PartitionSpec as P

HEADS = 12
SEQ = 512
EPSILON = 1e-06
LARGE_NEG = -1000000000.0
BF = jnp.bfloat16
F32 = jnp.float32
ROWS = 512
WIDE = 384
DIRECT = 0
QUEUE = 1.0


def dot_of(left, right, over):
    return lax.dot_general(left, right, (over, ((), ())), preferred_element_type=F32)


def dot_nn(left, right):
    return dot_of(left, right, ((1,), (0,)))


def dot_nt(left, right):
    return dot_of(left, right, ((1,), (1,)))


def dot_tn(left, right):
    return dot_of(left, right, ((0,), (0,)))


def at(index, size):
    return pl.ds(pl.multiple_of(index * size, size), size)


def span(start, size):
    return pl.ds(pl.multiple_of(start, 128), size)


def mean_of(value):
    return jnp.sum(value, -1, keepdims=True) * (1.0 / value.shape[-1])


def normed(value):
    centre = value - mean_of(value)
    inverse = lax.rsqrt(mean_of(centre * centre) + EPSILON)
    return centre * inverse, inverse


def down_sum(value):
    return jnp.sum(value, 0, keepdims=True)


def gelu_pair(value):
    cumulative = 0.5 + 0.5 * lax.erf(value * 0.7071067811865476)
    density = jnp.exp(-0.5 * value * value) * 0.3989422804014327
    return value * cumulative, cumulative + value * density


def norm_back(grad, xhat, inverse, gain):
    scaled = grad * gain
    return inverse * (scaled - mean_of(scaled) - xhat * mean_of(scaled * xhat))


class Sizes:
    def __init__(self, rows, width, hidden, shards):
        self.rows, self.width, self.hidden, self.shards = rows, width, hidden, shards
        self.seqs = rows // SEQ
        self.pairs = HEADS // 2
        share = hidden // shards
        self.tiles = max(n for n in range(1, 7) if share % n == 0 and (share // n) % 128 == 0)
        self.share = share
        self.piece = share // self.tiles
        self.tile = self.piece * shards
        self.blocks = rows // ROWS


def setup_masks(s, seg, segcol):
    for i in range(s.seqs):
        segcol[i] = jnp.broadcast_to(seg[i].astype(F32), (128, SEQ)).T


def norm_one(s, tok, vec, a1):
    def step(i, _):
        rows = at(i, ROWS)
        xhat, _inv = normed(tok[rows, :].astype(F32))
        a1[rows, :] = (xhat * vec[0:1, :] + vec[1:2, :]).astype(BF)
        return 0

    lax.fori_loop(0, s.blocks, step, 0)


def norm_one_flipped(s, tok, vec, a1T):
    def step(i, _):
        rows = at(i, ROWS)
        xhat, _inv = normed(tok[rows, :].astype(F32))
        a1T[:, rows] = (xhat * vec[0:1, :] + vec[1:2, :]).T.astype(BF)
        return 0

    lax.fori_loop(0, s.blocks, step, 0)


def project_qkv(s, act, wqkv, vec, qkv, group):
    width = s.width
    n = width // 3
    cols = slice(group * n, group * n + n)
    for j in range(3):
        lin = dot_nn(act[...], wqkv[j, :, cols])
        if j != 1:
            row = 2 + j // 2
            lin = lin + vec[row : row + 1, cols]
        qkv[:, j * width + group * n : j * width + group * n + n] = lin.astype(BF)


def allowed_of(seg, segcol, i):
    col = segcol[i]
    full = jnp.concatenate([col] * (SEQ // 128), axis=1)
    return full == seg[i].astype(F32)


def lane_of(half):
    lanes = lax.broadcasted_iota(jnp.int32, (1, 128), 1)
    return (lanes < 64) if half == 0 else (lanes >= 64)


def pick_lanes(half, value):
    return jnp.where(lane_of(half), value, jnp.zeros_like(value))


def attend(s, group, qkv, seg, segcol, lse, att, attT):
    width, count = s.width, s.pairs // 3

    def step(i, _):
        rows = at(i, SEQ)
        ok = allowed_of(seg, segcol, i)
        items, raws, outs = [], {}, {}
        for p in range(group * count, group * count + count):
            q = qkv[rows, p * 128 : p * 128 + 128] * jnp.asarray(0.125, BF)
            k = qkv[rows, width + p * 128 : width + p * 128 + 128]
            vT = qkv[rows, 2 * width + p * 128 : 2 * width + p * 128 + 128].T
            items += [(p, q, k, vT, half) for half in (0, 1)]

        def raw(x):
            _p, q, k, _v, half = items[x]
            raws[x] = dot_nt(k, pick_lanes(half, q))

        def soft(x):
            p, _q, _k, _v, half = items[x]
            scores = jnp.where(ok, raws[x], LARGE_NEG)
            top = jnp.max(scores, 0, keepdims=True)
            expo = jnp.exp(scores - top)
            total = jnp.sum(expo, 0, keepdims=True)
            lse[2 * (i * s.pairs + p) + half] = top + jnp.log(total)
            outs[x] = expo.astype(BF), 1.0 / total

        def out(x):
            p, _q, _k, vT, half = items[x]
            expo, inverse = outs[x]
            outs[x] = dot_nn(vT[64 * half : 64 * half + 64], expo) * inverse
            if half == 1:
                both = jnp.concatenate([outs[x - 1], outs[x]], 0)
                attT[p * 128 : p * 128 + 128, rows] = both.astype(BF)
                att[rows, p * 128 : p * 128 + 128] = both.T.astype(BF)

        raw(0)
        for x in range(len(items)):
            if x + 1 < len(items):
                raw(x + 1)
            soft(x)
            if x >= 1:
                out(x - 1)
        out(len(items) - 1)
        return 0

    lax.fori_loop(0, s.seqs, step, 0)


def project_out(s, tok, vec, att, wout, x2, a2, a2T):
    def step(i, _):
        rows = at(i, ROWS)
        value = tok[rows, :].astype(F32) + (dot_nn(att[rows, :], wout[...]) + vec[4:5, :])
        x2[rows, :] = value
        xhat, _inv = normed(value)
        act = xhat * vec[5:6, :] + vec[6:7, :]
        a2[rows, :] = act.astype(BF)
        a2T[:, rows] = act.T.astype(BF)
        return 0

    lax.fori_loop(0, s.blocks, step, 0)


def mlp_tile(s, t, first, count, cot, ubias, a2, wup, wdown, mo, da2, hid, du, ugrad):
    starts = [f * s.share + t * s.piece for f in range(s.shards)]
    fresh = t == 0

    def step(i, sums):
        rows = at(first + i, ROWS)
        act, dy = a2[rows, :], cot[rows, :]
        more, back = 0.0, 0.0
        parts = []
        for f, start in enumerate(starts):
            up, down = wup[:, span(start, s.piece)], wdown[span(start, s.piece), :]
            u = dot_nn(act, up) + ubias[f, :, at(t, s.piece)]
            h, slope = gelu_pair(u)
            h = h.astype(BF)
            d = (dot_nt(dy, down) * slope).astype(BF)
            hid[rows, f * s.piece : (f + 1) * s.piece] = h
            du[rows, f * s.piece : (f + 1) * s.piece] = d
            more = more + dot_nn(h, down)
            back = back + dot_nt(d, up)
            parts.append(down_sum(d.astype(F32)))
        mo[rows, :] = jnp.where(fresh, 0.0, mo[rows, :]) + more
        da2[rows, :] = jnp.where(fresh, 0.0, da2[rows, :]) + back
        return tuple(a + b for a, b in zip(sums, parts))

    zero = jnp.zeros((1, s.piece), F32)
    sums = lax.fori_loop(0, count, step, (zero,) * s.shards)
    for f in range(s.shards):
        ugrad[f, :, at(t, s.piece)] = sums[f] + (ugrad[f, :, at(t, s.piece)] if first else 0.0)


def up_grad(s, a2T, du, unit):
    half = s.tile // 2

    def step(r, _):
        rows = at(r, WIDE)
        value = dot_nn(a2T[rows, :], du[...]).astype(BF)
        unit(0)[rows, :] = value[:, :half]
        unit(1)[rows, :] = value[:, half:]
        return 0

    lax.fori_loop(0, s.width // WIDE, step, 0)


def down_grad(s, hid, cot, unit):
    half = s.width // 2

    def step(r, _):
        rows = at(r, ROWS)
        value = dot_tn(hid[:, rows], cot[...]).astype(BF)
        unit(0)[rows, :] = value[:, :half]
        unit(1)[rows, :] = value[:, half:]
        return 0

    lax.fori_loop(0, s.tile // ROWS, step, 0)


def norm_two_back(s, cot, vec, x2, mo, da2, out, dbr, vgrad):
    def step(i, sums):
        rows = at(i, ROWS)
        value = x2[rows, :]
        dy = cot[rows, :].astype(F32)
        out[rows, :] = (value + (mo[rows, :] + vec[7:8, :])).astype(BF)
        xhat, inverse = normed(value)
        grad = da2[rows, :]
        total = dy + norm_back(grad, xhat, inverse, vec[5:6, :])
        x2[rows, :] = total
        low = total.astype(BF)
        dbr[rows, :] = low
        return tuple(
            a + down_sum(b) for a, b in zip(sums, (low.astype(F32), grad * xhat, grad, dy))
        )

    zero = jnp.zeros((1, s.width), F32)
    sums = lax.fori_loop(0, s.blocks, step, (zero,) * 4)
    for j, value in enumerate(sums):
        vgrad[4 + j : 5 + j, :] = value


def att_grad(s, dbr, wout, datt):
    def step(i, _):
        rows = at(i, ROWS)
        datt[rows, :] = dot_nt(dbr[rows, :], wout[...]).astype(BF)
        return 0

    lax.fori_loop(0, s.blocks, step, 0)


def out_grad(s, attT, dbr, unit):
    half = s.width // 2

    def step(r, _):
        rows = at(r, WIDE)
        value = dot_nn(attT[rows, :], dbr[...]).astype(BF)
        unit(0)[rows, :] = value[:, :half]
        unit(1)[rows, :] = value[:, half:]
        return 0

    lax.fori_loop(0, s.width // WIDE, step, 0)


def attend_back(s, p, qkv, seg, segcol, lse, datt, qsum, vsum):
    width = s.width
    qc, kc, vc = [slice(j * width + p * 128, j * width + p * 128 + 128) for j in range(3)]

    def step(i, sums):
        rows = at(i, SEQ)
        q = qkv[rows, qc] * jnp.asarray(0.125, BF)
        k, v, g = qkv[rows, kc], qkv[rows, vc], datt[rows, qc]
        kT = k.T
        ok = allowed_of(seg, segcol, i)
        dqs, dks, dvs = [], [], []
        for half in (0, 1):
            scores = jnp.where(ok, dot_nt(k, pick_lanes(half, q)), LARGE_NEG)
            prob = jnp.exp(scores - lse[2 * (i * s.pairs + p) + half])
            dprob = dot_nt(v, pick_lanes(half, g))
            weighted = jnp.sum(prob * dprob, 0, keepdims=True)
            dscore = (prob * (dprob - weighted)).astype(BF)
            dvs.append(dot_nn(prob.astype(BF), g))
            dks.append(dot_nn(dscore, q))
            dqs.append(dot_nn(kT[64 * half : 64 * half + 64], dscore))
        mask = lane_of(0)
        dq = (jnp.concatenate(dqs, 0) * 0.125).T.astype(BF)
        dk = jnp.where(mask, dks[0], dks[1]).astype(BF)
        dv = jnp.where(mask, dvs[0], dvs[1]).astype(BF)
        qkv[rows, qc] = dq
        qkv[rows, kc] = dk
        qkv[rows, vc] = dv
        return sums[0] + down_sum(dq.astype(F32)), sums[1] + down_sum(dv.astype(F32))

    zero = jnp.zeros((1, 128), F32)
    qs, vs = lax.fori_loop(0, s.seqs, step, (zero, zero))
    qsum[:, p * 128 : p * 128 + 128] = qs
    vsum[:, p * 128 : p * 128 + 128] = vs


def qkv_grad(s, a1T, dqkv, p, part):
    width = s.width

    def step(r, _):
        rows = at(r, WIDE)
        for j in range(3):
            cols = slice(j * width + p * 128, j * width + p * 128 + 128)
            part(j)[rows, :] = dot_nn(a1T[rows, :], dqkv[:, cols]).astype(BF)
        return 0

    lax.fori_loop(0, width // WIDE, step, 0)


def norm_one_back(s, tok, vec, dqkv, wqkv, dx2, ingrad, vgrad):
    def step(i, sums):
        rows = at(i, ROWS)
        width = s.width
        grad = sum(dot_nt(dqkv[rows, j * width : (j + 1) * width], wqkv[j]) for j in range(3))
        xhat, inverse = normed(tok[rows, :].astype(F32))
        ingrad[rows, :] = (dx2[rows, :] + norm_back(grad, xhat, inverse, vec[0:1, :])).astype(BF)
        return sums[0] + down_sum(grad * xhat), sums[1] + down_sum(grad)

    zero = jnp.zeros((1, s.width), F32)
    sums = lax.fori_loop(0, s.blocks, step, (zero,) * 2)
    vgrad[0:1, :] = sums[0]
    vgrad[1:2, :] = sums[1]


def block_kernel(
    s, tok_h, cot_h, seg, vec, ubias, wqkv_h, wout_h, wup_h, wdown_h,
    out_h, ingrad_h, gqkv_h, gout_h, gup_h, gdown_h, vgrad, ugrad,
    tok, cot, act, actT, attT, qkv, x2, mo, da2, hid, du,
    wqkv, wout, wup, wdown, segcol, lse, narrow, wide, thin, sems,
):
    rows, width = s.rows, s.width
    loads = [
        pltpu.make_async_copy(a, b, sems.at[i])
        for i, (a, b) in enumerate(
            [(tok_h, tok), (wout_h, wout), (wup_h, wup), (wdown_h, wdown)]
            + [(wqkv_h.at[:, j * width : (j + 1) * width], wqkv.at[j]) for j in range(3)]
        )
    ]
    for load in loads:
        load.start()
    setup_masks(s, seg, segcol)
    vgrad[...] = jnp.zeros_like(vgrad)
    loads[0].wait()
    norm_one(s, tok, vec, act)
    for load in loads[4:]:
        load.wait()
    for group in range(3):
        project_qkv(s, act, wqkv, vec, qkv, group)
        attend(s, group, qkv, seg, segcol, lse, cot, attT)
    loads[1].wait()
    project_out(s, tok, vec, cot, wout, x2, act, actT)
    load = pltpu.make_async_copy(cot_h, cot, sems.at[7])
    load.start()
    load.wait()
    loads[2].wait()
    loads[3].wait()

    def dump(src, dst):
        copy = pltpu.make_async_copy(src, dst, sems.at[8])
        copy.start()
        copy.wait()

    def tile_step(t, _):
        mlp_tile(s, t, 0, s.blocks, cot, ubias, act, wup, wdown, mo, da2, hid, du, ugrad)
        up_grad(s, actT, du, lambda h: narrow.at[h])
        dump(narrow, gup_h.at[t])
        down_grad(s, hid, cot, lambda h: wide.at[h, pl.ds(0, s.tile)])
        dump(wide.at[:, pl.ds(0, s.tile)], gdown_h.at[t])
        return 0

    lax.fori_loop(0, s.tiles, tile_step, 0)
    datt, dbr, stage = (wdown.at[j * rows : (j + 1) * rows] for j in range(3))
    a1T = wup.at[:, 0:rows]
    norm_two_back(s, cot, vec, x2, mo, da2, stage, dbr, vgrad)
    dump(stage, out_h)
    att_grad(s, dbr, wout, datt)
    out_grad(s, attT, dbr, lambda h: wide.at[h, pl.ds(0, width)])
    dump(wide.at[:, pl.ds(0, width)], gout_h)
    norm_one_flipped(s, tok, vec, a1T)
    for g in range(s.pairs // 2):
        for h in range(2):
            p = 2 * g + h
            attend_back(s, p, qkv, seg, segcol, lse, datt, vgrad.at[2:3, :], vgrad.at[3:4, :])
            qkv_grad(s, a1T, qkv, p, lambda j: thin.at[h, j])
        dump(thin, gqkv_h.at[g])
    norm_one_back(s, tok, vec, qkv, wqkv, x2, stage, vgrad)
    dump(stage, ingrad_h)


MESH = pl.DeviceIdType.MESH
LINK_RATE = 90e3
CORE_RATE = 400e3
LATENCY = 4.5


class Timeline:
    def __init__(self):
        self.now, self.free, self.jobs = 0.0, {}, []

    def begin(self, job):
        self.jobs.append(job)
        self.launch(job, job.first)

    def launch(self, job, made):
        link, cost = made
        start = max(self.now, self.free.get(link, 0.0))
        self.free[link] = start + cost
        job.ready = start + cost + LATENCY

    def advance(self, job):
        self.now = max(self.now, job.ready)
        made = job.steps[job.done]()
        job.done += 1
        if made is None:
            self.jobs.remove(job)
        else:
            self.launch(job, made)

    def due(self, job):
        link = job.links[job.done]
        return max(job.ready, self.free.get(link, 0.0) - QUEUE) if link in ("x", "y", "z") else job.ready

    def next(self):
        return min(self.jobs, key=self.due)

    def tick(self, cost):
        end = self.now + cost
        while self.jobs:
            job = self.next()
            if self.due(job) > end:
                break
            self.now = max(self.now, min(self.due(job), end))
            self.advance(job)
        self.now = max(self.now, end)

    def need(self, job, steps=None):
        while job in self.jobs and (steps is None or job.done < steps):
            self.advance(self.next())

    def drain(self):
        while self.jobs:
            self.advance(self.next())


class Job:
    def __init__(self, first, steps, links):
        self.first, self.steps, self.links, self.done, self.ready = first, steps, links, 0, 0.0


def cut(ref, start, count):
    rows = pl.ds(pl.multiple_of(start, 16), count)
    return ref.at[rows, :] if len(ref.shape) == 2 else ref.at[:, rows, :]


def size_of(ref):
    total = 2
    for n in ref.shape:
        total *= n
    return total


class Place:
    def __init__(self, far):
        d, self.f = lax.axis_index("dp"), lax.axis_index("fsdp")
        self.d, self.far = d, far
        self.c, self.b, self.a = d % 2, (d // 2) % 2, d // 4
        self.core = {"dp": d + 1 - 2 * self.c, "fsdp": self.f}
        self.near = {"dp": d + 2 - 4 * self.b, "fsdp": self.f}
        self.across = {"dp": d, "fsdp": 1 - self.f}

    def other(self, k):
        return {"dp": lax.rem(self.a + k, self.far) * 4 + self.b * 2 + self.c, "fsdp": self.f}

    def spot(self, k):
        place = lax.rem(self.b * self.far + self.a + k, 2 * self.far)
        return {"dp": place % self.far * 4 + place // self.far * 2 + self.c, "fsdp": self.f}, place

    def bit(self, level):
        return (self.a // 2**level) % 2

    def flipped(self, level):
        step = (1 - 2 * self.bit(level)) * 2**level
        return {"dp": self.d + 4 * step, "fsdp": self.f}


def remote(src, dst, send, recv, device):
    return pltpu.make_async_remote_copy(
        src_ref=src, dst_ref=dst, send_sem=send, recv_sem=recv, device_id=device, device_id_type=MESH
    )


def gather_job(s, me, j, view, sems):
    send, recv = sems
    size = s.width // 2 // 4
    quarter = (me.c * 2 + me.b) * size
    first = remote(view(j, me.f, quarter, size), view(j, me.f, quarter, size), send.at[j, 0], recv.at[j, 0], me.across)
    g = 1 - me.f
    second = remote(view(j, g, quarter, size), view(j, g, quarter, size), send.at[j, 1], recv.at[j, 1], me.near)
    half = me.c * 2 * size
    third = remote(view(j, g, half, 2 * size), view(j, g, half, 2 * size), send.at[j, 2], recv.at[j, 2], me.core)
    cost = 2 * 2 * size * s.width / LINK_RATE

    def step_one():
        first.wait_recv()
        second.start()
        return ("y", cost)

    def step_two():
        second.wait_recv()
        third.start()
        return ("core", 2 * 2 * size * s.width / CORE_RATE)

    def step_three():
        third.wait_recv()
        return None

    first.start()
    return Job(("x", cost), [step_one, step_two, step_three], ["y", "core", ""]), [first, second, third]


class Unit:
    def __init__(self, index, own, other, into, out, direct=False):
        self.index, self.own, self.other, self.into, self.out, self.direct = index, own, other, into, out, direct
        self.rows = own.shape[-2]


def unit_job(s, me, unit, send, recv, give, take):
    u, own, far = unit.index, unit.own, me.far
    half, quarter = unit.rows // 2, unit.rows // 4
    piece = quarter // far
    r1, r2, r3 = unit.into
    r4 = cut(r3, quarter, r3.shape[-2] - quarter)
    r3 = cut(r3, 0, quarter)
    size = size_of(own)
    levels = far.bit_length() - 1
    mine, mine_b = me.f * half, me.f * half + me.b * quarter
    one = remote(unit.other, r1, send.at[u, 0], recv.at[u, 0], me.core)
    two = remote(cut(own, (1 - me.f) * half, half), r2, send.at[u, 1], recv.at[u, 1], me.across)
    three = remote(cut(own, mine + (1 - me.b) * quarter, quarter), r3, send.at[u, 2], recv.at[u, 2], me.near)
    four, kept, offset, used = [], [], 0, 0
    for level in range(levels):
        part, bit = quarter >> (level + 1), me.bit(level)
        arrived = cut(r4, used, part)
        theirs = cut(own, mine_b + offset + (1 - bit) * part, part)
        four.append(remote(theirs, arrived, send.at[u, 3 + level], recv.at[u, 3 + level], me.flipped(level)))
        offset = offset + bit * part
        kept.append((cut(own, mine_b + offset, part), arrived))
        used += part
    final = cut(own, mine_b + offset, piece)
    target = unit.out(me.b * quarter + offset, piece)
    base = 2 + levels
    five = [remote(final, target, send.at[u, base + k], recv.at[u, base + k], me.other(k)) for k in range(1, far)]
    n = base + far
    keep = pltpu.make_async_copy(final, target, send.at[u, n + 2])
    block = unit.out(me.b * quarter, quarter)
    six = remote(block, block, send.at[u, n], recv.at[u, n], me.near)
    all_rows = unit.out(0, half)
    seven = remote(all_rows, all_rows, send.at[u, n + 1], recv.at[u, n + 1], me.core)

    def add_into(part, arrived):
        part[...] = part[...] + arrived[...]

    def step_one():
        one.wait_recv()
        add_into(own, r1)
        if give is not None:
            pl.semaphore_signal(give, inc=1, device_id=me.core, device_id_type=MESH)
        two.start()
        return ("x", size / LINK_RATE)

    def step_two():
        two.wait_recv()
        add_into(cut(own, mine, half), r2)
        three.start()
        return ("y", size / 2 / LINK_RATE)

    def step_three():
        three.wait_recv()
        add_into(cut(own, mine_b, quarter), r3)
        four[0].start()
        return ("z", size / 4 / LINK_RATE)

    def fold(level):
        def step():
            four[level].wait_recv()
            add_into(*kept[level])
            if level + 1 < levels:
                four[level + 1].start()
                return ("z", size / 4 / LINK_RATE)
            keep.start()
            for copy in five:
                copy.start()
            return ("z", size / 2 / LINK_RATE)

        return step

    def step_five():
        keep.wait()
        for copy in five:
            copy.wait_recv()
        six.start()
        return ("y", size / 2 / LINK_RATE)

    def step_six():
        six.wait_recv()
        seven.start()
        return ("core", size / 2 / CORE_RATE)

    def step_seven():
        seven.wait_recv()
        return None

    def step_seven_of(copy):
        def step():
            copy().wait_recv()
            return None

        return step

    def direct_two():
        two.wait_recv()
        add_into(cut(own, mine, half), r2)
        for copy in parts:
            copy.start()
        return ("z", size / LINK_RATE)

    def direct_three():
        value = final[...].astype(F32)
        for k, copy in enumerate(parts):
            copy.wait_recv()
            value = value + cut(unit.into[2], k * piece, piece)[...].astype(F32)
        final[...] = value.astype(BF)
        keep.start()
        for copy in five:
            copy.start()
        return ("z", size / LINK_RATE)

    def direct_four():
        keep.wait()
        for copy in five:
            copy.wait_recv()
        seven.start()
        return ("core", size / 2 / CORE_RATE)

    if take is not None:
        pl.semaphore_wait(take, 1)
    one.start()
    if unit.direct:
        here = me.b * far + me.a
        final = cut(own, mine + here * piece, piece)
        target = unit.out(here * piece, piece)
        parts, five = [], []
        for k in range(1, 2 * far):
            device, place = me.spot(k)
            slot = cut(unit.into[2], (k - 1) * piece, piece)
            parts.append(remote(cut(own, mine + place * piece, piece), slot, send.at[u, 1 + k], recv.at[u, 1 + k], device))
            five.append(remote(final, target, send.at[u, 2 * far + k], recv.at[u, 2 * far + k], device))
        n = 4 * far - 1
        keep = pltpu.make_async_copy(final, target, send.at[u, n + 2])
        seven = remote(all_rows, all_rows, send.at[u, n + 1], recv.at[u, n + 1], me.core)
        steps = [step_one, direct_two, direct_three, direct_four, step_seven_of(lambda: seven)]
        return Job(("core", size / CORE_RATE), steps, ["x", "z", "z", "core", ""]), one, [two, *parts, *five, seven]
    folds = [fold(level) for level in range(levels)]
    steps = [step_one, step_two, step_three, *folds, step_five, step_six, step_seven]
    links = ["x", "y"] + ["z"] * (levels + 1) + ["y", "core", ""]
    return Job(("core", size / CORE_RATE), steps, links), one, [two, three, *four, *five, six, seven]


def vector_job(me, slots, sends, recvs, finish):
    core_s, x_s, near_s, far_s = slots
    stops = ((core_s, me.c, me.core), (x_s, me.f, me.across), (near_s, me.b, me.near))
    hops = [remote(s.at[i], s.at[i], sends.at[n], recvs.at[n], device) for n, (s, i, device) in enumerate(stops)]
    last = [
        remote(far_s.at[me.a], far_s.at[me.a], sends.at[2 + k], recvs.at[2 + k], me.other(k)) for k in range(1, me.far)
    ]
    cost = ("small", 0.4)

    def hop(n):
        def step():
            hops[n].wait()
            total = stops[n][0][0] + stops[n][0][1]
            if n < 2:
                stops[n + 1][0][stops[n + 1][1]] = total
                hops[n + 1].start()
            else:
                far_s[me.a] = total
                for copy in last:
                    copy.start()
            return cost

        return step

    def end():
        for copy in last:
            copy.wait()
        total = far_s[0]
        for k in range(1, me.far):
            total = total + far_s[k]
        far_s[0] = total
        finish()
        return None

    hops[0].start()
    return Job(cost, [hop(0), hop(1), hop(2), end], ["small"] * 3 + [""])


def linked_kernel(
    s, far, tok_h, cot_h, seg, g1_h, s1_h, qb_h, vb_h, ob_h, g2_h, s2_h, db_h, ub_h, wqkv_h, wout_h, wup_h, wdown_h,
    out_h, ingrad_h, gqkv_h, gout_h, gup_h, gdown_h, vout,
    tok, cot, act, actT, attT, qkv, x2, mo, da2, hid, du,
    wqkv, wout, wup, wdown, segcol, lse, raw, raw_up, packed, vec, ubias, ugrad, core_s, x_s, near_s, far_s,
    own_up, own_down, oth_up, oth_down,
    r1_up, r1_down, r1_out, r1_qkv, r2_up, r2_down, r2_out, r2_qkv,
    r3_up, r3_down, r3_out, r3_qkv,
    loads, wsend, wrecv, usend, urecv, vsend, vrecv, credit,
):
    rows, width = s.rows, s.width
    me = Place(far)
    line = Timeline()
    shard, third = width // 2, width // 3
    count = s.hidden // width

    barrier = pltpu.get_barrier_semaphore()
    partners = [me.core, me.across] + [me.spot(k)[0] for k in range(1, 2 * far)]
    for device in partners:
        pl.semaphore_signal(barrier, inc=1, device_id=device, device_id_type=MESH)

    names = [("qkv", 0), ("qkv", 1), ("qkv", 2), ("out", 0)]
    order = [i for k in range(count // 2) for i in (k, k + count // 2)]
    for n in range(0, count, 2):
        names += [("up", order[n]), ("up", order[n + 1]), ("down", n), ("down", n + 1)]

    def view(j, f, start, size):
        kind, i = names[j]
        if kind == "down":
            return wdown.at[pl.ds(pl.multiple_of(f * s.share + i * shard + start, 16), size), :]
        part = pl.ds(pl.multiple_of(f * shard + start, 16), size)
        if kind == "out":
            return wout.at[part, :]
        if kind == "qkv":
            return wqkv.at[:, part, i * third : (i + 1) * third]
        return wup.at[part, i * width : (i + 1) * width]

    def masters(j):
        kind, i = names[j]
        if kind == "down":
            return [(wdown_h.at[i * shard : (i + 1) * shard, :], stages[j % 4])]
        if kind == "out":
            return [(wout_h.at[...], stages[j % 4])]
        if kind == "up":
            return [(wup_h.at[:, i * width : (i + 1) * width], stages[j % 4])]
        starts = [n * width + i * third for n in range(3)]
        return [
            (wqkv_h.at[:, start : start + third], stages[j % 4].at[:, n * third : (n + 1) * third])
            for n, start in enumerate(starts)
        ]

    stages = [mo.at[0:shard], mo.at[shard : 2 * shard], da2.at[0:shard], da2.at[shard : 2 * shard]]
    copies = [
        [pltpu.make_async_copy(a, b, loads.at[j % 4, n]) for n, (a, b) in enumerate(masters(j))]
        for j in range(len(names))
    ]
    for j in range(4):
        for copy in copies[j]:
            copy.start()
    load_tok = pltpu.make_async_copy(tok_h, tok, loads.at[4, 0])
    load_tok.start()
    per = shard // 128
    small = [(a, raw.at[n]) for n, a in enumerate((g1_h, s1_h, qb_h, vb_h, ob_h, g2_h, s2_h, db_h))] + [(ub_h, raw_up)]
    small = [pltpu.make_async_copy(a, b, loads.at[6 + n // 3, n % 3]) for n, (a, b) in enumerate(small)]
    for copy in small:
        copy.start()
    share_small = remote(packed.at[me.f], packed.at[me.f], vsend.at[2 + far], vrecv.at[2 + far], me.across)
    pl.semaphore_wait(barrier, len(partners))
    sent, moved, jobs = [share_small], [], []
    for j in range(len(names)):
        for copy in copies[j]:
            copy.wait()
        if names[j][0] == "qkv":
            for n in range(3):
                view(j, me.f, 0, shard)[n] = stages[j % 4][:, n * third : (n + 1) * third].astype(BF)
        else:
            view(j, me.f, 0, shard)[...] = stages[j % 4][...].astype(BF)
        if j + 4 < len(names):
            for copy in copies[j + 4]:
                copy.start()
        if j == 2:
            for copy in small:
                copy.wait()
            packed[me.f] = jnp.zeros((packed.shape[1], 128), F32)
            for n in range(8):
                packed[me.f, n * per : n * per + per, :] = raw[n].astype(BF).astype(F32)
            packed[me.f, 8 * per : 8 * per + s.share // 128, :] = raw_up[...].astype(BF).astype(F32)
            share_small.start()
        job, made = gather_job(s, me, j, view, (wsend, wrecv))
        line.begin(job)
        line.now += 0.5
        jobs.append(job)
        (moved if names[j][0] in ("up", "down") else sent).extend(made)
    setup_masks(s, seg, segcol)
    core_s[...] = jnp.zeros_like(core_s)
    share_small.wait_recv()
    for f in range(2):
        for i in range(8 * per):
            r, col = i // per, f * shard + i % per * 128
            vec[r : r + 1, col : col + 128] = packed[f, i : i + 1, :]
        for i in range(s.share // 128):
            ubias[f, :, i * 128 : (i + 1) * 128] = packed[f, 8 * per + i : 8 * per + i + 1, :]
    load_tok.wait()
    norm_one(s, tok, vec, act)
    line.tick(3.0)
    for group in range(3):
        line.need(jobs[group])
        project_qkv(s, act, wqkv, vec, qkv, group)
        line.tick(1.6)
        attend(s, group, qkv, seg, segcol, lse, cot, attT)
        line.tick(3.8)
    line.need(jobs[3])
    project_out(s, tok, vec, cot, wout, x2, act, actT)
    load_cot = pltpu.make_async_copy(cot_h, cot, loads.at[5, 0])
    load_cot.start()
    line.tick(2.5)

    c = me.c
    units, firsts, later = [], [], []
    pending = {}

    def start_unit(unit, kind=None, slot=0, reuse=False, again=False):
        give = credit.at[kind * 2 + slot] if again else None
        take = credit.at[kind * 2 + slot] if reuse else None
        job, one, made = unit_job(s, me, unit, usend, urecv, give, take)
        line.begin(job)
        later.extend(made)
        return job, one

    vgrad = core_s.at[c]
    load_cot.wait()
    for t in range(s.tiles):
        for j, (kind, i) in enumerate(names):
            if kind == "up":
                lo, hi = i * width, (i + 1) * width
                used = any(f * s.share + t * s.piece < hi and f * s.share + (t + 1) * s.piece > lo for f in range(2))
            elif kind == "down":
                used = t * s.piece < (i + 1) * shard and (t + 1) * s.piece > i * shard
            else:
                used = False
            if used:
                line.need(jobs[j])
        slot = t % 2
        mlp_tile(s, t, 0, s.blocks, cot, ubias, act, wup, wdown, mo, da2, hid, du, ugrad)
        line.tick(4.2)
        if t >= 2:
            job, one = pending["up", t - 2]
            line.need(job, 1)
            one.wait_send()
        up_grad_linked(s, actT, du, c, own_up.at[t], oth_up.at[slot])
        unit = Unit(
            2 * t, own_up.at[t], oth_up.at[slot],
            (r1_up.at[slot], r2_up.at[t], r3_up.at[t]),
            lambda start, n, t=t: gup_h.at[pl.ds(pl.multiple_of(start, 16), n), span(c * s.share + t * s.piece, s.piece)],
        )
        pending["up", t] = start_unit(unit, 0, slot, t >= 2, t + 2 < s.tiles)
        line.tick(1.5)
        if t >= 2:
            job, one = pending["down", t - 2]
            line.need(job, 1)
            one.wait_send()
        down_grad_linked(s, hid, cot, c, own_down.at[t], oth_down.at[slot])
        unit = Unit(
            2 * t + 1, own_down.at[t], oth_down.at[slot],
            (r1_down.at[slot], r2_down.at[t], r3_down.at[t]),
            lambda start, n, t=t: gdown_h.at[
                pl.ds(pl.multiple_of(t * s.piece + start, 16), n), span(c * shard, shard)
            ],
        )
        pending["down", t] = start_unit(unit, 1, slot, t >= 2, t + 2 < s.tiles)
        line.tick(1.3)
    for job in jobs:
        line.need(job)
    for copy in moved:
        copy.wait_send()
    datt, dbr, stage = (wdown.at[j * rows : (j + 1) * rows] for j in range(3))
    a1T = wup.at[:, 0:rows]
    own_out, oth_out = (wup.at[:, rows + j * shard : rows + (j + 1) * shard] for j in range(2))
    spare = [wup.at[:, n : n + 128] for n in range(rows + width, s.hidden, 128)]
    spare += [actT.at[:, n : n + 128] for n in range(0, rows, 128)]
    own_qkv, oth_qkv = spare[: 3 * s.pairs // 2], spare[3 * s.pairs // 2 :]
    norm_two_back(s, cot, vec, x2, mo, da2, stage, dbr, vgrad)
    save_out = pltpu.make_async_copy(stage, out_h, loads.at[5, 0])
    save_out.start()
    line.tick(2.5)
    out_grad_linked(s, attT, dbr, c, own_out, oth_out)
    unit = Unit(
        2 * s.tiles, own_out, oth_out,
        (r1_out, r2_out, r3_out),
        lambda start, n: gout_h.at[pl.ds(pl.multiple_of(start, 16), n), span(c * shard, shard)],
    )
    pending["out"] = start_unit(unit)
    line.tick(1.3)
    att_grad(s, dbr, wout, datt)
    line.tick(2.2)
    norm_one_flipped(s, tok, vec, a1T)
    line.tick(1.7)
    for g in range(s.pairs // 2):
        for h in range(2):
            attend_back(s, 2 * g + h, qkv, seg, segcol, lse, datt, vgrad.at[2:3, :], vgrad.at[3:4, :])
            line.tick(3.8)
        for j in range(3):
            n = 3 * g + j
            own, other = own_qkv[n], oth_qkv[n]
            qkv_grad_linked(s, a1T, qkv, g, j, c, own, other)
            unit = Unit(
                2 * s.tiles + 1 + n, own, other, (r1_qkv.at[n], r2_qkv.at[n], r3_qkv.at[n]),
                lambda start, size, g=g, j=j: gqkv_h.at[
                    pl.ds(pl.multiple_of(start, 16), size), span(j * width + (2 * g + c) * 128, 128)
                ],
                g >= s.pairs // 2 - DIRECT,
            )
            pending["qkv", n] = start_unit(unit)
            line.tick(0.6)
    save_out.wait()
    norm_one_back(s, tok, vec, qkv, wqkv, x2, stage, vgrad)
    line.tick(5.0)
    save_in = pltpu.make_async_copy(stage, ingrad_h, loads.at[4, 0])
    save_in.start()
    part = math.gcd(s.share, width)
    for i in range(s.hidden // part):
        start = i * part
        f, off = start // s.share, start % s.share
        r, col = 8 + start // width, start % width
        vgrad[r : r + 1, col : col + part] = ugrad[f, :, off : off + part]

    def finish():
        vout[...] = jnp.zeros_like(vout)
        for f in range(2):

            @pl.when(me.f == f)
            def _(f=f):
                for i in range(8 * per):
                    r, col = i // per, f * shard + i % per * 128
                    vout[i : i + 1, :] = far_s[0, r : r + 1, col : col + 128]
                for i in range(s.share // 128):
                    flat = f * s.share + i * 128
                    r, col = 8 + flat // width, flat % width
                    vout[8 * per + i : 8 * per + i + 1, :] = far_s[0, r : r + 1, col : col + 128]

    line.begin(vector_job(me, (core_s, x_s, near_s, far_s), vsend, vrecv, finish))
    line.drain()
    save_in.wait()
    for key, (job, one) in pending.items():
        if key == "out" or key[0] == "qkv" or key[1] + 2 >= s.tiles:
            one.wait_send()
    for copy in later + sent:
        copy.wait_send()


def split_store(c, value, own, other, rows):
    half = value.shape[-1] // 2
    left, right = value[:, :half].astype(BF), value[:, half:].astype(BF)
    own[rows, :] = jnp.where(c == 0, left, right)
    other[rows, :] = jnp.where(c == 0, right, left)


def up_grad_linked(s, a2T, du, c, own, other):
    def step(r, _):
        rows = at(r, WIDE)
        split_store(c, dot_nn(a2T[rows, :], du[...]), own, other, rows)
        return 0

    lax.fori_loop(0, s.width // WIDE, step, 0)


def down_grad_linked(s, hid, cot, c, own, other):
    def step(r, _):
        rows = at(r, ROWS)
        split_store(c, dot_tn(hid[:, rows], cot[...]), own, other, rows)
        return 0

    lax.fori_loop(0, s.tile // ROWS, step, 0)


def out_grad_linked(s, attT, dbr, c, own, other):
    def step(r, _):
        rows = at(r, WIDE)
        split_store(c, dot_nn(attT[rows, :], dbr[...]), own, other, rows)
        return 0

    lax.fori_loop(0, s.width // WIDE, step, 0)


def qkv_grad_linked(s, a1T, dqkv, g, j, c, own, other):
    start = j * s.width + 2 * g * 128
    split_store(c, dot_nn(a1T[...], dqkv[:, start : start + 256]), own, other, slice(None))


def linked_body(far, tokens, segment_ids, cotangent, *params):
    (
        norm1_gain, norm1_shift, qkv_weight, query_bias, value_bias, out_weight, out_bias, norm2_gain, norm2_shift,
        up_weight, up_bias, down_weight, down_bias,
    ) = params
    rows, width = tokens.shape
    hidden = up_weight.shape[1]
    s = Sizes(rows, width, hidden, 2)
    shard, tiles, tile, groups = width // 2, s.tiles, s.tile, 3 * s.pairs // 2
    vectors = [norm1_gain, norm1_shift, query_bias, value_bias, out_bias, norm2_gain, norm2_shift, down_bias]
    vectors = [v.reshape(-1, 128) for v in vectors + [up_bias]]
    lines_all = -(-sum(v.shape[0] for v in vectors) // 8) * 8
    seg = segment_ids.reshape(s.seqs, 1, SEQ)
    whole = pl.BlockSpec(memory_space=pltpu.VMEM)
    away = pl.BlockSpec(memory_space=pl.ANY)

    def vm(*shape, kind=BF):
        return pltpu.VMEM(shape, kind)

    n_units, n_blocks = 2 * tiles + 1 + groups, 4 + 2 * (hidden // width)
    up, down, out, qk = (width, tile // 2), (tile, shard), (width, shard), (width, 128)

    def part(shape, by):
        return shape[:-2] + (shape[-2] // by, shape[-1])

    def rest(shape):
        return shape[:-2] + (shape[-2] // (4 * far) * (2 * far - 1), shape[-1])

    slots = min(2, tiles)
    scratch = [
        vm(rows, width), vm(rows, width), vm(rows, width), vm(width, rows), vm(width, rows), vm(rows, 3 * width),
        vm(rows, width, kind=F32), vm(rows, width, kind=F32), vm(rows, width, kind=F32), vm(rows, tile), vm(rows, tile),
        vm(3, width, width), vm(width, width), vm(width, hidden), vm(hidden, width),
        vm(s.seqs, SEQ, 128, kind=F32), vm(s.seqs * HEADS, 1, SEQ, kind=F32),
        vm(8, shard // 128, 128, kind=F32), vm(s.share // 128, 128, kind=F32),
        vm(2, lines_all, 128, kind=F32), vm(8, width, kind=F32), vm(2, 1, s.share, kind=F32), vm(2, 1, s.share, kind=F32),
        vm(2, 16, width, kind=F32), vm(2, 16, width, kind=F32), vm(2, 16, width, kind=F32), vm(far, 16, width, kind=F32),
        vm(tiles, *up), vm(tiles, *down), vm(slots, *up), vm(slots, *down),
        vm(slots, *up), vm(slots, *down), vm(*out), vm(groups, *qk),
        vm(tiles, *part(up, 2)), vm(tiles, *part(down, 2)), vm(*part(out, 2)), vm(groups, *part(qk, 2)),
        vm(tiles, *rest(up)), vm(tiles, *rest(down)), vm(*rest(out)), vm(groups, *rest(qk)),
        pltpu.SemaphoreType.DMA((9, 3)),
        pltpu.SemaphoreType.DMA((n_blocks, 3)),
        pltpu.SemaphoreType.DMA((n_blocks, 3)),
        pltpu.SemaphoreType.DMA((n_units, 4 * far + 2)),
        pltpu.SemaphoreType.DMA((n_units, 4 * far + 2)),
        pltpu.SemaphoreType.DMA((far + 3,)),
        pltpu.SemaphoreType.DMA((far + 3,)),
        pltpu.SemaphoreType.REGULAR((4,)),
    ]
    output, input_grad, gqkv, gout, gup, gdown, v = pl.pallas_call(
        functools.partial(linked_kernel, s, far),
        out_shape=(
            jax.ShapeDtypeStruct((rows, width), BF),
            jax.ShapeDtypeStruct((rows, width), BF),
            jax.ShapeDtypeStruct((shard, 3 * width), BF),
            jax.ShapeDtypeStruct((shard, width), BF),
            jax.ShapeDtypeStruct((shard, hidden), BF),
            jax.ShapeDtypeStruct((hidden // 2, width), BF),
            jax.ShapeDtypeStruct((lines_all, 128), F32),
        ),
        in_specs=[away, away, whole] + [away] * 13,
        out_specs=(away,) * 6 + (whole,),
        scratch_shapes=scratch,
        compiler_params=pltpu.CompilerParams(
            vmem_limit_bytes=61 << 20, collective_id=0, has_side_effects=True
        ),
    )(tokens, cotangent, seg, *vectors, qkv_weight, out_weight, up_weight, down_weight)
    grads = (gqkv, gout, gup, gdown)
    lines = [shard // 128] * 8 + [s.share // 128]
    final = pl.pallas_call(
        functools.partial(finish_kernel, lines),
        out_shape=(
            [jax.ShapeDtypeStruct((rows, width), BF)] * 2
            + [jax.ShapeDtypeStruct(g.shape, F32) for g in grads]
            + [jax.ShapeDtypeStruct((n, 128), F32) for n in lines]
        ),
        in_specs=[away] * 6 + [whole],
        out_specs=[away] * 6 + [whole] * len(lines),
        scratch_shapes=(
            [pltpu.VMEM(g.shape, BF) for g in grads]
            + [pltpu.VMEM(g.shape, F32) for g in grads]
            + [pltpu.VMEM((2, rows, width), BF)]
            + [pltpu.SemaphoreType.DMA((2,)), pltpu.SemaphoreType.DMA((4, CHUNKS)), pltpu.SemaphoreType.DMA((4, CHUNKS))]
        ),
        compiler_params=pltpu.CompilerParams(vmem_limit_bytes=61 << 20),
    )(output, input_grad, *grads, v)
    output, input_grad, gqkv, gout, gup, gdown = final[:6]
    v = [value.reshape(-1) for value in final[6:]]
    return (
        output, input_grad, v[0], v[1], gqkv, v[2], v[3], gout, v[4], v[5], v[6], gup, v[8], gdown, v[7],
    )


CHUNKS = 4


def finish_kernel(lines, *refs):
    ins, v, outs, small = refs[:6], refs[6], refs[7:13], refs[13 : 13 + len(lines)]
    held, wide = refs[13 + len(lines) : 17 + len(lines)], refs[17 + len(lines) : 21 + len(lines)]
    passing, whole, loads, stores = refs[21 + len(lines) :]
    lift = [pltpu.make_async_copy(ins[n], passing.at[n], whole.at[n]) for n in range(2)]
    drop = [pltpu.make_async_copy(passing.at[n], outs[n], whole.at[n]) for n in range(2)]
    chunks = []
    for n in range(4):
        rows = held[n].shape[0] // CHUNKS
        for i in range(CHUNKS):
            part = pl.ds(i * rows, rows)
            chunks.append((n, i, part))
    into = [pltpu.make_async_copy(ins[2 + n].at[part], held[n].at[part], loads.at[n, i]) for n, i, part in chunks]
    back = [pltpu.make_async_copy(wide[n].at[part], outs[2 + n].at[part], stores.at[n, i]) for n, i, part in chunks]
    for copy in lift + into:
        copy.start()
    start = 0
    for ref, count in zip(small, lines):
        ref[...] = v[start : start + count, :]
        start += count
    for n in range(2):
        lift[n].wait()
        drop[n].start()
    for (n, _i, part), load, store in zip(chunks, into, back):
        load.wait()
        wide[n][part, :] = held[n][part, :].astype(F32)
        store.start()
    for copy in back + drop:
        copy.wait()


def body(
    tokens, segment_ids, cotangent, norm1_gain, norm1_shift, qkv_weight, query_bias, value_bias,
    out_weight, out_bias, norm2_gain, norm2_shift, up_weight, up_bias, down_weight, down_bias,
):
    shards = lax.axis_size("fsdp")
    rows, width = tokens.shape
    hidden = up_weight.shape[1]
    s = Sizes(rows, width, hidden, shards)
    small = [norm1_gain, norm1_shift, query_bias, value_bias, out_bias, norm2_gain, norm2_shift, down_bias]
    vec = lax.all_gather(jnp.stack(small).astype(BF), "fsdp", axis=1, tiled=True).astype(F32)
    ubias = lax.all_gather(up_bias.astype(BF), "fsdp", axis=0).astype(F32)[:, None, :]
    weights = [
        lax.all_gather(w.astype(BF), "fsdp", axis=0, tiled=True)
        for w in (qkv_weight, out_weight, up_weight, down_weight)
    ]
    seg = segment_ids.reshape(s.seqs, 1, SEQ)
    whole = pl.BlockSpec(memory_space=pltpu.VMEM)
    away = pl.BlockSpec(memory_space=pl.ANY)
    groups = s.pairs // 2
    results = pl.pallas_call(
        functools.partial(block_kernel, s),
        out_shape=(
            jax.ShapeDtypeStruct((rows, width), BF),
            jax.ShapeDtypeStruct((rows, width), BF),
            jax.ShapeDtypeStruct((groups, 2, 3, width, 128), BF),
            jax.ShapeDtypeStruct((2, width, width // 2), BF),
            jax.ShapeDtypeStruct((s.tiles, 2, width, s.tile // 2), BF),
            jax.ShapeDtypeStruct((s.tiles, 2, s.tile, width // 2), BF),
            jax.ShapeDtypeStruct((8, width), F32),
            jax.ShapeDtypeStruct((shards, 1, s.share), F32),
        ),
        in_specs=[away, away, whole, whole, whole, away, away, away, away],
        out_specs=(away,) * 6 + (whole, whole),
        scratch_shapes=[
            pltpu.VMEM((rows, width), BF),
            pltpu.VMEM((rows, width), BF),
            pltpu.VMEM((rows, width), BF),
            pltpu.VMEM((width, rows), BF),
            pltpu.VMEM((width, rows), BF),
            pltpu.VMEM((rows, 3 * width), BF),
            pltpu.VMEM((rows, width), F32),
            pltpu.VMEM((rows, width), F32),
            pltpu.VMEM((rows, width), F32),
            pltpu.VMEM((rows, s.tile), BF),
            pltpu.VMEM((rows, s.tile), BF),
            pltpu.VMEM((3, width, width), BF),
            pltpu.VMEM((width, width), BF),
            pltpu.VMEM((width, hidden), BF),
            pltpu.VMEM((hidden, width), BF),
            pltpu.VMEM((s.seqs, SEQ, 128), F32),
            pltpu.VMEM((s.seqs * HEADS, 1, SEQ), F32),
            pltpu.VMEM((2, width, s.tile // 2), BF),
            pltpu.VMEM((2, max(width, s.tile), width // 2), BF),
            pltpu.VMEM((2, 3, width, 128), BF),
            pltpu.SemaphoreType.DMA((9,)),
        ],
        compiler_params=pltpu.CompilerParams(vmem_limit_bytes=61 << 20),
    )(tokens, cotangent, seg, vec, ubias, *weights)
    output, input_grad, gqkv, gout, gup, gdown, vgrad, ugrad = results
    gqkv = gqkv.transpose(3, 2, 0, 1, 4).reshape(width, 3 * width)
    gout = gout.transpose(1, 0, 2).reshape(width, width)
    half = s.tile // 2
    gup = gup.transpose(2, 0, 1, 3).reshape(width, s.tiles, shards, s.piece)
    gup = gup.transpose(0, 2, 1, 3).reshape(width, hidden)
    gdown = gdown.transpose(0, 2, 1, 3).reshape(s.tiles, shards, s.piece, width)
    gdown = gdown.transpose(1, 0, 2, 3).reshape(hidden, width)

    def summed(value):
        part = lax.psum_scatter(value.astype(BF), "fsdp", scatter_dimension=0, tiled=True)
        return lax.psum(part, "dp").astype(F32)

    gqkv, gout, gup, gdown = [summed(v) for v in (gqkv, gout, gup, gdown)]
    ugrad = summed(ugrad.reshape(hidden))
    v = [summed(vgrad[i]) for i in range(8)]
    return (
        output, input_grad, v[0], v[1], gqkv, v[2], v[3], gout, v[4], v[5], v[6], gup, ugrad, gdown, v[7],
    )


def solution(mesh):
    rows, wide, long = P(("dp", "fsdp"), None), P("fsdp", None), P("fsdp")
    shards, copies = mesh.shape["fsdp"], mesh.shape["dp"]
    linked = shards == 2 and copies in (8, 16)
    return jax.shard_map(
        functools.partial(linked_body, copies // 4) if linked else body,
        mesh=mesh,
        in_specs=(
            rows, P(("dp", "fsdp")), rows, long, long, wide, long, long, wide, long, long, long, wide, long, wide, long,
        ),
        out_specs=(
            rows, rows, long, long, wide, long, long, wide, long, long, long, wide, long, wide, long,
        ),
        check_vma=False,
    )
```

```python
import functools
import math

import jax
import jax.numpy as jnp
from jax import lax
from jax.experimental import pallas as pl
from jax.experimental.pallas import tpu as pltpu
from jax.sharding import PartitionSpec as P

HEADS = 12
SEQ = 512
EPSILON = 1e-06
LARGE_NEG = -1000000000.0
BF = jnp.bfloat16
F32 = jnp.float32
ROWS = 512
WIDE = 384
DIRECT = 0
QUEUE = 1.0


def dot_of(left, right, over):
    return lax.dot_general(left, right, (over, ((), ())), preferred_element_type=F32)


def dot_nn(left, right):
    return dot_of(left, right, ((1,), (0,)))


def dot_nt(left, right):
    return dot_of(left, right, ((1,), (1,)))


def dot_tn(left, right):
    return dot_of(left, right, ((0,), (0,)))


def at(index, size):
    return pl.ds(pl.multiple_of(index * size, size), size)


def span(start, size):
    return pl.ds(pl.multiple_of(start, 128), size)


def mean_of(value):
    return jnp.sum(value, -1, keepdims=True) * (1.0 / value.shape[-1])


def normed(value):
    centre = value - mean_of(value)
    inverse = lax.rsqrt(mean_of(centre * centre) + EPSILON)
    return centre * inverse, inverse


def down_sum(value):
    return jnp.sum(value, 0, keepdims=True)


def gelu_pair(value):
    cumulative = 0.5 + 0.5 * lax.erf(value * 0.7071067811865476)
    density = jnp.exp(-0.5 * value * value) * 0.3989422804014327
    return value * cumulative, cumulative + value * density


def norm_back(grad, xhat, inverse, gain):
    scaled = grad * gain
    return inverse * (scaled - mean_of(scaled) - xhat * mean_of(scaled * xhat))


class Sizes:
    def __init__(self, rows, width, hidden, shards):
        self.rows, self.width, self.hidden, self.shards = rows, width, hidden, shards
        self.seqs = rows // SEQ
        self.pairs = HEADS // 2
        share = hidden // shards
        self.tiles = max(n for n in range(1, 7) if share % n == 0 and (share // n) % 128 == 0)
        self.share = share
        self.piece = share // self.tiles
        self.tile = self.piece * shards
        self.blocks = rows // ROWS


def setup_masks(s, seg, segcol):
    for i in range(s.seqs):
        segcol[i] = jnp.broadcast_to(seg[i].astype(F32), (128, SEQ)).T


def norm_one(s, tok, vec, a1):
    def step(i, _):
        rows = at(i, ROWS)
        xhat, _inv = normed(tok[rows, :].astype(F32))
        a1[rows, :] = (xhat * vec[0:1, :] + vec[1:2, :]).astype(BF)
        return 0

    lax.fori_loop(0, s.blocks, step, 0)


def norm_one_flipped(s, tok, vec, a1T):
    def step(i, _):
        rows = at(i, ROWS)
        xhat, _inv = normed(tok[rows, :].astype(F32))
        a1T[:, rows] = (xhat * vec[0:1, :] + vec[1:2, :]).T.astype(BF)
        return 0

    lax.fori_loop(0, s.blocks, step, 0)


def project_qkv(s, act, wqkv, vec, qkv, group):
    width = s.width
    n = width // 3
    cols = slice(group * n, group * n + n)
    for j in range(3):
        lin = dot_nn(act[...], wqkv[j, :, cols])
        if j != 1:
            row = 2 + j // 2
            lin = lin + vec[row : row + 1, cols]
        qkv[:, j * width + group * n : j * width + group * n + n] = lin.astype(BF)


def allowed_of(seg, segcol, i):
    col = segcol[i]
    full = jnp.concatenate([col] * (SEQ // 128), axis=1)
    return full == seg[i].astype(F32)


def lane_of(half):
    lanes = lax.broadcasted_iota(jnp.int32, (1, 128), 1)
    return (lanes < 64) if half == 0 else (lanes >= 64)


def pick_lanes(half, value):
    return jnp.where(lane_of(half), value, jnp.zeros_like(value))


def attend(s, group, qkv, seg, segcol, lse, att, attT):
    width, count = s.width, s.pairs // 3

    def step(i, _):
        rows = at(i, SEQ)
        ok = allowed_of(seg, segcol, i)
        items, raws, outs = [], {}, {}
        for p in range(group * count, group * count + count):
            q = qkv[rows, p * 128 : p * 128 + 128] * jnp.asarray(0.125, BF)
            k = qkv[rows, width + p * 128 : width + p * 128 + 128]
            vT = qkv[rows, 2 * width + p * 128 : 2 * width + p * 128 + 128].T
            items += [(p, q, k, vT, half) for half in (0, 1)]

        def raw(x):
            _p, q, k, _v, half = items[x]
            raws[x] = dot_nt(k, pick_lanes(half, q))

        def soft(x):
            p, _q, _k, _v, half = items[x]
            scores = jnp.where(ok, raws[x], LARGE_NEG)
            top = jnp.max(scores, 0, keepdims=True)
            expo = jnp.exp(scores - top)
            total = jnp.sum(expo, 0, keepdims=True)
            lse[2 * (i * s.pairs + p) + half] = top + jnp.log(total)
            outs[x] = expo.astype(BF), 1.0 / total

        def out(x):
            p, _q, _k, vT, half = items[x]
            expo, inverse = outs[x]
            outs[x] = dot_nn(vT[64 * half : 64 * half + 64], expo) * inverse
            if half == 1:
                both = jnp.concatenate([outs[x - 1], outs[x]], 0)
                attT[p * 128 : p * 128 + 128, rows] = both.astype(BF)
                att[rows, p * 128 : p * 128 + 128] = both.T.astype(BF)

        raw(0)
        for x in range(len(items)):
            if x + 1 < len(items):
                raw(x + 1)
            soft(x)
            if x >= 1:
                out(x - 1)
        out(len(items) - 1)
        return 0

    lax.fori_loop(0, s.seqs, step, 0)


def project_out(s, tok, vec, att, wout, x2, a2, a2T):
    def step(i, _):
        rows = at(i, ROWS)
        value = tok[rows, :].astype(F32) + (dot_nn(att[rows, :], wout[...]) + vec[4:5, :])
        x2[rows, :] = value
        xhat, _inv = normed(value)
        act = xhat * vec[5:6, :] + vec[6:7, :]
        a2[rows, :] = act.astype(BF)
        a2T[:, rows] = act.T.astype(BF)
        return 0

    lax.fori_loop(0, s.blocks, step, 0)


def mlp_tile(s, t, first, count, cot, ubias, a2, wup, wdown, mo, da2, hid, du, ugrad):
    starts = [f * s.share + t * s.piece for f in range(s.shards)]
    fresh = t == 0

    def step(i, sums):
        rows = at(first + i, ROWS)
        act, dy = a2[rows, :], cot[rows, :]
        more, back = 0.0, 0.0
        parts = []
        for f, start in enumerate(starts):
            up, down = wup[:, span(start, s.piece)], wdown[span(start, s.piece), :]
            u = dot_nn(act, up) + ubias[f, :, at(t, s.piece)]
            h, slope = gelu_pair(u)
            h = h.astype(BF)
            d = (dot_nt(dy, down) * slope).astype(BF)
            hid[rows, f * s.piece : (f + 1) * s.piece] = h
            du[rows, f * s.piece : (f + 1) * s.piece] = d
            more = more + dot_nn(h, down)
            back = back + dot_nt(d, up)
            parts.append(down_sum(d.astype(F32)))
        mo[rows, :] = jnp.where(fresh, 0.0, mo[rows, :]) + more
        da2[rows, :] = jnp.where(fresh, 0.0, da2[rows, :]) + back
        return tuple(a + b for a, b in zip(sums, parts))

    zero = jnp.zeros((1, s.piece), F32)
    sums = lax.fori_loop(0, count, step, (zero,) * s.shards)
    for f in range(s.shards):
        ugrad[f, :, at(t, s.piece)] = sums[f] + (ugrad[f, :, at(t, s.piece)] if first else 0.0)


def up_grad(s, a2T, du, unit):
    half = s.tile // 2

    def step(r, _):
        rows = at(r, WIDE)
        value = dot_nn(a2T[rows, :], du[...]).astype(BF)
        unit(0)[rows, :] = value[:, :half]
        unit(1)[rows, :] = value[:, half:]
        return 0

    lax.fori_loop(0, s.width // WIDE, step, 0)


def down_grad(s, hid, cot, unit):
    half = s.width // 2

    def step(r, _):
        rows = at(r, ROWS)
        value = dot_tn(hid[:, rows], cot[...]).astype(BF)
        unit(0)[rows, :] = value[:, :half]
        unit(1)[rows, :] = value[:, half:]
        return 0

    lax.fori_loop(0, s.tile // ROWS, step, 0)


def norm_two_back(s, cot, vec, x2, mo, da2, out, dbr, vgrad):
    def step(i, sums):
        rows = at(i, ROWS)
        value = x2[rows, :]
        dy = cot[rows, :].astype(F32)
        out[rows, :] = (value + (mo[rows, :] + vec[7:8, :])).astype(BF)
        xhat, inverse = normed(value)
        grad = da2[rows, :]
        total = dy + norm_back(grad, xhat, inverse, vec[5:6, :])
        x2[rows, :] = total
        low = total.astype(BF)
        dbr[rows, :] = low
        return tuple(
            a + down_sum(b) for a, b in zip(sums, (low.astype(F32), grad * xhat, grad, dy))
        )

    zero = jnp.zeros((1, s.width), F32)
    sums = lax.fori_loop(0, s.blocks, step, (zero,) * 4)
    for j, value in enumerate(sums):
        vgrad[4 + j : 5 + j, :] = value


def att_grad(s, dbr, wout, datt):
    def step(i, _):
        rows = at(i, ROWS)
        datt[rows, :] = dot_nt(dbr[rows, :], wout[...]).astype(BF)
        return 0

    lax.fori_loop(0, s.blocks, step, 0)


def out_grad(s, attT, dbr, unit):
    half = s.width // 2

    def step(r, _):
        rows = at(r, WIDE)
        value = dot_nn(attT[rows, :], dbr[...]).astype(BF)
        unit(0)[rows, :] = value[:, :half]
        unit(1)[rows, :] = value[:, half:]
        return 0

    lax.fori_loop(0, s.width // WIDE, step, 0)


def attend_back(s, p, qkv, seg, segcol, lse, datt, qsum, vsum):
    width = s.width
    qc, kc, vc = [slice(j * width + p * 128, j * width + p * 128 + 128) for j in range(3)]

    def step(i, sums):
        rows = at(i, SEQ)
        q = qkv[rows, qc] * jnp.asarray(0.125, BF)
        k, v, g = qkv[rows, kc], qkv[rows, vc], datt[rows, qc]
        kT = k.T
        ok = allowed_of(seg, segcol, i)
        dqs, dks, dvs = [], [], []
        for half in (0, 1):
            scores = jnp.where(ok, dot_nt(k, pick_lanes(half, q)), LARGE_NEG)
            prob = jnp.exp(scores - lse[2 * (i * s.pairs + p) + half])
            dprob = dot_nt(v, pick_lanes(half, g))
            weighted = jnp.sum(prob * dprob, 0, keepdims=True)
            dscore = (prob * (dprob - weighted)).astype(BF)
            dvs.append(dot_nn(prob.astype(BF), g))
            dks.append(dot_nn(dscore, q))
            dqs.append(dot_nn(kT[64 * half : 64 * half + 64], dscore))
        mask = lane_of(0)
        dq = (jnp.concatenate(dqs, 0) * 0.125).T.astype(BF)
        dk = jnp.where(mask, dks[0], dks[1]).astype(BF)
        dv = jnp.where(mask, dvs[0], dvs[1]).astype(BF)
        qkv[rows, qc] = dq
        qkv[rows, kc] = dk
        qkv[rows, vc] = dv
        return sums[0] + down_sum(dq.astype(F32)), sums[1] + down_sum(dv.astype(F32))

    zero = jnp.zeros((1, 128), F32)
    qs, vs = lax.fori_loop(0, s.seqs, step, (zero, zero))
    qsum[:, p * 128 : p * 128 + 128] = qs
    vsum[:, p * 128 : p * 128 + 128] = vs


def qkv_grad(s, a1T, dqkv, p, part):
    width = s.width

    def step(r, _):
        rows = at(r, WIDE)
        for j in range(3):
            cols = slice(j * width + p * 128, j * width + p * 128 + 128)
            part(j)[rows, :] = dot_nn(a1T[rows, :], dqkv[:, cols]).astype(BF)
        return 0

    lax.fori_loop(0, width // WIDE, step, 0)


def norm_one_back(s, tok, vec, dqkv, wqkv, dx2, ingrad, vgrad):
    def step(i, sums):
        rows = at(i, ROWS)
        width = s.width
        grad = sum(dot_nt(dqkv[rows, j * width : (j + 1) * width], wqkv[j]) for j in range(3))
        xhat, inverse = normed(tok[rows, :].astype(F32))
        ingrad[rows, :] = (dx2[rows, :] + norm_back(grad, xhat, inverse, vec[0:1, :])).astype(BF)
        return sums[0] + down_sum(grad * xhat), sums[1] + down_sum(grad)

    zero = jnp.zeros((1, s.width), F32)
    sums = lax.fori_loop(0, s.blocks, step, (zero,) * 2)
    vgrad[0:1, :] = sums[0]
    vgrad[1:2, :] = sums[1]


def block_kernel(
    s, tok_h, cot_h, seg, vec, ubias, wqkv_h, wout_h, wup_h, wdown_h,
    out_h, ingrad_h, gqkv_h, gout_h, gup_h, gdown_h, vgrad, ugrad,
    tok, cot, act, actT, attT, qkv, x2, mo, da2, hid, du,
    wqkv, wout, wup, wdown, segcol, lse, narrow, wide, thin, sems,
):
    rows, width = s.rows, s.width
    loads = [
        pltpu.make_async_copy(a, b, sems.at[i])
        for i, (a, b) in enumerate(
            [(tok_h, tok), (wout_h, wout), (wup_h, wup), (wdown_h, wdown)]
            + [(wqkv_h.at[:, j * width : (j + 1) * width], wqkv.at[j]) for j in range(3)]
        )
    ]
    for load in loads:
        load.start()
    setup_masks(s, seg, segcol)
    vgrad[...] = jnp.zeros_like(vgrad)
    loads[0].wait()
    norm_one(s, tok, vec, act)
    for load in loads[4:]:
        load.wait()
    for group in range(3):
        project_qkv(s, act, wqkv, vec, qkv, group)
        attend(s, group, qkv, seg, segcol, lse, cot, attT)
    loads[1].wait()
    project_out(s, tok, vec, cot, wout, x2, act, actT)
    load = pltpu.make_async_copy(cot_h, cot, sems.at[7])
    load.start()
    load.wait()
    loads[2].wait()
    loads[3].wait()

    def dump(src, dst):
        copy = pltpu.make_async_copy(src, dst, sems.at[8])
        copy.start()
        copy.wait()

    def tile_step(t, _):
        mlp_tile(s, t, 0, s.blocks, cot, ubias, act, wup, wdown, mo, da2, hid, du, ugrad)
        up_grad(s, actT, du, lambda h: narrow.at[h])
        dump(narrow, gup_h.at[t])
        down_grad(s, hid, cot, lambda h: wide.at[h, pl.ds(0, s.tile)])
        dump(wide.at[:, pl.ds(0, s.tile)], gdown_h.at[t])
        return 0

    lax.fori_loop(0, s.tiles, tile_step, 0)
    datt, dbr, stage = (wdown.at[j * rows : (j + 1) * rows] for j in range(3))
    a1T = wup.at[:, 0:rows]
    norm_two_back(s, cot, vec, x2, mo, da2, stage, dbr, vgrad)
    dump(stage, out_h)
    att_grad(s, dbr, wout, datt)
    out_grad(s, attT, dbr, lambda h: wide.at[h, pl.ds(0, width)])
    dump(wide.at[:, pl.ds(0, width)], gout_h)
    norm_one_flipped(s, tok, vec, a1T)
    for g in range(s.pairs // 2):
        for h in range(2):
            p = 2 * g + h
            attend_back(s, p, qkv, seg, segcol, lse, datt, vgrad.at[2:3, :], vgrad.at[3:4, :])
            qkv_grad(s, a1T, qkv, p, lambda j: thin.at[h, j])
        dump(thin, gqkv_h.at[g])
    norm_one_back(s, tok, vec, qkv, wqkv, x2, stage, vgrad)
    dump(stage, ingrad_h)


MESH = pl.DeviceIdType.MESH
LINK_RATE = 90e3
CORE_RATE = 400e3
LATENCY = 4.5


class Timeline:
    def __init__(self):
        self.now, self.free, self.jobs = 0.0, {}, []

    def begin(self, job):
        self.jobs.append(job)
        self.launch(job, job.first)

    def launch(self, job, made):
        link, cost = made
        start = max(self.now, self.free.get(link, 0.0))
        self.free[link] = start + cost
        job.ready = start + cost + LATENCY

    def advance(self, job):
        self.now = max(self.now, job.ready)
        made = job.steps[job.done]()
        job.done += 1
        if made is None:
            self.jobs.remove(job)
        else:
            self.launch(job, made)

    def due(self, job):
        link = job.links[job.done]
        return max(job.ready, self.free.get(link, 0.0) - QUEUE) if link in ("x", "y", "z") else job.ready

    def next(self):
        return min(self.jobs, key=self.due)

    def tick(self, cost):
        end = self.now + cost
        while self.jobs:
            job = self.next()
            if self.due(job) > end:
                break
            self.now = max(self.now, min(self.due(job), end))
            self.advance(job)
        self.now = max(self.now, end)

    def need(self, job, steps=None):
        while job in self.jobs and (steps is None or job.done < steps):
            self.advance(self.next())

    def drain(self):
        while self.jobs:
            self.advance(self.next())


class Job:
    def __init__(self, first, steps, links):
        self.first, self.steps, self.links, self.done, self.ready = first, steps, links, 0, 0.0


def cut(ref, start, count):
    rows = pl.ds(pl.multiple_of(start, 16), count)
    return ref.at[rows, :] if len(ref.shape) == 2 else ref.at[:, rows, :]


def size_of(ref):
    total = 2
    for n in ref.shape:
        total *= n
    return total


class Place:
    def __init__(self, far):
        d, self.f = lax.axis_index("dp"), lax.axis_index("fsdp")
        self.d, self.far = d, far
        self.c, self.b, self.a = d % 2, (d // 2) % 2, d // 4
        self.core = {"dp": d + 1 - 2 * self.c, "fsdp": self.f}
        self.near = {"dp": d + 2 - 4 * self.b, "fsdp": self.f}
        self.across = {"dp": d, "fsdp": 1 - self.f}

    def other(self, k):
        return {"dp": lax.rem(self.a + k, self.far) * 4 + self.b * 2 + self.c, "fsdp": self.f}

    def spot(self, k):
        place = lax.rem(self.b * self.far + self.a + k, 2 * self.far)
        return {"dp": place % self.far * 4 + place // self.far * 2 + self.c, "fsdp": self.f}, place

    def bit(self, level):
        return (self.a // 2**level) % 2

    def flipped(self, level):
        step = (1 - 2 * self.bit(level)) * 2**level
        return {"dp": self.d + 4 * step, "fsdp": self.f}


def remote(src, dst, send, recv, device):
    return pltpu.make_async_remote_copy(
        src_ref=src, dst_ref=dst, send_sem=send, recv_sem=recv, device_id=device, device_id_type=MESH
    )


def gather_job(s, me, j, view, sems):
    send, recv = sems
    size = s.width // 2 // 4
    quarter = (me.c * 2 + me.b) * size
    first = remote(view(j, me.f, quarter, size), view(j, me.f, quarter, size), send.at[j, 0], recv.at[j, 0], me.across)
    g = 1 - me.f
    second = remote(view(j, g, quarter, size), view(j, g, quarter, size), send.at[j, 1], recv.at[j, 1], me.near)
    half = me.c * 2 * size
    third = remote(view(j, g, half, 2 * size), view(j, g, half, 2 * size), send.at[j, 2], recv.at[j, 2], me.core)
    cost = 2 * 2 * size * s.width / LINK_RATE

    def step_one():
        first.wait_recv()
        second.start()
        return ("y", cost)

    def step_two():
        second.wait_recv()
        third.start()
        return ("core", 2 * 2 * size * s.width / CORE_RATE)

    def step_three():
        third.wait_recv()
        return None

    first.start()
    return Job(("x", cost), [step_one, step_two, step_three], ["y", "core", ""]), [first, second, third]


class Unit:
    def __init__(self, index, own, other, into, out, direct=False):
        self.index, self.own, self.other, self.into, self.out, self.direct = index, own, other, into, out, direct
        self.rows = own.shape[-2]


def unit_job(s, me, unit, send, recv, give, take):
    u, own, far = unit.index, unit.own, me.far
    half, quarter = unit.rows // 2, unit.rows // 4
    piece = quarter // far
    r1, r2, r3 = unit.into
    r4 = cut(r3, quarter, r3.shape[-2] - quarter)
    r3 = cut(r3, 0, quarter)
    size = size_of(own)
    levels = far.bit_length() - 1
    mine, mine_b = me.f * half, me.f * half + me.b * quarter
    one = remote(unit.other, r1, send.at[u, 0], recv.at[u, 0], me.core)
    two = remote(cut(own, (1 - me.f) * half, half), r2, send.at[u, 1], recv.at[u, 1], me.across)
    three = remote(cut(own, mine + (1 - me.b) * quarter, quarter), r3, send.at[u, 2], recv.at[u, 2], me.near)
    four, kept, offset, used = [], [], 0, 0
    for level in range(levels):
        part, bit = quarter >> (level + 1), me.bit(level)
        arrived = cut(r4, used, part)
        theirs = cut(own, mine_b + offset + (1 - bit) * part, part)
        four.append(remote(theirs, arrived, send.at[u, 3 + level], recv.at[u, 3 + level], me.flipped(level)))
        offset = offset + bit * part
        kept.append((cut(own, mine_b + offset, part), arrived))
        used += part
    final = cut(own, mine_b + offset, piece)
    target = unit.out(me.b * quarter + offset, piece)
    base = 2 + levels
    five = [remote(final, target, send.at[u, base + k], recv.at[u, base + k], me.other(k)) for k in range(1, far)]
    n = base + far
    keep = pltpu.make_async_copy(final, target, send.at[u, n + 2])
    block = unit.out(me.b * quarter, quarter)
    six = remote(block, block, send.at[u, n], recv.at[u, n], me.near)
    all_rows = unit.out(0, half)
    seven = remote(all_rows, all_rows, send.at[u, n + 1], recv.at[u, n + 1], me.core)

    def add_into(part, arrived):
        part[...] = part[...] + arrived[...]

    def step_one():
        one.wait_recv()
        add_into(own, r1)
        if give is not None:
            pl.semaphore_signal(give, inc=1, device_id=me.core, device_id_type=MESH)
        two.start()
        return ("x", size / LINK_RATE)

    def step_two():
        two.wait_recv()
        add_into(cut(own, mine, half), r2)
        three.start()
        return ("y", size / 2 / LINK_RATE)

    def step_three():
        three.wait_recv()
        add_into(cut(own, mine_b, quarter), r3)
        four[0].start()
        return ("z", size / 4 / LINK_RATE)

    def fold(level):
        def step():
            four[level].wait_recv()
            add_into(*kept[level])
            if level + 1 < levels:
                four[level + 1].start()
                return ("z", size / 4 / LINK_RATE)
            keep.start()
            for copy in five:
                copy.start()
            return ("z", size / 2 / LINK_RATE)

        return step

    def step_five():
        keep.wait()
        for copy in five:
            copy.wait_recv()
        six.start()
        return ("y", size / 2 / LINK_RATE)

    def step_six():
        six.wait_recv()
        seven.start()
        return ("core", size / 2 / CORE_RATE)

    def step_seven():
        seven.wait_recv()
        return None

    def step_seven_of(copy):
        def step():
            copy().wait_recv()
            return None

        return step

    def direct_two():
        two.wait_recv()
        add_into(cut(own, mine, half), r2)
        for copy in parts:
            copy.start()
        return ("z", size / LINK_RATE)

    def direct_three():
        value = final[...].astype(F32)
        for k, copy in enumerate(parts):
            copy.wait_recv()
            value = value + cut(unit.into[2], k * piece, piece)[...].astype(F32)
        final[...] = value.astype(BF)
        keep.start()
        for copy in five:
            copy.start()
        return ("z", size / LINK_RATE)

    def direct_four():
        keep.wait()
        for copy in five:
            copy.wait_recv()
        seven.start()
        return ("core", size / 2 / CORE_RATE)

    if take is not None:
        pl.semaphore_wait(take, 1)
    one.start()
    if unit.direct:
        here = me.b * far + me.a
        final = cut(own, mine + here * piece, piece)
        target = unit.out(here * piece, piece)
        parts, five = [], []
        for k in range(1, 2 * far):
            device, place = me.spot(k)
            slot = cut(unit.into[2], (k - 1) * piece, piece)
            parts.append(remote(cut(own, mine + place * piece, piece), slot, send.at[u, 1 + k], recv.at[u, 1 + k], device))
            five.append(remote(final, target, send.at[u, 2 * far + k], recv.at[u, 2 * far + k], device))
        n = 4 * far - 1
        keep = pltpu.make_async_copy(final, target, send.at[u, n + 2])
        seven = remote(all_rows, all_rows, send.at[u, n + 1], recv.at[u, n + 1], me.core)
        steps = [step_one, direct_two, direct_three, direct_four, step_seven_of(lambda: seven)]
        return Job(("core", size / CORE_RATE), steps, ["x", "z", "z", "core", ""]), one, [two, *parts, *five, seven]
    folds = [fold(level) for level in range(levels)]
    steps = [step_one, step_two, step_three, *folds, step_five, step_six, step_seven]
    links = ["x", "y"] + ["z"] * (levels + 1) + ["y", "core", ""]
    return Job(("core", size / CORE_RATE), steps, links), one, [two, three, *four, *five, six, seven]


def vector_job(me, slots, sends, recvs, finish):
    core_s, x_s, near_s, far_s = slots
    stops = ((core_s, me.c, me.core), (x_s, me.f, me.across), (near_s, me.b, me.near))
    hops = [remote(s.at[i], s.at[i], sends.at[n], recvs.at[n], device) for n, (s, i, device) in enumerate(stops)]
    last = [
        remote(far_s.at[me.a], far_s.at[me.a], sends.at[2 + k], recvs.at[2 + k], me.other(k)) for k in range(1, me.far)
    ]
    cost = ("small", 0.4)

    def hop(n):
        def step():
            hops[n].wait()
            total = stops[n][0][0] + stops[n][0][1]
            if n < 2:
                stops[n + 1][0][stops[n + 1][1]] = total
                hops[n + 1].start()
            else:
                far_s[me.a] = total
                for copy in last:
                    copy.start()
            return cost

        return step

    def end():
        for copy in last:
            copy.wait()
        total = far_s[0]
        for k in range(1, me.far):
            total = total + far_s[k]
        far_s[0] = total
        finish()
        return None

    hops[0].start()
    return Job(cost, [hop(0), hop(1), hop(2), end], ["small"] * 3 + [""])


def linked_kernel(
    s, far, tok_h, cot_h, seg, g1_h, s1_h, qb_h, vb_h, ob_h, g2_h, s2_h, db_h, ub_h, wqkv_h, wout_h, wup_h, wdown_h,
    out_h, ingrad_h, gqkv_h, gout_h, gup_h, gdown_h, vout,
    tok, cot, act, actT, attT, qkv, x2, mo, da2, hid, du,
    wqkv, wout, wup, wdown, segcol, lse, raw, raw_up, packed, vec, ubias, ugrad, core_s, x_s, near_s, far_s,
    own_up, own_down, oth_up, oth_down,
    r1_up, r1_down, r1_out, r1_qkv, r2_up, r2_down, r2_out, r2_qkv,
    r3_up, r3_down, r3_out, r3_qkv,
    loads, wsend, wrecv, usend, urecv, vsend, vrecv, credit,
):
    rows, width = s.rows, s.width
    me = Place(far)
    line = Timeline()
    shard, third = width // 2, width // 3
    count = s.hidden // width

    barrier = pltpu.get_barrier_semaphore()
    partners = [me.core, me.across] + [me.spot(k)[0] for k in range(1, 2 * far)]
    for device in partners:
        pl.semaphore_signal(barrier, inc=1, device_id=device, device_id_type=MESH)

    names = [("qkv", 0), ("qkv", 1), ("qkv", 2), ("out", 0)]
    order = [i for k in range(count // 2) for i in (k, k + count // 2)]
    for n in range(0, count, 2):
        names += [("up", order[n]), ("up", order[n + 1]), ("down", n), ("down", n + 1)]

    def view(j, f, start, size):
        kind, i = names[j]
        if kind == "down":
            return wdown.at[pl.ds(pl.multiple_of(f * s.share + i * shard + start, 16), size), :]
        part = pl.ds(pl.multiple_of(f * shard + start, 16), size)
        if kind == "out":
            return wout.at[part, :]
        if kind == "qkv":
            return wqkv.at[:, part, i * third : (i + 1) * third]
        return wup.at[part, i * width : (i + 1) * width]

    def masters(j):
        kind, i = names[j]
        if kind == "down":
            return [(wdown_h.at[i * shard : (i + 1) * shard, :], stages[j % 4])]
        if kind == "out":
            return [(wout_h.at[...], stages[j % 4])]
        if kind == "up":
            return [(wup_h.at[:, i * width : (i + 1) * width], stages[j % 4])]
        starts = [n * width + i * third for n in range(3)]
        return [
            (wqkv_h.at[:, start : start + third], stages[j % 4].at[:, n * third : (n + 1) * third])
            for n, start in enumerate(starts)
        ]

    stages = [mo.at[0:shard], mo.at[shard : 2 * shard], da2.at[0:shard], da2.at[shard : 2 * shard]]
    copies = [
        [pltpu.make_async_copy(a, b, loads.at[j % 4, n]) for n, (a, b) in enumerate(masters(j))]
        for j in range(len(names))
    ]
    for j in range(4):
        for copy in copies[j]:
            copy.start()
    load_tok = pltpu.make_async_copy(tok_h, tok, loads.at[4, 0])
    load_tok.start()
    per = shard // 128
    small = [(a, raw.at[n]) for n, a in enumerate((g1_h, s1_h, qb_h, vb_h, ob_h, g2_h, s2_h, db_h))] + [(ub_h, raw_up)]
    small = [pltpu.make_async_copy(a, b, loads.at[6 + n // 3, n % 3]) for n, (a, b) in enumerate(small)]
    for copy in small:
        copy.start()
    share_small = remote(packed.at[me.f], packed.at[me.f], vsend.at[2 + far], vrecv.at[2 + far], me.across)
    pl.semaphore_wait(barrier, len(partners))
    sent, moved, jobs = [share_small], [], []
    for j in range(len(names)):
        for copy in copies[j]:
            copy.wait()
        if names[j][0] == "qkv":
            for n in range(3):
                view(j, me.f, 0, shard)[n] = stages[j % 4][:, n * third : (n + 1) * third].astype(BF)
        else:
            view(j, me.f, 0, shard)[...] = stages[j % 4][...].astype(BF)
        if j + 4 < len(names):
            for copy in copies[j + 4]:
                copy.start()
        if j == 2:
            for copy in small:
                copy.wait()
            packed[me.f] = jnp.zeros((packed.shape[1], 128), F32)
            for n in range(8):
                packed[me.f, n * per : n * per + per, :] = raw[n].astype(BF).astype(F32)
            packed[me.f, 8 * per : 8 * per + s.share // 128, :] = raw_up[...].astype(BF).astype(F32)
            share_small.start()
        job, made = gather_job(s, me, j, view, (wsend, wrecv))
        line.begin(job)
        line.now += 0.5
        jobs.append(job)
        (moved if names[j][0] in ("up", "down") else sent).extend(made)
    setup_masks(s, seg, segcol)
    core_s[...] = jnp.zeros_like(core_s)
    share_small.wait_recv()
    for f in range(2):
        for i in range(8 * per):
            r, col = i // per, f * shard + i % per * 128
            vec[r : r + 1, col : col + 128] = packed[f, i : i + 1, :]
        for i in range(s.share // 128):
            ubias[f, :, i * 128 : (i + 1) * 128] = packed[f, 8 * per + i : 8 * per + i + 1, :]
    load_tok.wait()
    norm_one(s, tok, vec, act)
    line.tick(3.0)
    for group in range(3):
        line.need(jobs[group])
        project_qkv(s, act, wqkv, vec, qkv, group)
        line.tick(1.6)
        attend(s, group, qkv, seg, segcol, lse, cot, attT)
        line.tick(3.8)
    line.need(jobs[3])
    project_out(s, tok, vec, cot, wout, x2, act, actT)
    load_cot = pltpu.make_async_copy(cot_h, cot, loads.at[5, 0])
    load_cot.start()
    line.tick(2.5)

    c = me.c
    units, firsts, later = [], [], []
    pending = {}

    def start_unit(unit, kind=None, slot=0, reuse=False, again=False):
        give = credit.at[kind * 2 + slot] if again else None
        take = credit.at[kind * 2 + slot] if reuse else None
        job, one, made = unit_job(s, me, unit, usend, urecv, give, take)
        line.begin(job)
        later.extend(made)
        return job, one

    vgrad = core_s.at[c]
    load_cot.wait()
    for t in range(s.tiles):
        for j, (kind, i) in enumerate(names):
            if kind == "up":
                lo, hi = i * width, (i + 1) * width
                used = any(f * s.share + t * s.piece < hi and f * s.share + (t + 1) * s.piece > lo for f in range(2))
            elif kind == "down":
                used = t * s.piece < (i + 1) * shard and (t + 1) * s.piece > i * shard
            else:
                used = False
            if used:
                line.need(jobs[j])
        slot = t % 2
        mlp_tile(s, t, 0, s.blocks, cot, ubias, act, wup, wdown, mo, da2, hid, du, ugrad)
        line.tick(4.2)
        if t >= 2:
            job, one = pending["up", t - 2]
            line.need(job, 1)
            one.wait_send()
        up_grad_linked(s, actT, du, c, own_up.at[t], oth_up.at[slot])
        unit = Unit(
            2 * t, own_up.at[t], oth_up.at[slot],
            (r1_up.at[slot], r2_up.at[t], r3_up.at[t]),
            lambda start, n, t=t: gup_h.at[pl.ds(pl.multiple_of(start, 16), n), span(c * s.share + t * s.piece, s.piece)],
        )
        pending["up", t] = start_unit(unit, 0, slot, t >= 2, t + 2 < s.tiles)
        line.tick(1.5)
        if t >= 2:
            job, one = pending["down", t - 2]
            line.need(job, 1)
            one.wait_send()
        down_grad_linked(s, hid, cot, c, own_down.at[t], oth_down.at[slot])
        unit = Unit(
            2 * t + 1, own_down.at[t], oth_down.at[slot],
            (r1_down.at[slot], r2_down.at[t], r3_down.at[t]),
            lambda start, n, t=t: gdown_h.at[
                pl.ds(pl.multiple_of(t * s.piece + start, 16), n), span(c * shard, shard)
            ],
        )
        pending["down", t] = start_unit(unit, 1, slot, t >= 2, t + 2 < s.tiles)
        line.tick(1.3)
    for job in jobs:
        line.need(job)
    for copy in moved:
        copy.wait_send()
    datt, dbr, stage = (wdown.at[j * rows : (j + 1) * rows] for j in range(3))
    a1T = wup.at[:, 0:rows]
    own_out, oth_out = (wup.at[:, rows + j * shard : rows + (j + 1) * shard] for j in range(2))
    own_qkv = [wup.at[:, n : n + 384] for n in range(rows + width, s.hidden - 383, 384)]
    oth_qkv = [actT.at[:, n : n + 384] for n in range(0, rows - 383, 384)]
    norm_two_back(s, cot, vec, x2, mo, da2, stage, dbr, vgrad)
    save_out = pltpu.make_async_copy(stage, out_h, loads.at[5, 0])
    save_out.start()
    line.tick(2.5)
    out_grad_linked(s, attT, dbr, c, own_out, oth_out)
    unit = Unit(
        2 * s.tiles, own_out, oth_out,
        (r1_out, r2_out, r3_out),
        lambda start, n: gout_h.at[pl.ds(pl.multiple_of(start, 16), n), span(c * shard, shard)],
    )
    pending["out"] = start_unit(unit)
    line.tick(1.3)
    att_grad(s, dbr, wout, datt)
    line.tick(2.2)
    norm_one_flipped(s, tok, vec, a1T)
    line.tick(1.7)
    for g in range(s.pairs // 2):
        for h in range(2):
            attend_back(s, 2 * g + h, qkv, seg, segcol, lse, datt, vgrad.at[2:3, :], vgrad.at[3:4, :])
            line.tick(3.8)
        own, other = own_qkv[g], oth_qkv[g % len(oth_qkv)]
        if g >= len(oth_qkv):
            pending["qkv", g - len(oth_qkv)][1].wait_send()
        for j in range(3):
            cols = slice(j * 128, j * 128 + 128)
            qkv_grad_linked(s, a1T, qkv, g, j, c, own.at[:, cols], other.at[:, cols])
        unit = Unit(
            2 * s.tiles + 1 + g, own, other, (r1_qkv.at[g], r2_qkv.at[g], r3_qkv.at[g]),
            lambda start, size, g=g: gqkv_h.at[
                pl.ds(pl.multiple_of(start, 16), size), span((2 * g + c) * 384, 384)
            ],
        )
        pending["qkv", g] = start_unit(unit)
        line.tick(1.8)
    save_out.wait()
    norm_one_back(s, tok, vec, qkv, wqkv, x2, stage, vgrad)
    line.tick(5.0)
    save_in = pltpu.make_async_copy(stage, ingrad_h, loads.at[4, 0])
    save_in.start()
    part = math.gcd(s.share, width)
    for i in range(s.hidden // part):
        start = i * part
        f, off = start // s.share, start % s.share
        r, col = 8 + start // width, start % width
        vgrad[r : r + 1, col : col + part] = ugrad[f, :, off : off + part]

    def finish():
        vout[...] = jnp.zeros_like(vout)
        for f in range(2):

            @pl.when(me.f == f)
            def _(f=f):
                for i in range(8 * per):
                    r, col = i // per, f * shard + i % per * 128
                    vout[i : i + 1, :] = far_s[0, r : r + 1, col : col + 128]
                for i in range(s.share // 128):
                    flat = f * s.share + i * 128
                    r, col = 8 + flat // width, flat % width
                    vout[8 * per + i : 8 * per + i + 1, :] = far_s[0, r : r + 1, col : col + 128]

    line.begin(vector_job(me, (core_s, x_s, near_s, far_s), vsend, vrecv, finish))
    line.drain()
    save_in.wait()
    for key, (job, one) in pending.items():
        if key == "out" or key[1] + 2 >= (s.pairs // 2 if key[0] == "qkv" else s.tiles):
            one.wait_send()
    for copy in later + sent:
        copy.wait_send()


def split_store(c, value, own, other, rows):
    half = value.shape[-1] // 2
    left, right = value[:, :half].astype(BF), value[:, half:].astype(BF)
    own[rows, :] = jnp.where(c == 0, left, right)
    other[rows, :] = jnp.where(c == 0, right, left)


def up_grad_linked(s, a2T, du, c, own, other):
    def step(r, _):
        rows = at(r, WIDE)
        split_store(c, dot_nn(a2T[rows, :], du[...]), own, other, rows)
        return 0

    lax.fori_loop(0, s.width // WIDE, step, 0)


def down_grad_linked(s, hid, cot, c, own, other):
    def step(r, _):
        rows = at(r, ROWS)
        split_store(c, dot_tn(hid[:, rows], cot[...]), own, other, rows)
        return 0

    lax.fori_loop(0, s.tile // ROWS, step, 0)


def out_grad_linked(s, attT, dbr, c, own, other):
    def step(r, _):
        rows = at(r, WIDE)
        split_store(c, dot_nn(attT[rows, :], dbr[...]), own, other, rows)
        return 0

    lax.fori_loop(0, s.width // WIDE, step, 0)


def qkv_grad_linked(s, a1T, dqkv, g, j, c, own, other):
    start = j * s.width + 2 * g * 128
    split_store(c, dot_nn(a1T[...], dqkv[:, start : start + 256]), own, other, slice(None))


def linked_body(far, tokens, segment_ids, cotangent, *params):
    (
        norm1_gain, norm1_shift, qkv_weight, query_bias, value_bias, out_weight, out_bias, norm2_gain, norm2_shift,
        up_weight, up_bias, down_weight, down_bias,
    ) = params
    rows, width = tokens.shape
    hidden = up_weight.shape[1]
    s = Sizes(rows, width, hidden, 2)
    shard, tiles, tile, groups = width // 2, s.tiles, s.tile, s.pairs // 2
    vectors = [norm1_gain, norm1_shift, query_bias, value_bias, out_bias, norm2_gain, norm2_shift, down_bias]
    vectors = [v.reshape(-1, 128) for v in vectors + [up_bias]]
    lines_all = -(-sum(v.shape[0] for v in vectors) // 8) * 8
    seg = segment_ids.reshape(s.seqs, 1, SEQ)
    whole = pl.BlockSpec(memory_space=pltpu.VMEM)
    away = pl.BlockSpec(memory_space=pl.ANY)

    def vm(*shape, kind=BF):
        return pltpu.VMEM(shape, kind)

    n_units, n_blocks = 2 * tiles + 1 + groups, 4 + 2 * (hidden // width)
    up, down, out, qk = (width, tile // 2), (tile, shard), (width, shard), (width, 384)

    def part(shape, by):
        return shape[:-2] + (shape[-2] // by, shape[-1])

    def rest(shape):
        return shape[:-2] + (shape[-2] // (4 * far) * (2 * far - 1), shape[-1])

    slots = min(2, tiles)
    scratch = [
        vm(rows, width), vm(rows, width), vm(rows, width), vm(width, rows), vm(width, rows), vm(rows, 3 * width),
        vm(rows, width, kind=F32), vm(rows, width, kind=F32), vm(rows, width, kind=F32), vm(rows, tile), vm(rows, tile),
        vm(3, width, width), vm(width, width), vm(width, hidden), vm(hidden, width),
        vm(s.seqs, SEQ, 128, kind=F32), vm(s.seqs * HEADS, 1, SEQ, kind=F32),
        vm(8, shard // 128, 128, kind=F32), vm(s.share // 128, 128, kind=F32),
        vm(2, lines_all, 128, kind=F32), vm(8, width, kind=F32), vm(2, 1, s.share, kind=F32), vm(2, 1, s.share, kind=F32),
        vm(2, 16, width, kind=F32), vm(2, 16, width, kind=F32), vm(2, 16, width, kind=F32), vm(far, 16, width, kind=F32),
        vm(tiles, *up), vm(tiles, *down), vm(slots, *up), vm(slots, *down),
        vm(slots, *up), vm(slots, *down), vm(*out), vm(groups, *qk),
        vm(tiles, *part(up, 2)), vm(tiles, *part(down, 2)), vm(*part(out, 2)), vm(groups, *part(qk, 2)),
        vm(tiles, *rest(up)), vm(tiles, *rest(down)), vm(*rest(out)), vm(groups, *rest(qk)),
        pltpu.SemaphoreType.DMA((9, 3)),
        pltpu.SemaphoreType.DMA((n_blocks, 3)),
        pltpu.SemaphoreType.DMA((n_blocks, 3)),
        pltpu.SemaphoreType.DMA((n_units, 4 * far + 2)),
        pltpu.SemaphoreType.DMA((n_units, 4 * far + 2)),
        pltpu.SemaphoreType.DMA((far + 3,)),
        pltpu.SemaphoreType.DMA((far + 3,)),
        pltpu.SemaphoreType.REGULAR((4,)),
    ]
    output, input_grad, gqkv, gout, gup, gdown, v = pl.pallas_call(
        functools.partial(linked_kernel, s, far),
        out_shape=(
            jax.ShapeDtypeStruct((rows, width), BF),
            jax.ShapeDtypeStruct((rows, width), BF),
            jax.ShapeDtypeStruct((shard, 3 * width), BF),
            jax.ShapeDtypeStruct((shard, width), BF),
            jax.ShapeDtypeStruct((shard, hidden), BF),
            jax.ShapeDtypeStruct((hidden // 2, width), BF),
            jax.ShapeDtypeStruct((lines_all, 128), F32),
        ),
        in_specs=[away, away, whole] + [away] * 13,
        out_specs=(away,) * 6 + (whole,),
        scratch_shapes=scratch,
        compiler_params=pltpu.CompilerParams(
            vmem_limit_bytes=61 << 20, collective_id=0, has_side_effects=True
        ),
    )(tokens, cotangent, seg, *vectors, qkv_weight, out_weight, up_weight, down_weight)
    grads = (gqkv, gout, gup, gdown)
    lines = [shard // 128] * 8 + [s.share // 128]
    final = pl.pallas_call(
        functools.partial(finish_kernel, lines),
        out_shape=(
            [jax.ShapeDtypeStruct((rows, width), BF)] * 2
            + [jax.ShapeDtypeStruct(g.shape, F32) for g in grads]
            + [jax.ShapeDtypeStruct((n, 128), F32) for n in lines]
        ),
        in_specs=[away] * 6 + [whole],
        out_specs=[away] * 6 + [whole] * len(lines),
        scratch_shapes=(
            [pltpu.VMEM(g.shape, BF) for g in grads]
            + [pltpu.VMEM(g.shape, F32) for g in grads]
            + [pltpu.VMEM((2, rows, width), BF)]
            + [pltpu.SemaphoreType.DMA((2,)), pltpu.SemaphoreType.DMA((4, CHUNKS)), pltpu.SemaphoreType.DMA((4, CHUNKS))]
        ),
        compiler_params=pltpu.CompilerParams(vmem_limit_bytes=61 << 20),
    )(output, input_grad, *grads, v)
    output, input_grad, gqkv, gout, gup, gdown = final[:6]
    v = [value.reshape(-1) for value in final[6:]]
    return (
        output, input_grad, v[0], v[1], gqkv, v[2], v[3], gout, v[4], v[5], v[6], gup, v[8], gdown, v[7],
    )


CHUNKS = 4


def finish_kernel(lines, *refs):
    ins, v, outs, small = refs[:6], refs[6], refs[7:13], refs[13 : 13 + len(lines)]
    held, wide = refs[13 + len(lines) : 17 + len(lines)], refs[17 + len(lines) : 21 + len(lines)]
    passing, whole, loads, stores = refs[21 + len(lines) :]
    lift = [pltpu.make_async_copy(ins[n], passing.at[n], whole.at[n]) for n in range(2)]
    drop = [pltpu.make_async_copy(passing.at[n], outs[n], whole.at[n]) for n in range(2)]
    chunks = []
    for n in range(4):
        rows = held[n].shape[0] // CHUNKS
        for i in range(CHUNKS):
            part = pl.ds(i * rows, rows)
            chunks.append((n, i, part))
    into = [pltpu.make_async_copy(ins[2 + n].at[part], held[n].at[part], loads.at[n, i]) for n, i, part in chunks]
    back = [pltpu.make_async_copy(wide[n].at[part], outs[2 + n].at[part], stores.at[n, i]) for n, i, part in chunks]
    for copy in lift + into:
        copy.start()
    start = 0
    for ref, count in zip(small, lines):
        ref[...] = v[start : start + count, :]
        start += count
    for n in range(2):
        lift[n].wait()
        drop[n].start()
    for (n, _i, part), load, store in zip(chunks, into, back):
        load.wait()
        if n:
            wide[n][part, :] = held[n][part, :].astype(F32)
        else:
            for p in range(HEADS // 2):
                for j in range(3):
                    value = held[n][part, p * 384 + j * 128 : p * 384 + j * 128 + 128]
                    start = (j * (HEADS // 2) + p) * 128
                    wide[n][part, start : start + 128] = value.astype(F32)
        store.start()
    for copy in back + drop:
        copy.wait()


def body(
    tokens, segment_ids, cotangent, norm1_gain, norm1_shift, qkv_weight, query_bias, value_bias,
    out_weight, out_bias, norm2_gain, norm2_shift, up_weight, up_bias, down_weight, down_bias,
):
    shards = lax.axis_size("fsdp")
    rows, width = tokens.shape
    hidden = up_weight.shape[1]
    s = Sizes(rows, width, hidden, shards)
    small = [norm1_gain, norm1_shift, query_bias, value_bias, out_bias, norm2_gain, norm2_shift, down_bias]
    vec = lax.all_gather(jnp.stack(small).astype(BF), "fsdp", axis=1, tiled=True).astype(F32)
    ubias = lax.all_gather(up_bias.astype(BF), "fsdp", axis=0).astype(F32)[:, None, :]
    weights = [
        lax.all_gather(w.astype(BF), "fsdp", axis=0, tiled=True)
        for w in (qkv_weight, out_weight, up_weight, down_weight)
    ]
    seg = segment_ids.reshape(s.seqs, 1, SEQ)
    whole = pl.BlockSpec(memory_space=pltpu.VMEM)
    away = pl.BlockSpec(memory_space=pl.ANY)
    groups = s.pairs // 2
    results = pl.pallas_call(
        functools.partial(block_kernel, s),
        out_shape=(
            jax.ShapeDtypeStruct((rows, width), BF),
            jax.ShapeDtypeStruct((rows, width), BF),
            jax.ShapeDtypeStruct((groups, 2, 3, width, 128), BF),
            jax.ShapeDtypeStruct((2, width, width // 2), BF),
            jax.ShapeDtypeStruct((s.tiles, 2, width, s.tile // 2), BF),
            jax.ShapeDtypeStruct((s.tiles, 2, s.tile, width // 2), BF),
            jax.ShapeDtypeStruct((8, width), F32),
            jax.ShapeDtypeStruct((shards, 1, s.share), F32),
        ),
        in_specs=[away, away, whole, whole, whole, away, away, away, away],
        out_specs=(away,) * 6 + (whole, whole),
        scratch_shapes=[
            pltpu.VMEM((rows, width), BF),
            pltpu.VMEM((rows, width), BF),
            pltpu.VMEM((rows, width), BF),
            pltpu.VMEM((width, rows), BF),
            pltpu.VMEM((width, rows), BF),
            pltpu.VMEM((rows, 3 * width), BF),
            pltpu.VMEM((rows, width), F32),
            pltpu.VMEM((rows, width), F32),
            pltpu.VMEM((rows, width), F32),
            pltpu.VMEM((rows, s.tile), BF),
            pltpu.VMEM((rows, s.tile), BF),
            pltpu.VMEM((3, width, width), BF),
            pltpu.VMEM((width, width), BF),
            pltpu.VMEM((width, hidden), BF),
            pltpu.VMEM((hidden, width), BF),
            pltpu.VMEM((s.seqs, SEQ, 128), F32),
            pltpu.VMEM((s.seqs * HEADS, 1, SEQ), F32),
            pltpu.VMEM((2, width, s.tile // 2), BF),
            pltpu.VMEM((2, max(width, s.tile), width // 2), BF),
            pltpu.VMEM((2, 3, width, 128), BF),
            pltpu.SemaphoreType.DMA((9,)),
        ],
        compiler_params=pltpu.CompilerParams(vmem_limit_bytes=61 << 20),
    )(tokens, cotangent, seg, vec, ubias, *weights)
    output, input_grad, gqkv, gout, gup, gdown, vgrad, ugrad = results
    gqkv = gqkv.transpose(3, 2, 0, 1, 4).reshape(width, 3 * width)
    gout = gout.transpose(1, 0, 2).reshape(width, width)
    half = s.tile // 2
    gup = gup.transpose(2, 0, 1, 3).reshape(width, s.tiles, shards, s.piece)
    gup = gup.transpose(0, 2, 1, 3).reshape(width, hidden)
    gdown = gdown.transpose(0, 2, 1, 3).reshape(s.tiles, shards, s.piece, width)
    gdown = gdown.transpose(1, 0, 2, 3).reshape(hidden, width)

    def summed(value):
        part = lax.psum_scatter(value.astype(BF), "fsdp", scatter_dimension=0, tiled=True)
        return lax.psum(part, "dp").astype(F32)

    gqkv, gout, gup, gdown = [summed(v) for v in (gqkv, gout, gup, gdown)]
    ugrad = summed(ugrad.reshape(hidden))
    v = [summed(vgrad[i]) for i in range(8)]
    return (
        output, input_grad, v[0], v[1], gqkv, v[2], v[3], gout, v[4], v[5], v[6], gup, ugrad, gdown, v[7],
    )


def solution(mesh):
    rows, wide, long = P(("dp", "fsdp"), None), P("fsdp", None), P("fsdp")
    shards, copies = mesh.shape["fsdp"], mesh.shape["dp"]
    linked = shards == 2 and copies in (8, 16)
    return jax.shard_map(
        functools.partial(linked_body, copies // 4) if linked else body,
        mesh=mesh,
        in_specs=(
            rows, P(("dp", "fsdp")), rows, long, long, wide, long, long, wide, long, long, long, wide, long, wide, long,
        ),
        out_specs=(
            rows, rows, long, long, wide, long, long, wide, long, long, long, wide, long, wide, long,
        ),
        check_vma=False,
    )
```

```python
import functools
import math

import jax
import jax.numpy as jnp
from jax import lax
from jax.experimental import pallas as pl
from jax.experimental.pallas import tpu as pltpu
from jax.sharding import PartitionSpec as P

HEADS = 12
SEQ = 512
EPSILON = 1e-06
LARGE_NEG = -1000000000.0
BF = jnp.bfloat16
F32 = jnp.float32
ROWS = 512
WIDE = 384
DIRECT = 0
QUEUE = 1.0


def dot_of(left, right, over):
    return lax.dot_general(left, right, (over, ((), ())), preferred_element_type=F32)


def dot_nn(left, right):
    return dot_of(left, right, ((1,), (0,)))


def dot_nt(left, right):
    return dot_of(left, right, ((1,), (1,)))


def dot_tn(left, right):
    return dot_of(left, right, ((0,), (0,)))


def at(index, size):
    return pl.ds(pl.multiple_of(index * size, size), size)


def span(start, size):
    return pl.ds(pl.multiple_of(start, 128), size)


def mean_of(value):
    return jnp.sum(value, -1, keepdims=True) * (1.0 / value.shape[-1])


def normed(value):
    centre = value - mean_of(value)
    inverse = lax.rsqrt(mean_of(centre * centre) + EPSILON)
    return centre * inverse, inverse


def down_sum(value):
    return jnp.sum(value, 0, keepdims=True)


def gelu_pair(value):
    cumulative = 0.5 + 0.5 * lax.erf(value * 0.7071067811865476)
    density = jnp.exp(-0.5 * value * value) * 0.3989422804014327
    return value * cumulative, cumulative + value * density


def norm_back(grad, xhat, inverse, gain):
    scaled = grad * gain
    return inverse * (scaled - mean_of(scaled) - xhat * mean_of(scaled * xhat))


class Sizes:
    def __init__(self, rows, width, hidden, shards):
        self.rows, self.width, self.hidden, self.shards = rows, width, hidden, shards
        self.seqs = rows // SEQ
        self.pairs = HEADS // 2
        share = hidden // shards
        self.tiles = max(n for n in range(1, 7) if share % n == 0 and (share // n) % 128 == 0)
        self.share = share
        self.piece = share // self.tiles
        self.tile = self.piece * shards
        self.blocks = rows // ROWS


def setup_masks(s, seg, segcol):
    for i in range(s.seqs):
        segcol[i] = jnp.broadcast_to(seg[i].astype(F32), (128, SEQ)).T


def norm_one(s, tok, vec, a1):
    def step(i, _):
        rows = at(i, ROWS)
        xhat, _inv = normed(tok[rows, :].astype(F32))
        a1[rows, :] = (xhat * vec[0:1, :] + vec[1:2, :]).astype(BF)
        return 0

    lax.fori_loop(0, s.blocks, step, 0)


def norm_one_flipped(s, tok, vec, a1T):
    def step(i, _):
        rows = at(i, ROWS)
        xhat, _inv = normed(tok[rows, :].astype(F32))
        a1T[:, rows] = (xhat * vec[0:1, :] + vec[1:2, :]).T.astype(BF)
        return 0

    lax.fori_loop(0, s.blocks, step, 0)


def project_qkv(s, act, wqkv, vec, qkv, group):
    width = s.width
    n = width // 3
    cols = slice(group * n, group * n + n)
    for j in range(3):
        lin = dot_nn(act[...], wqkv[j, :, cols])
        if j != 1:
            row = 2 + j // 2
            lin = lin + vec[row : row + 1, cols]
        qkv[:, j * width + group * n : j * width + group * n + n] = lin.astype(BF)


def allowed_of(seg, segcol, i):
    col = segcol[i]
    full = jnp.concatenate([col] * (SEQ // 128), axis=1)
    return full == seg[i].astype(F32)


def lane_of(half):
    lanes = lax.broadcasted_iota(jnp.int32, (1, 128), 1)
    return (lanes < 64) if half == 0 else (lanes >= 64)


def pick_lanes(half, value):
    return jnp.where(lane_of(half), value, jnp.zeros_like(value))


def attend(s, group, qkv, seg, segcol, lse, att, attT):
    width, count = s.width, s.pairs // 3

    def step(i, _):
        rows = at(i, SEQ)
        ok = allowed_of(seg, segcol, i)
        items, raws, outs = [], {}, {}
        for p in range(group * count, group * count + count):
            q = qkv[rows, p * 128 : p * 128 + 128] * jnp.asarray(0.125, BF)
            k = qkv[rows, width + p * 128 : width + p * 128 + 128]
            vT = qkv[rows, 2 * width + p * 128 : 2 * width + p * 128 + 128].T
            items += [(p, q, k, vT, half) for half in (0, 1)]

        def raw(x):
            _p, q, k, _v, half = items[x]
            raws[x] = dot_nt(k, pick_lanes(half, q))

        def soft(x):
            p, _q, _k, _v, half = items[x]
            scores = jnp.where(ok, raws[x], LARGE_NEG)
            top = jnp.max(scores, 0, keepdims=True)
            expo = jnp.exp(scores - top)
            total = jnp.sum(expo, 0, keepdims=True)
            lse[2 * (i * s.pairs + p) + half] = top + jnp.log(total)
            outs[x] = expo.astype(BF), 1.0 / total

        def out(x):
            p, _q, _k, vT, half = items[x]
            expo, inverse = outs[x]
            outs[x] = dot_nn(vT[64 * half : 64 * half + 64], expo) * inverse
            if half == 1:
                both = jnp.concatenate([outs[x - 1], outs[x]], 0)
                attT[p * 128 : p * 128 + 128, rows] = both.astype(BF)
                att[rows, p * 128 : p * 128 + 128] = both.T.astype(BF)

        raw(0)
        for x in range(len(items)):
            if x + 1 < len(items):
                raw(x + 1)
            soft(x)
            if x >= 1:
                out(x - 1)
        out(len(items) - 1)
        return 0

    lax.fori_loop(0, s.seqs, step, 0)


def project_out(s, tok, vec, att, wout, x2, a2, a2T):
    def step(i, _):
        rows = at(i, ROWS)
        value = tok[rows, :].astype(F32) + (dot_nn(att[rows, :], wout[...]) + vec[4:5, :])
        x2[rows, :] = value
        xhat, _inv = normed(value)
        act = xhat * vec[5:6, :] + vec[6:7, :]
        a2[rows, :] = act.astype(BF)
        a2T[:, rows] = act.T.astype(BF)
        return 0

    lax.fori_loop(0, s.blocks, step, 0)


def mlp_tile(s, t, first, count, cot, ubias, a2, wup, wdown, mo, da2, hid, du, ugrad):
    starts = [f * s.share + t * s.piece for f in range(s.shards)]
    fresh = t == 0

    def step(i, sums):
        rows = at(first + i, ROWS)
        act, dy = a2[rows, :], cot[rows, :]
        more, back = 0.0, 0.0
        parts = []
        for f, start in enumerate(starts):
            up, down = wup[:, span(start, s.piece)], wdown[span(start, s.piece), :]
            u = dot_nn(act, up) + ubias[f, :, at(t, s.piece)]
            h, slope = gelu_pair(u)
            h = h.astype(BF)
            d = (dot_nt(dy, down) * slope).astype(BF)
            hid[rows, f * s.piece : (f + 1) * s.piece] = h
            du[rows, f * s.piece : (f + 1) * s.piece] = d
            more = more + dot_nn(h, down)
            back = back + dot_nt(d, up)
            parts.append(down_sum(d.astype(F32)))
        mo[rows, :] = jnp.where(fresh, 0.0, mo[rows, :]) + more
        da2[rows, :] = jnp.where(fresh, 0.0, da2[rows, :]) + back
        return tuple(a + b for a, b in zip(sums, parts))

    zero = jnp.zeros((1, s.piece), F32)
    sums = lax.fori_loop(0, count, step, (zero,) * s.shards)
    for f in range(s.shards):
        ugrad[f, :, at(t, s.piece)] = sums[f] + (ugrad[f, :, at(t, s.piece)] if first else 0.0)


def up_grad(s, a2T, du, unit):
    half = s.tile // 2

    def step(r, _):
        rows = at(r, WIDE)
        value = dot_nn(a2T[rows, :], du[...]).astype(BF)
        unit(0)[rows, :] = value[:, :half]
        unit(1)[rows, :] = value[:, half:]
        return 0

    lax.fori_loop(0, s.width // WIDE, step, 0)


def down_grad(s, hid, cot, unit):
    half = s.width // 2

    def step(r, _):
        rows = at(r, ROWS)
        value = dot_tn(hid[:, rows], cot[...]).astype(BF)
        unit(0)[rows, :] = value[:, :half]
        unit(1)[rows, :] = value[:, half:]
        return 0

    lax.fori_loop(0, s.tile // ROWS, step, 0)


def norm_two_back(s, cot, vec, x2, mo, da2, out, dbr, vgrad):
    def step(i, sums):
        rows = at(i, ROWS)
        value = x2[rows, :]
        dy = cot[rows, :].astype(F32)
        out[rows, :] = (value + (mo[rows, :] + vec[7:8, :])).astype(BF)
        xhat, inverse = normed(value)
        grad = da2[rows, :]
        total = dy + norm_back(grad, xhat, inverse, vec[5:6, :])
        x2[rows, :] = total
        low = total.astype(BF)
        dbr[rows, :] = low
        return tuple(
            a + down_sum(b) for a, b in zip(sums, (low.astype(F32), grad * xhat, grad, dy))
        )

    zero = jnp.zeros((1, s.width), F32)
    sums = lax.fori_loop(0, s.blocks, step, (zero,) * 4)
    for j, value in enumerate(sums):
        vgrad[4 + j : 5 + j, :] = value


def att_grad(s, dbr, wout, datt):
    def step(i, _):
        rows = at(i, ROWS)
        datt[rows, :] = dot_nt(dbr[rows, :], wout[...]).astype(BF)
        return 0

    lax.fori_loop(0, s.blocks, step, 0)


def out_grad(s, attT, dbr, unit):
    half = s.width // 2

    def step(r, _):
        rows = at(r, WIDE)
        value = dot_nn(attT[rows, :], dbr[...]).astype(BF)
        unit(0)[rows, :] = value[:, :half]
        unit(1)[rows, :] = value[:, half:]
        return 0

    lax.fori_loop(0, s.width // WIDE, step, 0)


def attend_back(s, p, qkv, seg, segcol, lse, datt, qsum, vsum):
    width = s.width
    qc, kc, vc = [slice(j * width + p * 128, j * width + p * 128 + 128) for j in range(3)]

    def step(i, sums):
        rows = at(i, SEQ)
        q = qkv[rows, qc] * jnp.asarray(0.125, BF)
        k, v, g = qkv[rows, kc], qkv[rows, vc], datt[rows, qc]
        kT = k.T
        ok = allowed_of(seg, segcol, i)
        dqs, dks, dvs = [], [], []
        for half in (0, 1):
            scores = jnp.where(ok, dot_nt(k, pick_lanes(half, q)), LARGE_NEG)
            prob = jnp.exp(scores - lse[2 * (i * s.pairs + p) + half])
            dprob = dot_nt(v, pick_lanes(half, g))
            weighted = jnp.sum(prob * dprob, 0, keepdims=True)
            dscore = (prob * (dprob - weighted)).astype(BF)
            dvs.append(dot_nn(prob.astype(BF), g))
            dks.append(dot_nn(dscore, q))
            dqs.append(dot_nn(kT[64 * half : 64 * half + 64], dscore))
        mask = lane_of(0)
        dq = (jnp.concatenate(dqs, 0) * 0.125).T.astype(BF)
        dk = jnp.where(mask, dks[0], dks[1]).astype(BF)
        dv = jnp.where(mask, dvs[0], dvs[1]).astype(BF)
        qkv[rows, qc] = dq
        qkv[rows, kc] = dk
        qkv[rows, vc] = dv
        return sums[0] + down_sum(dq.astype(F32)), sums[1] + down_sum(dv.astype(F32))

    zero = jnp.zeros((1, 128), F32)
    qs, vs = lax.fori_loop(0, s.seqs, step, (zero, zero))
    qsum[:, p * 128 : p * 128 + 128] = qs
    vsum[:, p * 128 : p * 128 + 128] = vs


def qkv_grad(s, a1T, dqkv, p, part):
    width = s.width

    def step(r, _):
        rows = at(r, WIDE)
        for j in range(3):
            cols = slice(j * width + p * 128, j * width + p * 128 + 128)
            part(j)[rows, :] = dot_nn(a1T[rows, :], dqkv[:, cols]).astype(BF)
        return 0

    lax.fori_loop(0, width // WIDE, step, 0)


def norm_one_back(s, tok, vec, dqkv, wqkv, dx2, ingrad, vgrad):
    def step(i, sums):
        rows = at(i, ROWS)
        width = s.width
        grad = sum(dot_nt(dqkv[rows, j * width : (j + 1) * width], wqkv[j]) for j in range(3))
        xhat, inverse = normed(tok[rows, :].astype(F32))
        ingrad[rows, :] = (dx2[rows, :] + norm_back(grad, xhat, inverse, vec[0:1, :])).astype(BF)
        return sums[0] + down_sum(grad * xhat), sums[1] + down_sum(grad)

    zero = jnp.zeros((1, s.width), F32)
    sums = lax.fori_loop(0, s.blocks, step, (zero,) * 2)
    vgrad[0:1, :] = sums[0]
    vgrad[1:2, :] = sums[1]


def block_kernel(
    s, tok_h, cot_h, seg, vec, ubias, wqkv_h, wout_h, wup_h, wdown_h,
    out_h, ingrad_h, gqkv_h, gout_h, gup_h, gdown_h, vgrad, ugrad,
    tok, cot, act, actT, attT, qkv, x2, mo, da2, hid, du,
    wqkv, wout, wup, wdown, segcol, lse, narrow, wide, thin, sems,
):
    rows, width = s.rows, s.width
    loads = [
        pltpu.make_async_copy(a, b, sems.at[i])
        for i, (a, b) in enumerate(
            [(tok_h, tok), (wout_h, wout), (wup_h, wup), (wdown_h, wdown)]
            + [(wqkv_h.at[:, j * width : (j + 1) * width], wqkv.at[j]) for j in range(3)]
        )
    ]
    for load in loads:
        load.start()
    setup_masks(s, seg, segcol)
    vgrad[...] = jnp.zeros_like(vgrad)
    loads[0].wait()
    norm_one(s, tok, vec, act)
    for load in loads[4:]:
        load.wait()
    for group in range(3):
        project_qkv(s, act, wqkv, vec, qkv, group)
        attend(s, group, qkv, seg, segcol, lse, cot, attT)
    loads[1].wait()
    project_out(s, tok, vec, cot, wout, x2, act, actT)
    load = pltpu.make_async_copy(cot_h, cot, sems.at[7])
    load.start()
    load.wait()
    loads[2].wait()
    loads[3].wait()

    def dump(src, dst):
        copy = pltpu.make_async_copy(src, dst, sems.at[8])
        copy.start()
        copy.wait()

    def tile_step(t, _):
        mlp_tile(s, t, 0, s.blocks, cot, ubias, act, wup, wdown, mo, da2, hid, du, ugrad)
        up_grad(s, actT, du, lambda h: narrow.at[h])
        dump(narrow, gup_h.at[t])
        down_grad(s, hid, cot, lambda h: wide.at[h, pl.ds(0, s.tile)])
        dump(wide.at[:, pl.ds(0, s.tile)], gdown_h.at[t])
        return 0

    lax.fori_loop(0, s.tiles, tile_step, 0)
    datt, dbr, stage = (wdown.at[j * rows : (j + 1) * rows] for j in range(3))
    a1T = wup.at[:, 0:rows]
    norm_two_back(s, cot, vec, x2, mo, da2, stage, dbr, vgrad)
    dump(stage, out_h)
    att_grad(s, dbr, wout, datt)
    out_grad(s, attT, dbr, lambda h: wide.at[h, pl.ds(0, width)])
    dump(wide.at[:, pl.ds(0, width)], gout_h)
    norm_one_flipped(s, tok, vec, a1T)
    for g in range(s.pairs // 2):
        for h in range(2):
            p = 2 * g + h
            attend_back(s, p, qkv, seg, segcol, lse, datt, vgrad.at[2:3, :], vgrad.at[3:4, :])
            qkv_grad(s, a1T, qkv, p, lambda j: thin.at[h, j])
        dump(thin, gqkv_h.at[g])
    norm_one_back(s, tok, vec, qkv, wqkv, x2, stage, vgrad)
    dump(stage, ingrad_h)


MESH = pl.DeviceIdType.MESH
LINK_RATE = 90e3
CORE_RATE = 400e3
LATENCY = 4.5


class Timeline:
    def __init__(self):
        self.now, self.free, self.jobs = 0.0, {}, []

    def begin(self, job):
        self.jobs.append(job)
        self.launch(job, job.first)

    def launch(self, job, made):
        link, cost = made
        start = max(self.now, self.free.get(link, 0.0))
        self.free[link] = start + cost
        job.ready = start + cost + LATENCY

    def advance(self, job):
        self.now = max(self.now, job.ready)
        made = job.steps[job.done]()
        job.done += 1
        if made is None:
            self.jobs.remove(job)
        else:
            self.launch(job, made)

    def due(self, job):
        link = job.links[job.done]
        return max(job.ready, self.free.get(link, 0.0) - QUEUE) if link in ("x", "y", "z") else job.ready

    def next(self):
        return min(self.jobs, key=self.due)

    def tick(self, cost):
        end = self.now + cost
        while self.jobs:
            job = self.next()
            if self.due(job) > end:
                break
            self.now = max(self.now, min(self.due(job), end))
            self.advance(job)
        self.now = max(self.now, end)

    def need(self, job, steps=None):
        while job in self.jobs and (steps is None or job.done < steps):
            self.advance(self.next())

    def drain(self):
        while self.jobs:
            self.advance(self.next())


class Job:
    def __init__(self, first, steps, links):
        self.first, self.steps, self.links, self.done, self.ready = first, steps, links, 0, 0.0


def cut(ref, start, count):
    rows = pl.ds(pl.multiple_of(start, 16), count)
    return ref.at[rows, :] if len(ref.shape) == 2 else ref.at[:, rows, :]


def size_of(ref):
    total = 2
    for n in ref.shape:
        total *= n
    return total


class Place:
    def __init__(self, far):
        d, self.f = lax.axis_index("dp"), lax.axis_index("fsdp")
        self.d, self.far = d, far
        self.c, self.b, self.a = d % 2, (d // 2) % 2, d // 4
        self.core = {"dp": d + 1 - 2 * self.c, "fsdp": self.f}
        self.near = {"dp": d + 2 - 4 * self.b, "fsdp": self.f}
        self.across = {"dp": d, "fsdp": 1 - self.f}

    def other(self, k):
        return {"dp": lax.rem(self.a + k, self.far) * 4 + self.b * 2 + self.c, "fsdp": self.f}

    def spot(self, k):
        place = lax.rem(self.b * self.far + self.a + k, 2 * self.far)
        return {"dp": place % self.far * 4 + place // self.far * 2 + self.c, "fsdp": self.f}, place

    def bit(self, level):
        return (self.a // 2**level) % 2

    def flipped(self, level):
        step = (1 - 2 * self.bit(level)) * 2**level
        return {"dp": self.d + 4 * step, "fsdp": self.f}


def remote(src, dst, send, recv, device):
    return pltpu.make_async_remote_copy(
        src_ref=src, dst_ref=dst, send_sem=send, recv_sem=recv, device_id=device, device_id_type=MESH
    )


def gather_job(s, me, j, view, sems):
    send, recv = sems
    size = s.width // 2 // 4
    quarter = (me.c * 2 + me.b) * size
    first = remote(view(j, me.f, quarter, size), view(j, me.f, quarter, size), send.at[j, 0], recv.at[j, 0], me.across)
    g = 1 - me.f
    second = remote(view(j, g, quarter, size), view(j, g, quarter, size), send.at[j, 1], recv.at[j, 1], me.near)
    half = me.c * 2 * size
    third = remote(view(j, g, half, 2 * size), view(j, g, half, 2 * size), send.at[j, 2], recv.at[j, 2], me.core)
    cost = 2 * 2 * size * s.width / LINK_RATE

    def step_one():
        first.wait_recv()
        second.start()
        return ("y", cost)

    def step_two():
        second.wait_recv()
        third.start()
        return ("core", 2 * 2 * size * s.width / CORE_RATE)

    def step_three():
        third.wait_recv()
        return None

    first.start()
    return Job(("x", cost), [step_one, step_two, step_three], ["y", "core", ""]), [first, second, third]


class Unit:
    def __init__(self, index, own, other, into, out, direct=False):
        self.index, self.own, self.other, self.into, self.out, self.direct = index, own, other, into, out, direct
        self.rows = own.shape[-2]


def unit_job(s, me, unit, send, recv, give, take):
    u, own, far = unit.index, unit.own, me.far
    half, quarter = unit.rows // 2, unit.rows // 4
    piece = quarter // far
    r1, r2, r3 = unit.into
    r4 = cut(r3, quarter, r3.shape[-2] - quarter)
    r3 = cut(r3, 0, quarter)
    size = size_of(own)
    levels = far.bit_length() - 1
    mine, mine_b = me.f * half, me.f * half + me.b * quarter
    one = remote(unit.other, r1, send.at[u, 0], recv.at[u, 0], me.core)
    two = remote(cut(own, (1 - me.f) * half, half), r2, send.at[u, 1], recv.at[u, 1], me.across)
    three = remote(cut(own, mine + (1 - me.b) * quarter, quarter), r3, send.at[u, 2], recv.at[u, 2], me.near)
    four, kept, offset, used = [], [], 0, 0
    for level in range(levels):
        part, bit = quarter >> (level + 1), me.bit(level)
        arrived = cut(r4, used, part)
        theirs = cut(own, mine_b + offset + (1 - bit) * part, part)
        four.append(remote(theirs, arrived, send.at[u, 3 + level], recv.at[u, 3 + level], me.flipped(level)))
        offset = offset + bit * part
        kept.append((cut(own, mine_b + offset, part), arrived))
        used += part
    final = cut(own, mine_b + offset, piece)
    target = unit.out(me.b * quarter + offset, piece)
    base = 2 + levels
    five = [remote(final, target, send.at[u, base + k], recv.at[u, base + k], me.other(k)) for k in range(1, far)]
    n = base + far
    keep = pltpu.make_async_copy(final, target, send.at[u, n + 2])
    block = unit.out(me.b * quarter, quarter)
    six = remote(block, block, send.at[u, n], recv.at[u, n], me.near)
    all_rows = unit.out(0, half)
    seven = remote(all_rows, all_rows, send.at[u, n + 1], recv.at[u, n + 1], me.core)

    def add_into(part, arrived):
        part[...] = part[...] + arrived[...]

    def step_one():
        one.wait_recv()
        add_into(own, r1)
        if give is not None:
            pl.semaphore_signal(give, inc=1, device_id=me.core, device_id_type=MESH)
        two.start()
        return ("x", size / LINK_RATE)

    def step_two():
        two.wait_recv()
        add_into(cut(own, mine, half), r2)
        three.start()
        return ("y", size / 2 / LINK_RATE)

    def step_three():
        three.wait_recv()
        add_into(cut(own, mine_b, quarter), r3)
        four[0].start()
        return ("z", size / 4 / LINK_RATE)

    def fold(level):
        def step():
            four[level].wait_recv()
            add_into(*kept[level])
            if level + 1 < levels:
                four[level + 1].start()
                return ("z", size / 4 / LINK_RATE)
            keep.start()
            for copy in five:
                copy.start()
            return ("z", size / 2 / LINK_RATE)

        return step

    def step_five():
        keep.wait()
        for copy in five:
            copy.wait_recv()
        six.start()
        return ("y", size / 2 / LINK_RATE)

    def step_six():
        six.wait_recv()
        seven.start()
        return ("core", size / 2 / CORE_RATE)

    def step_seven():
        seven.wait_recv()
        return None

    def step_seven_of(copy):
        def step():
            copy().wait_recv()
            return None

        return step

    def direct_two():
        two.wait_recv()
        add_into(cut(own, mine, half), r2)
        for copy in parts:
            copy.start()
        return ("z", size / LINK_RATE)

    def direct_three():
        value = final[...].astype(F32)
        for k, copy in enumerate(parts):
            copy.wait_recv()
            value = value + cut(unit.into[2], k * piece, piece)[...].astype(F32)
        final[...] = value.astype(BF)
        keep.start()
        for copy in five:
            copy.start()
        return ("z", size / LINK_RATE)

    def direct_four():
        keep.wait()
        for copy in five:
            copy.wait_recv()
        seven.start()
        return ("core", size / 2 / CORE_RATE)

    if take is not None:
        pl.semaphore_wait(take, 1)
    one.start()
    if unit.direct:
        here = me.b * far + me.a
        final = cut(own, mine + here * piece, piece)
        target = unit.out(here * piece, piece)
        parts, five = [], []
        for k in range(1, 2 * far):
            device, place = me.spot(k)
            slot = cut(unit.into[2], (k - 1) * piece, piece)
            parts.append(remote(cut(own, mine + place * piece, piece), slot, send.at[u, 1 + k], recv.at[u, 1 + k], device))
            five.append(remote(final, target, send.at[u, 2 * far + k], recv.at[u, 2 * far + k], device))
        n = 4 * far - 1
        keep = pltpu.make_async_copy(final, target, send.at[u, n + 2])
        seven = remote(all_rows, all_rows, send.at[u, n + 1], recv.at[u, n + 1], me.core)
        steps = [step_one, direct_two, direct_three, direct_four, step_seven_of(lambda: seven)]
        return Job(("core", size / CORE_RATE), steps, ["x", "z", "z", "core", ""]), one, [two, *parts, *five, seven]
    folds = [fold(level) for level in range(levels)]
    steps = [step_one, step_two, step_three, *folds, step_five, step_six, step_seven]
    links = ["x", "y"] + ["z"] * (levels + 1) + ["y", "core", ""]
    return Job(("core", size / CORE_RATE), steps, links), one, [two, three, *four, *five, six, seven]


def vector_job(me, slots, sends, recvs, finish):
    core_s, x_s, near_s, far_s = slots
    stops = ((core_s, me.c, me.core), (x_s, me.f, me.across), (near_s, me.b, me.near))
    hops = [remote(s.at[i], s.at[i], sends.at[n], recvs.at[n], device) for n, (s, i, device) in enumerate(stops)]
    last = [
        remote(far_s.at[me.a], far_s.at[me.a], sends.at[2 + k], recvs.at[2 + k], me.other(k)) for k in range(1, me.far)
    ]
    cost = ("small", 0.4)

    def hop(n):
        def step():
            hops[n].wait()
            total = stops[n][0][0] + stops[n][0][1]
            if n < 2:
                stops[n + 1][0][stops[n + 1][1]] = total
                hops[n + 1].start()
            else:
                far_s[me.a] = total
                for copy in last:
                    copy.start()
            return cost

        return step

    def end():
        for copy in last:
            copy.wait()
        total = far_s[0]
        for k in range(1, me.far):
            total = total + far_s[k]
        far_s[0] = total
        finish()
        return None

    hops[0].start()
    return Job(cost, [hop(0), hop(1), hop(2), end], ["small"] * 3 + [""])


def linked_kernel(
    s, far, tok_h, cot_h, seg, g1_h, s1_h, qb_h, vb_h, ob_h, g2_h, s2_h, db_h, ub_h, wqkv_h, wout_h, wup_h, wdown_h,
    out_h, ingrad_h, gqkv_h, gout_h, gup_h, gdown_h, vout,
    tok, cot, act, actT, attT, qkv, x2, mo, da2, hid, du,
    wqkv, wout, wup, wdown, segcol, lse, raw, raw_up, packed, vec, ubias, ugrad, core_s, x_s, near_s, far_s,
    own_up, own_down, oth_up, oth_down,
    r1_up, r1_down, r1_out, r1_qkv, r2_up, r2_down, r2_out, r2_qkv,
    r3_up, r3_down, r3_out, r3_qkv,
    loads, wsend, wrecv, usend, urecv, vsend, vrecv, credit,
):
    rows, width = s.rows, s.width
    me = Place(far)
    line = Timeline()
    shard, third = width // 2, width // 3
    count = s.hidden // width

    barrier = pltpu.get_barrier_semaphore()
    partners = [me.core, me.across] + [me.spot(k)[0] for k in range(1, 2 * far)]
    for device in partners:
        pl.semaphore_signal(barrier, inc=1, device_id=device, device_id_type=MESH)

    names = [("qkv", 0), ("qkv", 1), ("qkv", 2), ("out", 0)]
    order = [i for k in range(count // 2) for i in (k, k + count // 2)]
    for n in range(0, count, 2):
        names += [("up", order[n]), ("up", order[n + 1]), ("down", n), ("down", n + 1)]

    def view(j, f, start, size):
        kind, i = names[j]
        if kind == "down":
            return wdown.at[pl.ds(pl.multiple_of(f * s.share + i * shard + start, 16), size), :]
        part = pl.ds(pl.multiple_of(f * shard + start, 16), size)
        if kind == "out":
            return wout.at[part, :]
        if kind == "qkv":
            return wqkv.at[:, part, i * third : (i + 1) * third]
        return wup.at[part, i * width : (i + 1) * width]

    def masters(j):
        kind, i = names[j]
        if kind == "down":
            return [(wdown_h.at[i * shard : (i + 1) * shard, :], stages[j % 4])]
        if kind == "out":
            return [(wout_h.at[...], stages[j % 4])]
        if kind == "up":
            return [(wup_h.at[:, i * width : (i + 1) * width], stages[j % 4])]
        starts = [n * width + i * third for n in range(3)]
        return [
            (wqkv_h.at[:, start : start + third], stages[j % 4].at[:, n * third : (n + 1) * third])
            for n, start in enumerate(starts)
        ]

    stages = [mo.at[0:shard], mo.at[shard : 2 * shard], da2.at[0:shard], da2.at[shard : 2 * shard]]
    copies = [
        [pltpu.make_async_copy(a, b, loads.at[j % 4, n]) for n, (a, b) in enumerate(masters(j))]
        for j in range(len(names))
    ]
    for j in range(4):
        for copy in copies[j]:
            copy.start()
    load_tok = pltpu.make_async_copy(tok_h, tok, loads.at[4, 0])
    load_tok.start()
    per = shard // 128
    small = [(a, raw.at[n]) for n, a in enumerate((g1_h, s1_h, qb_h, vb_h, ob_h, g2_h, s2_h, db_h))] + [(ub_h, raw_up)]
    small = [pltpu.make_async_copy(a, b, loads.at[6 + n // 3, n % 3]) for n, (a, b) in enumerate(small)]
    for copy in small:
        copy.start()
    share_small = remote(packed.at[me.f], packed.at[me.f], vsend.at[2 + far], vrecv.at[2 + far], me.across)
    pl.semaphore_wait(barrier, len(partners))
    sent, moved, jobs = [share_small], [], []
    for j in range(len(names)):
        for copy in copies[j]:
            copy.wait()
        if names[j][0] == "qkv":
            for n in range(3):
                view(j, me.f, 0, shard)[n] = stages[j % 4][:, n * third : (n + 1) * third].astype(BF)
        else:
            view(j, me.f, 0, shard)[...] = stages[j % 4][...].astype(BF)
        if j + 4 < len(names):
            for copy in copies[j + 4]:
                copy.start()
        if j == 2:
            for copy in small:
                copy.wait()
            packed[me.f] = jnp.zeros((packed.shape[1], 128), F32)
            for n in range(8):
                packed[me.f, n * per : n * per + per, :] = raw[n].astype(BF).astype(F32)
            packed[me.f, 8 * per : 8 * per + s.share // 128, :] = raw_up[...].astype(BF).astype(F32)
            share_small.start()
        job, made = gather_job(s, me, j, view, (wsend, wrecv))
        line.begin(job)
        line.now += 0.5
        jobs.append(job)
        (moved if names[j][0] in ("up", "down") else sent).extend(made)
    setup_masks(s, seg, segcol)
    core_s[...] = jnp.zeros_like(core_s)
    share_small.wait_recv()
    for f in range(2):
        for i in range(8 * per):
            r, col = i // per, f * shard + i % per * 128
            vec[r : r + 1, col : col + 128] = packed[f, i : i + 1, :]
        for i in range(s.share // 128):
            ubias[f, :, i * 128 : (i + 1) * 128] = packed[f, 8 * per + i : 8 * per + i + 1, :]
    load_tok.wait()
    norm_one(s, tok, vec, act)
    line.tick(3.0)
    for group in range(3):
        line.need(jobs[group])
        project_qkv(s, act, wqkv, vec, qkv, group)
        line.tick(1.6)
        attend(s, group, qkv, seg, segcol, lse, cot, attT)
        line.tick(3.8)
    line.need(jobs[3])
    project_out(s, tok, vec, cot, wout, x2, act, actT)
    load_cot = pltpu.make_async_copy(cot_h, cot, loads.at[5, 0])
    load_cot.start()
    line.tick(2.5)

    c = me.c
    units, firsts, later = [], [], []
    pending = {}

    def start_unit(unit, kind=None, slot=0, reuse=False, again=False):
        give = credit.at[kind * 2 + slot] if again else None
        take = credit.at[kind * 2 + slot] if reuse else None
        job, one, made = unit_job(s, me, unit, usend, urecv, give, take)
        line.begin(job)
        later.extend(made)
        return job, one

    vgrad = core_s.at[c]
    load_cot.wait()
    for t in range(s.tiles):
        for j, (kind, i) in enumerate(names):
            if kind == "up":
                lo, hi = i * width, (i + 1) * width
                used = any(f * s.share + t * s.piece < hi and f * s.share + (t + 1) * s.piece > lo for f in range(2))
            elif kind == "down":
                used = t * s.piece < (i + 1) * shard and (t + 1) * s.piece > i * shard
            else:
                used = False
            if used:
                line.need(jobs[j])
        slot = t % 2
        mlp_tile(s, t, 0, s.blocks, cot, ubias, act, wup, wdown, mo, da2, hid, du, ugrad)
        line.tick(4.2)
        if t >= 2:
            job, one = pending["up", t - 2]
            line.need(job, 1)
            one.wait_send()
        up_grad_linked(s, actT, du, c, own_up.at[t], oth_up.at[slot])
        unit = Unit(
            2 * t, own_up.at[t], oth_up.at[slot],
            (r1_up.at[slot], r2_up.at[t], r3_up.at[t]),
            lambda start, n, t=t: gup_h.at[pl.ds(pl.multiple_of(start, 16), n), span(c * s.share + t * s.piece, s.piece)],
        )
        pending["up", t] = start_unit(unit, 0, slot, t >= 2, t + 2 < s.tiles)
        line.tick(1.5)
        if t >= 2:
            job, one = pending["down", t - 2]
            line.need(job, 1)
            one.wait_send()
        down_grad_linked(s, hid, cot, c, own_down.at[t], oth_down.at[slot])
        unit = Unit(
            2 * t + 1, own_down.at[t], oth_down.at[slot],
            (r1_down.at[slot], r2_down.at[t], r3_down.at[t]),
            lambda start, n, t=t: gdown_h.at[
                pl.ds(pl.multiple_of(t * s.piece + start, 16), n), span(c * shard, shard)
            ],
        )
        pending["down", t] = start_unit(unit, 1, slot, t >= 2, t + 2 < s.tiles)
        line.tick(1.3)
    for job in jobs:
        line.need(job)
    for copy in moved:
        copy.wait_send()
    datt, dbr, stage = (wdown.at[j * rows : (j + 1) * rows] for j in range(3))
    a1T = wup.at[:, 0:rows]
    own_out, oth_out = (wup.at[:, rows + j * shard : rows + (j + 1) * shard] for j in range(2))
    own_qkv = [wup.at[:, n : n + 384] for n in range(rows + width, s.hidden - 383, 384)]
    oth_qkv = [actT.at[:, n : n + 384] for n in range(0, rows - 383, 384)]
    norm_two_back(s, cot, vec, x2, mo, da2, stage, dbr, vgrad)
    save_out = pltpu.make_async_copy(stage, out_h, loads.at[5, 0])
    save_out.start()
    line.tick(2.5)
    out_grad_linked(s, attT, dbr, c, own_out, oth_out)
    unit = Unit(
        2 * s.tiles, own_out, oth_out,
        (r1_out, r2_out, r3_out),
        lambda start, n: gout_h.at[pl.ds(pl.multiple_of(start, 16), n), span(c * shard, shard)],
    )
    pending["out"] = start_unit(unit)
    line.tick(1.3)
    att_grad(s, dbr, wout, datt)
    line.tick(2.2)
    norm_one_flipped(s, tok, vec, a1T)
    line.tick(1.7)
    for g in range(s.pairs // 2):
        for h in range(2):
            attend_back(s, 2 * g + h, qkv, seg, segcol, lse, datt, vgrad.at[2:3, :], vgrad.at[3:4, :])
            line.tick(3.8)
        own, other = own_qkv[g], oth_qkv[g % len(oth_qkv)]
        if g >= len(oth_qkv):
            pending["qkv", g - len(oth_qkv)][1].wait_send()
        for j in range(3):
            cols = slice(j * 128, j * 128 + 128)
            qkv_grad_linked(s, a1T, qkv, g, j, c, own.at[:, cols], other.at[:, cols])
        unit = Unit(
            2 * s.tiles + 1 + g, own, other, (r1_qkv.at[g], r2_qkv.at[g], r3_qkv.at[g]),
            lambda start, size, g=g: gqkv_h.at[
                pl.ds(pl.multiple_of(start, 16), size), span((2 * g + c) * 384, 384)
            ],
        )
        pending["qkv", g] = start_unit(unit)
        line.tick(1.8)
    save_out.wait()
    norm_one_back(s, tok, vec, qkv, wqkv, x2, stage, vgrad)
    line.tick(5.0)
    save_in = pltpu.make_async_copy(stage, ingrad_h, loads.at[4, 0])
    save_in.start()
    part = math.gcd(s.share, width)
    for i in range(s.hidden // part):
        start = i * part
        f, off = start // s.share, start % s.share
        r, col = 8 + start // width, start % width
        vgrad[r : r + 1, col : col + part] = ugrad[f, :, off : off + part]

    def finish():
        vout[...] = jnp.zeros_like(vout)
        for f in range(2):

            @pl.when(me.f == f)
            def _(f=f):
                for i in range(8 * per):
                    r, col = i // per, f * shard + i % per * 128
                    vout[i : i + 1, :] = far_s[0, r : r + 1, col : col + 128]
                for i in range(s.share // 128):
                    flat = f * s.share + i * 128
                    r, col = 8 + flat // width, flat % width
                    vout[8 * per + i : 8 * per + i + 1, :] = far_s[0, r : r + 1, col : col + 128]

    line.begin(vector_job(me, (core_s, x_s, near_s, far_s), vsend, vrecv, finish))
    line.drain()
    save_in.wait()
    for key, (job, one) in pending.items():
        if key == "out" or key[1] + 2 >= (s.pairs // 2 if key[0] == "qkv" else s.tiles):
            one.wait_send()
    for copy in later + sent:
        copy.wait_send()


def split_store(c, value, own, other, rows):
    half = value.shape[-1] // 2
    left, right = value[:, :half].astype(BF), value[:, half:].astype(BF)
    own[rows, :] = jnp.where(c == 0, left, right)
    other[rows, :] = jnp.where(c == 0, right, left)


def up_grad_linked(s, a2T, du, c, own, other):
    def step(r, _):
        rows = at(r, WIDE)
        split_store(c, dot_nn(a2T[rows, :], du[...]), own, other, rows)
        return 0

    lax.fori_loop(0, s.width // WIDE, step, 0)


def down_grad_linked(s, hid, cot, c, own, other):
    def step(r, _):
        rows = at(r, ROWS)
        split_store(c, dot_tn(hid[:, rows], cot[...]), own, other, rows)
        return 0

    lax.fori_loop(0, s.tile // ROWS, step, 0)


def out_grad_linked(s, attT, dbr, c, own, other):
    def step(r, _):
        rows = at(r, WIDE)
        split_store(c, dot_nn(attT[rows, :], dbr[...]), own, other, rows)
        return 0

    lax.fori_loop(0, s.width // WIDE, step, 0)


def qkv_grad_linked(s, a1T, dqkv, g, j, c, own, other):
    start = j * s.width + 2 * g * 128
    split_store(c, dot_nn(a1T[...], dqkv[:, start : start + 256]), own, other, slice(None))


def linked_body(far, tokens, segment_ids, cotangent, *params):
    (
        norm1_gain, norm1_shift, qkv_weight, query_bias, value_bias, out_weight, out_bias, norm2_gain, norm2_shift,
        up_weight, up_bias, down_weight, down_bias,
    ) = params
    rows, width = tokens.shape
    hidden = up_weight.shape[1]
    s = Sizes(rows, width, hidden, 2)
    shard, tiles, tile, groups = width // 2, s.tiles, s.tile, s.pairs // 2
    vectors = [norm1_gain, norm1_shift, query_bias, value_bias, out_bias, norm2_gain, norm2_shift, down_bias]
    vectors = [v.reshape(-1, 128) for v in vectors + [up_bias]]
    lines_all = -(-sum(v.shape[0] for v in vectors) // 8) * 8
    seg = segment_ids.reshape(s.seqs, 1, SEQ)
    whole = pl.BlockSpec(memory_space=pltpu.VMEM)
    away = pl.BlockSpec(memory_space=pl.ANY)

    def vm(*shape, kind=BF):
        return pltpu.VMEM(shape, kind)

    n_units, n_blocks = 2 * tiles + 1 + groups, 4 + 2 * (hidden // width)
    up, down, out, qk = (width, tile // 2), (tile, shard), (width, shard), (width, 384)

    def part(shape, by):
        return shape[:-2] + (shape[-2] // by, shape[-1])

    def rest(shape):
        return shape[:-2] + (shape[-2] // (4 * far) * (2 * far - 1), shape[-1])

    slots = min(2, tiles)
    scratch = [
        vm(rows, width), vm(rows, width), vm(rows, width), vm(width, rows), vm(width, rows), vm(rows, 3 * width),
        vm(rows, width, kind=F32), vm(rows, width, kind=F32), vm(rows, width, kind=F32), vm(rows, tile), vm(rows, tile),
        vm(3, width, width), vm(width, width), vm(width, hidden), vm(hidden, width),
        vm(s.seqs, SEQ, 128, kind=F32), vm(s.seqs * HEADS, 1, SEQ, kind=F32),
        vm(8, shard // 128, 128, kind=F32), vm(s.share // 128, 128, kind=F32),
        vm(2, lines_all, 128, kind=F32), vm(8, width, kind=F32), vm(2, 1, s.share, kind=F32), vm(2, 1, s.share, kind=F32),
        vm(2, 16, width, kind=F32), vm(2, 16, width, kind=F32), vm(2, 16, width, kind=F32), vm(far, 16, width, kind=F32),
        vm(tiles, *up), vm(tiles, *down), vm(slots, *up), vm(slots, *down),
        vm(slots, *up), vm(slots, *down), vm(*out), vm(groups, *qk),
        vm(tiles, *part(up, 2)), vm(tiles, *part(down, 2)), vm(*part(out, 2)), vm(groups, *part(qk, 2)),
        vm(tiles, *rest(up)), vm(tiles, *rest(down)), vm(*rest(out)), vm(groups, *rest(qk)),
        pltpu.SemaphoreType.DMA((9, 3)),
        pltpu.SemaphoreType.DMA((n_blocks, 3)),
        pltpu.SemaphoreType.DMA((n_blocks, 3)),
        pltpu.SemaphoreType.DMA((n_units, 4 * far + 2)),
        pltpu.SemaphoreType.DMA((n_units, 4 * far + 2)),
        pltpu.SemaphoreType.DMA((far + 3,)),
        pltpu.SemaphoreType.DMA((far + 3,)),
        pltpu.SemaphoreType.REGULAR((4,)),
    ]
    output, input_grad, gqkv, gout, gup, gdown, v = pl.pallas_call(
        functools.partial(linked_kernel, s, far),
        out_shape=(
            jax.ShapeDtypeStruct((rows, width), BF),
            jax.ShapeDtypeStruct((rows, width), BF),
            jax.ShapeDtypeStruct((shard, 3 * width), BF),
            jax.ShapeDtypeStruct((shard, width), BF),
            jax.ShapeDtypeStruct((shard, hidden), BF),
            jax.ShapeDtypeStruct((hidden // 2, width), BF),
            jax.ShapeDtypeStruct((lines_all, 128), F32),
        ),
        in_specs=[away, away, whole] + [away] * 13,
        out_specs=(away,) * 6 + (whole,),
        scratch_shapes=scratch,
        compiler_params=pltpu.CompilerParams(
            vmem_limit_bytes=61 << 20, collective_id=0, has_side_effects=True
        ),
    )(tokens, cotangent, seg, *vectors, qkv_weight, out_weight, up_weight, down_weight)
    grads = (gqkv, gout, gup, gdown)
    lines = [shard // 128] * 8 + [s.share // 128]
    final = pl.pallas_call(
        functools.partial(finish_kernel, lines),
        out_shape=(
            [jax.ShapeDtypeStruct((rows, width), BF)] * 2
            + [jax.ShapeDtypeStruct(g.shape, F32) for g in grads]
            + [jax.ShapeDtypeStruct((n, 128), F32) for n in lines]
        ),
        in_specs=[away] * 6 + [whole],
        out_specs=[away] * 6 + [whole] * len(lines),
        scratch_shapes=(
            [pltpu.VMEM(g.shape, BF) for g in grads]
            + [pltpu.VMEM(g.shape, F32) for g in grads]
            + [pltpu.VMEM((2, rows, width), BF)]
            + [pltpu.SemaphoreType.DMA((2,)), pltpu.SemaphoreType.DMA((4, CHUNKS)), pltpu.SemaphoreType.DMA((4, CHUNKS))]
        ),
        compiler_params=pltpu.CompilerParams(vmem_limit_bytes=61 << 20),
    )(output, input_grad, *grads, v)
    output, input_grad, gqkv, gout, gup, gdown = final[:6]
    v = [value.reshape(-1) for value in final[6:]]
    return (
        output, input_grad, v[0], v[1], gqkv, v[2], v[3], gout, v[4], v[5], v[6], gup, v[8], gdown, v[7],
    )


CHUNKS = 8


def finish_kernel(lines, *refs):
    ins, v, outs, small = refs[:6], refs[6], refs[7:13], refs[13 : 13 + len(lines)]
    held, wide = refs[13 + len(lines) : 17 + len(lines)], refs[17 + len(lines) : 21 + len(lines)]
    passing, whole, loads, stores = refs[21 + len(lines) :]
    lift = [pltpu.make_async_copy(ins[n], passing.at[n], whole.at[n]) for n in range(2)]
    drop = [pltpu.make_async_copy(passing.at[n], outs[n], whole.at[n]) for n in range(2)]
    chunks = []
    for n in range(4):
        rows = held[n].shape[0] // CHUNKS
        for i in range(CHUNKS):
            part = pl.ds(i * rows, rows)
            chunks.append((n, i, part))
    into = [pltpu.make_async_copy(ins[2 + n].at[part], held[n].at[part], loads.at[n, i]) for n, i, part in chunks]
    back = [pltpu.make_async_copy(wide[n].at[part], outs[2 + n].at[part], stores.at[n, i]) for n, i, part in chunks]
    for copy in lift + into:
        copy.start()
    start = 0
    for ref, count in zip(small, lines):
        ref[...] = v[start : start + count, :]
        start += count
    for n in range(2):
        lift[n].wait()
        drop[n].start()
    for (n, _i, part), load, store in zip(chunks, into, back):
        load.wait()
        if n:
            wide[n][part, :] = held[n][part, :].astype(F32)
        else:
            for p in range(HEADS // 2):
                for j in range(3):
                    value = held[n][part, p * 384 + j * 128 : p * 384 + j * 128 + 128]
                    start = (j * (HEADS // 2) + p) * 128
                    wide[n][part, start : start + 128] = value.astype(F32)
        store.start()
    for copy in back + drop:
        copy.wait()


def body(
    tokens, segment_ids, cotangent, norm1_gain, norm1_shift, qkv_weight, query_bias, value_bias,
    out_weight, out_bias, norm2_gain, norm2_shift, up_weight, up_bias, down_weight, down_bias,
):
    shards = lax.axis_size("fsdp")
    rows, width = tokens.shape
    hidden = up_weight.shape[1]
    s = Sizes(rows, width, hidden, shards)
    small = [norm1_gain, norm1_shift, query_bias, value_bias, out_bias, norm2_gain, norm2_shift, down_bias]
    vec = lax.all_gather(jnp.stack(small).astype(BF), "fsdp", axis=1, tiled=True).astype(F32)
    ubias = lax.all_gather(up_bias.astype(BF), "fsdp", axis=0).astype(F32)[:, None, :]
    weights = [
        lax.all_gather(w.astype(BF), "fsdp", axis=0, tiled=True)
        for w in (qkv_weight, out_weight, up_weight, down_weight)
    ]
    seg = segment_ids.reshape(s.seqs, 1, SEQ)
    whole = pl.BlockSpec(memory_space=pltpu.VMEM)
    away = pl.BlockSpec(memory_space=pl.ANY)
    groups = s.pairs // 2
    results = pl.pallas_call(
        functools.partial(block_kernel, s),
        out_shape=(
            jax.ShapeDtypeStruct((rows, width), BF),
            jax.ShapeDtypeStruct((rows, width), BF),
            jax.ShapeDtypeStruct((groups, 2, 3, width, 128), BF),
            jax.ShapeDtypeStruct((2, width, width // 2), BF),
            jax.ShapeDtypeStruct((s.tiles, 2, width, s.tile // 2), BF),
            jax.ShapeDtypeStruct((s.tiles, 2, s.tile, width // 2), BF),
            jax.ShapeDtypeStruct((8, width), F32),
            jax.ShapeDtypeStruct((shards, 1, s.share), F32),
        ),
        in_specs=[away, away, whole, whole, whole, away, away, away, away],
        out_specs=(away,) * 6 + (whole, whole),
        scratch_shapes=[
            pltpu.VMEM((rows, width), BF),
            pltpu.VMEM((rows, width), BF),
            pltpu.VMEM((rows, width), BF),
            pltpu.VMEM((width, rows), BF),
            pltpu.VMEM((width, rows), BF),
            pltpu.VMEM((rows, 3 * width), BF),
            pltpu.VMEM((rows, width), F32),
            pltpu.VMEM((rows, width), F32),
            pltpu.VMEM((rows, width), F32),
            pltpu.VMEM((rows, s.tile), BF),
            pltpu.VMEM((rows, s.tile), BF),
            pltpu.VMEM((3, width, width), BF),
            pltpu.VMEM((width, width), BF),
            pltpu.VMEM((width, hidden), BF),
            pltpu.VMEM((hidden, width), BF),
            pltpu.VMEM((s.seqs, SEQ, 128), F32),
            pltpu.VMEM((s.seqs * HEADS, 1, SEQ), F32),
            pltpu.VMEM((2, width, s.tile // 2), BF),
            pltpu.VMEM((2, max(width, s.tile), width // 2), BF),
            pltpu.VMEM((2, 3, width, 128), BF),
            pltpu.SemaphoreType.DMA((9,)),
        ],
        compiler_params=pltpu.CompilerParams(vmem_limit_bytes=61 << 20),
    )(tokens, cotangent, seg, vec, ubias, *weights)
    output, input_grad, gqkv, gout, gup, gdown, vgrad, ugrad = results
    gqkv = gqkv.transpose(3, 2, 0, 1, 4).reshape(width, 3 * width)
    gout = gout.transpose(1, 0, 2).reshape(width, width)
    half = s.tile // 2
    gup = gup.transpose(2, 0, 1, 3).reshape(width, s.tiles, shards, s.piece)
    gup = gup.transpose(0, 2, 1, 3).reshape(width, hidden)
    gdown = gdown.transpose(0, 2, 1, 3).reshape(s.tiles, shards, s.piece, width)
    gdown = gdown.transpose(1, 0, 2, 3).reshape(hidden, width)

    def summed(value):
        part = lax.psum_scatter(value.astype(BF), "fsdp", scatter_dimension=0, tiled=True)
        return lax.psum(part, "dp").astype(F32)

    gqkv, gout, gup, gdown = [summed(v) for v in (gqkv, gout, gup, gdown)]
    ugrad = summed(ugrad.reshape(hidden))
    v = [summed(vgrad[i]) for i in range(8)]
    return (
        output, input_grad, v[0], v[1], gqkv, v[2], v[3], gout, v[4], v[5], v[6], gup, ugrad, gdown, v[7],
    )


def solution(mesh):
    rows, wide, long = P(("dp", "fsdp"), None), P("fsdp", None), P("fsdp")
    shards, copies = mesh.shape["fsdp"], mesh.shape["dp"]
    linked = shards == 2 and copies in (8, 16)
    return jax.shard_map(
        functools.partial(linked_body, copies // 4) if linked else body,
        mesh=mesh,
        in_specs=(
            rows, P(("dp", "fsdp")), rows, long, long, wide, long, long, wide, long, long, long, wide, long, wide, long,
        ),
        out_specs=(
            rows, rows, long, long, wide, long, long, wide, long, long, long, wide, long, wide, long,
        ),
        check_vma=False,
    )
```
